768 devices in a mesh: dom: 64 (over y, x, core), sub: 12 (over z).
Axes of the slice: x: 4, y: 8, z: 12, core: 2. Of those that a mesh axis runs over, the one named last changes fastest.
Arguments:
- velocity: float32 [3, 320, 108, 128], P(None, 'dom', 'sub'), may hold values from -8 to 8, as said below
- displacement: float32 [3, 320, 108, 128], P(None, 'dom', 'sub'), may hold values from -0.02 to 0.02, as said below
- energy: float32 [8, 128, 48, 64], P(None, 'dom', 'sub'), may hold values from 0.5 to 2
- rho_weight: float32 [27, 128, 48, 64], P(None, 'dom', 'sub'), may hold values from 0.5 to 2
- mass_share: float32 [4, 128, 48, 64], P(None, 'dom', 'sub'), may hold values from 0.2 to 2
- energy_share: float32 [4, 128, 48, 64], P(None, 'dom', 'sub'), may hold values from 0.5 to 2
- material_id: int32 [128, 48, 64], P('dom', 'sub'), may hold values from 0 to 3
- mix_mask: int32 [4, 128, 48, 64], P(None, 'dom', 'sub'), may hold values 0 or 1
Outputs:
- accel: float32 [3, 320, 108, 128], P(None, 'dom', 'sub')
- residual: float32 [3, 320, 108, 128], P(None, 'dom', 'sub')
- energy_rate: float32 [8, 128, 48, 64], P(None, 'dom', 'sub')
The draws below stay inside these ranges and needn't reach their ends.
Inputs may be any that keep to these rules, and one draw needn't show every extreme that they name: `velocity`: every copy of a grid node holds the same value. `displacement`: every copy of a grid node holds the same value.
All inputs are finite; a program needn't handle non-finite values. No bound on the sum of `mix_mask` on one device may be relied on, other than what follows from the above.
Results may differ from the reference program's by a relative error of at most 0.0003.
Values sent between devices are 32-bit elements; how exact they have to be, the bound alone decides.
No kernel may reach another device: no remote copies, remote signals or barrier semaphores. Data moves between devices by JAX's collectives and lax.ppermute only.
A program may use at most 32 MiB of HBM per device.

```python
import math
import jax
import jax.numpy as jnp
import numpy as np
from jax import lax

CX = 2
CY = 4
MATS = 4
EQ_ITERS = 4
CG_ITERS = 3
NX = 128
NY = 48
NZ = 64
NODE_X = 320
NODE_Y = 108
N_DOM = 64
N_SUB = 12


def spread_nodes(unique):
    along_x = jnp.arange(NODE_X, dtype=jnp.int32)
    index_x = (along_x // (2 * CX + 1) * (2 * CX) + along_x % (2 * CX + 1)) % (2 * NX)
    along_y = jnp.arange(NODE_Y, dtype=jnp.int32)
    index_y = (along_y // (2 * CY + 1) * (2 * CY) + along_y % (2 * CY + 1)) % (2 * NY)
    return jnp.take(jnp.take(unique, index_x, axis=1), index_y, axis=2)


def draw_velocity(key, part):
    extent = (3, 2 * NX, 2 * NY, 2 * NZ)
    unique = jnp.clip(jax.random.normal(key, extent, jnp.float32), -8.0, 8.0)
    return spread_nodes(unique.astype(jnp.float32)).astype(jnp.float32)


def draw_displacement(key, part):
    extent = (3, 2 * NX, 2 * NY, 2 * NZ)
    unique = jax.random.uniform(key, extent, minval=-0.02, maxval=0.02)
    return spread_nodes(unique.astype(jnp.float32)).astype(jnp.float32)


def touch_ends(values, stream_key, least, largest):
    shape = values.shape
    spot = [jax.random.randint(jax.random.fold_in(stream_key, axis), (), 0, shape[axis]) for axis in range(len(shape))]
    values = values.at[tuple(spot)].set(least)
    longest = shape.index(max(shape))
    spot[longest] = (spot[longest] + 1) % shape[longest]
    return values.at[tuple(spot)].set(largest)


def shard_levels(own_key, shape, cuts, low, top_value):
    gain, own = 1.0, jax.random.fold_in(own_key, 6)
    for dim, shards_of in cuts:
        heights = jnp.exp(jax.random.uniform(jax.random.fold_in(own, dim), (shards_of,), jnp.float32, low / len(cuts), top_value / len(cuts)))
        gain = gain * jnp.repeat(heights, shape[dim] // shards_of).reshape([-1 if axis == dim else 1 for axis in range(len(shape))])
    return gain


def setup_inputs(seed: int = 0) -> dict:
    keys = jax.random.split(jax.random.key(seed), 9)
    return {
        "velocity": draw_velocity(jax.random.fold_in(keys[8], 71), 0),
        "displacement": draw_displacement(jax.random.fold_in(keys[8], 71), 0),
        "energy": jnp.clip(jnp.exp(math.log(2.0) - 1.3862944 * jax.random.uniform(keys[2], (8, NX, NY, NZ), jnp.float32) ** shard_levels(keys[2], (8, NX, NY, NZ), ((1, 64), (2, 12)), -0.2, 0.2)), 0.5, 2.0),
        "rho_weight": jnp.clip(jnp.exp(math.log(2.0) - 1.3862944 * jax.random.uniform(keys[3], (27, NX, NY, NZ), jnp.float32) ** shard_levels(keys[3], (27, NX, NY, NZ), ((1, 64), (2, 12)), -0.2, 0.2)), 0.5, 2.0),
        "mass_share": jnp.clip(jnp.exp(math.log(2.0) - 2.3025851 * jax.random.uniform(keys[4], (MATS, NX, NY, NZ), jnp.float32) ** shard_levels(keys[4], (MATS, NX, NY, NZ), ((1, 64), (2, 12)), -0.2, 0.2)), 0.2, 2.0),
        "energy_share": jnp.clip(jnp.exp(math.log(2.0) - 1.3862944 * jax.random.uniform(keys[5], (MATS, NX, NY, NZ), jnp.float32) ** shard_levels(keys[5], (MATS, NX, NY, NZ), ((1, 64), (2, 12)), -0.2, 0.2)), 0.5, 2.0),
        "material_id": touch_ends(jax.random.randint(keys[6], (NX, NY, NZ), 0, MATS), jax.random.fold_in(keys[6], 1), 0, MATS - 1).astype(jnp.int32),
        "mix_mask": touch_ends((jax.random.randint(keys[7], (MATS, NX, NY, NZ), 0, 2) < 1).astype(jnp.int32), jax.random.fold_in(keys[7], 1), 0, 1),
    }


gammas = (1.4, 1.67, 2.0, 3.0)
cold_terms = (0.3, 1.2, 0.6, 2.4)
highest = lax.Precision.HIGHEST

def tensor_three(first, second, third):
    grid = first[:, None, None, :, None, None] * second[None, :, None, None, :, None] * third[None, None, :, None, None, :]
    rows = first.shape[0] * second.shape[0] * third.shape[0]
    columns = first.shape[1] * second.shape[1] * third.shape[1]
    return grid.reshape(rows, columns)

def basis_tables():
    spread_root = math.sqrt(0.15)
    points = np.array([0.5 - spread_root, 0.5, 0.5 + spread_root])
    quad_one = np.array([5.0, 8.0, 5.0]) / 18.0
    value_one = np.stack([2.0 * (points - 0.5) * (points - 1.0), -4.0 * points * (points - 1.0), 2.0 * points * (points - 0.5)], 1)
    slope_one = np.stack([4.0 * points - 3.0, 4.0 - 8.0 * points, 4.0 * points - 1.0], 1)
    linear_one = np.stack([1.0 - points, points], 1)
    values = tensor_three(value_one, value_one, value_one)
    slopes = np.stack([tensor_three(slope_one, value_one, value_one), tensor_three(value_one, slope_one, value_one), tensor_three(value_one, value_one, slope_one)])
    linear = tensor_three(linear_one, linear_one, linear_one)
    weights = (quad_one[:, None, None] * quad_one[None, :, None] * quad_one[None, None, :]).reshape(27)
    return (jnp.asarray(values, jnp.float32), jnp.asarray(slopes, jnp.float32), jnp.asarray(linear, jnp.float32), jnp.asarray(weights, jnp.float32))

def close_axis(array_in, axis_at):
    head_layer = lax.slice_in_dim(array_in, 0, 1, axis=axis_at)
    return jnp.concatenate([array_in, head_layer], axis_at)

def fold_periodic(array_in, axis_at):
    length = array_in.shape[axis_at] - 1
    first_layer = lax.slice_in_dim(array_in, 0, 1, axis=axis_at) + lax.slice_in_dim(array_in, length, length + 1, axis=axis_at)
    return jnp.concatenate([first_layer, lax.slice_in_dim(array_in, 1, length, axis=axis_at)], axis_at)

def zone_corners(nodes_in, zone_x, zone_y, zone_z):
    pieces = []
    for shift_x in range(3):
        for shift_y in range(3):
            for shift_z in range(3):
                pieces.append(nodes_in[:, shift_x:shift_x + 2 * zone_x:2, shift_y:shift_y + 2 * zone_y:2, shift_z:shift_z + 2 * zone_z:2])
    return jnp.stack(pieces, 0)

def weave_axis(contrib, axis_at):
    lower_part, middle_part, upper_part = (contrib[0], contrib[1], contrib[2])
    zone_count = lower_part.shape[axis_at]
    high_pad = [(0, 0)] * lower_part.ndim
    high_pad[axis_at] = (0, 1)
    low_pad = [(0, 0)] * lower_part.ndim
    low_pad[axis_at] = (1, 0)
    even_rows = jnp.pad(lower_part, high_pad) + jnp.pad(upper_part, low_pad)
    even_head = lax.slice_in_dim(even_rows, 0, zone_count, axis=axis_at)
    even_tail = lax.slice_in_dim(even_rows, zone_count, zone_count + 1, axis=axis_at)
    woven_rows = jnp.stack([even_head, middle_part], axis_at + 1)
    extent = list(even_head.shape)
    extent[axis_at] = 2 * zone_count
    return jnp.concatenate([woven_rows.reshape(extent), even_tail], axis_at)

def place_zones(contrib):
    spread = contrib.reshape((3, 3, 3) + contrib.shape[1:])
    spread = weave_axis(spread, 3)
    spread = weave_axis(spread, 3)
    return weave_axis(spread, 3)

def adjugate_of(matrix):
    cofactors = []
    for column in range(3):
        entries = []
        for line_at in range(3):
            entries.append(matrix[(line_at + 1) % 3, (column + 1) % 3] * matrix[(line_at + 2) % 3, (column + 2) % 3] - matrix[(line_at + 1) % 3, (column + 2) % 3] * matrix[(line_at + 2) % 3, (column + 1) % 3])
        cofactors.append(jnp.stack(entries))
    return jnp.stack(cofactors)

def zone_force(disp_closed, vel_closed, energy, rho_weight, mass_share, energy_share, material_id, mix_mask, tables):
    value_table, slope_table, linear_table, weight_table = tables
    zone_x, zone_y, zone_z = (energy.shape[1], energy.shape[2], energy.shape[3])
    disp_zone = zone_corners(disp_closed, zone_x, zone_y, zone_z)
    vel_zone = zone_corners(vel_closed, zone_x, zone_y, zone_z)
    identity = jnp.eye(3, dtype=jnp.float32)[:, :, None, None, None, None]
    jacobian = jnp.einsum('dqn,ncxyz->cdqxyz', slope_table, disp_zone, precision=highest) + identity
    velgrad = jnp.einsum('dqn,ncxyz->cdqxyz', slope_table, vel_zone, precision=highest)
    adjugate = adjugate_of(jacobian)
    determinant = lax.optimization_barrier(jnp.sum(jacobian[0] * adjugate[:, 0], axis=0))
    density = rho_weight / determinant
    energy_points = jnp.einsum('qj,jxyz->qxyz', linear_table, energy, precision=highest)
    material = jnp.arange(MATS, dtype=jnp.int32)[:, None, None, None]
    present = jnp.where((mix_mask == 1) | (material_id[None] == material), 1.0, 0.0).astype(jnp.float32)
    weighted = present * mass_share
    mass_fraction = weighted / lax.optimization_barrier(jnp.sum(weighted, 0, keepdims=True))
    gamma_less = jnp.asarray(gammas, jnp.float32)[:, None, None, None, None] - 1.0
    cold_part = jnp.asarray(cold_terms, jnp.float32)[:, None, None, None, None]
    pressure_load = gamma_less * density[None] * (mass_fraction * energy_share)[:, None] * energy_points[None]
    fraction = jnp.broadcast_to((present / lax.optimization_barrier(jnp.sum(present, 0, keepdims=True)))[:, None], pressure_load.shape)
    for sweep_at in range(EQ_ITERS):
        grown_part = jnp.sqrt(fraction * (pressure_load + cold_part * fraction))
        fraction = grown_part / lax.optimization_barrier(jnp.sum(grown_part, 0, keepdims=True))
    pressure = lax.optimization_barrier(jnp.sum(pressure_load + cold_part * fraction, 0))
    stress = weight_table[:, None, None, None] * pressure
    force_zone = jnp.einsum('dqn,dcqxyz->ncxyz', slope_table, adjugate * stress[None, None], precision=highest)
    divergence = lax.optimization_barrier(jnp.sum(velgrad * jnp.swapaxes(adjugate, 0, 1), (0, 1)))
    work_rate = jnp.einsum('qj,qxyz->jxyz', linear_table, stress * divergence, precision=highest)
    lumped = jnp.einsum('qj,qxyz->jxyz', linear_table, weight_table[:, None, None, None] * rho_weight, precision=highest)
    return (force_zone, -work_rate / lumped)

def mass_zone(nodes_closed, mass_weight, tables):
    value_table = tables[0]
    corners = zone_corners(nodes_closed, mass_weight.shape[1], mass_weight.shape[2], mass_weight.shape[3])
    at_points = jnp.einsum('qn,ncxyz->cqxyz', value_table, corners, precision=highest) * mass_weight[None]
    return jnp.einsum('qn,cqxyz->ncxyz', value_table, at_points, precision=highest)

def compress(copies):
    components = copies.shape[0]
    blocks = copies.reshape(components, N_DOM, 2 * CX + 1, N_SUB, 2 * CY + 1, copies.shape[3])
    return blocks[:, :, :2 * CX, :, :2 * CY].reshape(components, 2 * NX, 2 * NY, copies.shape[3])

def expand(unique):
    along_x = jnp.arange(NODE_X, dtype=jnp.int32)
    index_x = (along_x // (2 * CX + 1) * (2 * CX) + along_x % (2 * CX + 1)) % (2 * NX)
    along_y = jnp.arange(NODE_Y, dtype=jnp.int32)
    index_y = (along_y // (2 * CY + 1) * (2 * CY) + along_y % (2 * CY + 1)) % (2 * NY)
    return jnp.take(jnp.take(unique, index_x, axis=1), index_y, axis=2)

def close_all(unique):
    return close_axis(close_axis(close_axis(unique, 1), 2), 3)

def node_slab(array_in, block_at):
    return lax.dynamic_slice_in_dim(array_in, block_at * (2 * CX), 2 * CX + 1, axis=1)

def zone_slab(array_in, block_at):
    return lax.dynamic_slice_in_dim(array_in, block_at * CX, CX, axis=array_in.ndim - 3)

def finish(contrib):
    return fold_periodic(fold_periodic(place_zones(contrib), 2), 3)

def join_blocks(placed):
    main_part = placed[:, :, :2 * CX]
    tail_part = jnp.roll(placed[:, :, 2 * CX], 1, axis=0)
    main_part = main_part.at[:, :, 0].add(tail_part)
    return jnp.moveaxis(main_part, 0, 1).reshape(3, 2 * NX, 2 * NY, 2 * NZ)

def reference(velocity, displacement, energy, rho_weight, mass_share, energy_share, material_id, mix_mask):
    tables = basis_tables()
    vel_closed = close_all(compress(velocity))
    disp_closed = close_all(compress(displacement))
    mass_weight = tables[3][:, None, None, None] * rho_weight
    block_ids = jnp.arange(N_DOM, dtype=jnp.int32)

    def force_block(block_at):
        force_zone, rate_block = zone_force(node_slab(disp_closed, block_at), node_slab(vel_closed, block_at), zone_slab(energy, block_at), zone_slab(rho_weight, block_at), zone_slab(mass_share, block_at), zone_slab(energy_share, block_at), zone_slab(material_id, block_at), zone_slab(mix_mask, block_at), tables)
        return (finish(force_zone), rate_block)
    placed, rate_blocks = lax.map(force_block, block_ids)
    force_total = join_blocks(placed)
    energy_rate = jnp.moveaxis(rate_blocks, 0, 1).reshape(8, NX, NY, NZ)

    def apply_mass(node_field):
        closed = close_all(node_field)

        def mass_block(block_at):
            return finish(mass_zone(node_slab(closed, block_at), zone_slab(mass_weight, block_at), tables))
        return join_blocks(lax.map(mass_block, block_ids))
    solution = jnp.zeros_like(force_total)
    residual = force_total
    direction = force_total
    norm_now = jnp.sum(residual * residual)
    for sweep_at in range(CG_ITERS):
        mapped = apply_mass(direction)
        step_size = norm_now / jnp.sum(direction * mapped)
        solution = solution + step_size * direction
        residual = residual - step_size * mapped
        norm_next = jnp.sum(residual * residual)
        direction = residual + norm_next / norm_now * direction
        norm_now = norm_next
    return (expand(solution), expand(residual), energy_rate)
```

```python
import math

import jax
import jax.numpy as jnp
import numpy as np
from jax import lax
from jax.sharding import Mesh
from jax.sharding import PartitionSpec as P

MATS = 4
EQ_ITERS = 4
CG_ITERS = 3
DOM_SUB = ("dom_0", "dom_1", "dom_2", "sub")
DOM = ("dom_0", "dom_1", "dom_2")


gammas = (1.4, 1.67, 2.0, 3.0)
cold_terms = (0.3, 1.2, 0.6, 2.4)
highest = lax.Precision.HIGHEST


def pair_groups(axes, offset):
    count = 1
    for axis in axes:
        count *= lax.axis_size(axis)
    return [[(i + offset) % count, (i + offset + 1) % count] for i in range(0, count, 2)]


def pair_sum(layer, axes, offset):
    gathered = lax.all_gather(layer, axes, axis_index_groups=pair_groups(axes, offset))
    return gathered[0] + gathered[1]


def join_axis(block, axes, dim):
    even = lax.axis_index(axes) % 2 == 0
    last = block.shape[dim] - 1
    low = lax.slice_in_dim(block, 0, 1, axis=dim)
    high = lax.slice_in_dim(block, last, last + 1, axis=dim)
    inner = pair_sum(jnp.where(even, high, low), axes, 0)
    outer = pair_sum(jnp.where(even, low, high), axes, 1)
    middle = lax.slice_in_dim(block, 1, last, axis=dim)
    return jnp.concatenate(
        [jnp.where(even, outer, inner), middle, jnp.where(even, inner, outer)], dim
    )


def total(values):
    for axes in (DOM, ("sub",)):
        count = 1
        for axis in axes:
            count *= lax.axis_size(axis)
        spread = jnp.broadcast_to(values[None], (count, values.shape[0]))
        values = jnp.sum(lax.all_to_all(spread, axes, 0, 0, tiled=True), 0)
    return values


def tensor_three(first, second, third):
    grid = (
        first[:, None, None, :, None, None]
        * second[None, :, None, None, :, None]
        * third[None, None, :, None, None, :]
    )
    rows = first.shape[0] * second.shape[0] * third.shape[0]
    columns = first.shape[1] * second.shape[1] * third.shape[1]
    return grid.reshape(rows, columns)


def basis_tables():
    spread_root = math.sqrt(0.15)
    points = np.array([0.5 - spread_root, 0.5, 0.5 + spread_root])
    quad_one = np.array([5.0, 8.0, 5.0]) / 18.0
    value_one = np.stack(
        [
            2.0 * (points - 0.5) * (points - 1.0),
            -4.0 * points * (points - 1.0),
            2.0 * points * (points - 0.5),
        ],
        1,
    )
    slope_one = np.stack([4.0 * points - 3.0, 4.0 - 8.0 * points, 4.0 * points - 1.0], 1)
    linear_one = np.stack([1.0 - points, points], 1)
    values = tensor_three(value_one, value_one, value_one)
    slopes = np.stack(
        [
            tensor_three(slope_one, value_one, value_one),
            tensor_three(value_one, slope_one, value_one),
            tensor_three(value_one, value_one, slope_one),
        ]
    )
    linear = tensor_three(linear_one, linear_one, linear_one)
    weights = (quad_one[:, None, None] * quad_one[None, :, None] * quad_one[None, None, :]).reshape(
        27
    )
    return (
        jnp.asarray(values, jnp.float32),
        jnp.asarray(slopes, jnp.float32),
        jnp.asarray(linear, jnp.float32),
        jnp.asarray(weights, jnp.float32),
    )


def depth_table(zone_z):
    layer = jnp.arange(2 * zone_z, dtype=jnp.int32)[:, None, None]
    offset = jnp.arange(3, dtype=jnp.int32)[None, :, None]
    zone_at = jnp.arange(zone_z, dtype=jnp.int32)[None, None, :]
    return jnp.where(layer == (2 * zone_at + offset) % (2 * zone_z), 1.0, 0.0).astype(jnp.float32)


def zone_corners(nodes_in, zone_x, zone_y, table):
    by_depth = jnp.einsum("cxyk,ksz->scxyz", nodes_in, table, precision=highest)
    pieces = []
    for shift_x in range(3):
        for shift_y in range(3):
            for shift_z in range(3):
                pieces.append(
                    by_depth[shift_z][
                        :, shift_x : shift_x + 2 * zone_x : 2, shift_y : shift_y + 2 * zone_y : 2
                    ]
                )
    return jnp.stack(pieces, 0)


def weave_axis(contrib, axis_at):
    lower_part, middle_part, upper_part = (contrib[0], contrib[1], contrib[2])
    zone_count = lower_part.shape[axis_at]
    high_pad = [(0, 0)] * lower_part.ndim
    high_pad[axis_at] = (0, 1)
    low_pad = [(0, 0)] * lower_part.ndim
    low_pad[axis_at] = (1, 0)
    even_rows = jnp.pad(lower_part, high_pad) + jnp.pad(upper_part, low_pad)
    even_head = lax.slice_in_dim(even_rows, 0, zone_count, axis=axis_at)
    even_tail = lax.slice_in_dim(even_rows, zone_count, zone_count + 1, axis=axis_at)
    woven_rows = jnp.stack([even_head, middle_part], axis_at + 1)
    extent = list(even_head.shape)
    extent[axis_at] = 2 * zone_count
    return jnp.concatenate([woven_rows.reshape(extent), even_tail], axis_at)


def place_zones(contrib, table):
    spread = contrib.reshape((3, 3, 3) + contrib.shape[1:])
    spread = weave_axis(spread, 3)
    spread = weave_axis(spread, 3)
    return jnp.einsum("scxyz,ksz->cxyk", spread, table, precision=highest)


def adjugate_of(matrix):
    cofactors = []
    for column in range(3):
        entries = []
        for line_at in range(3):
            entries.append(
                matrix[(line_at + 1) % 3, (column + 1) % 3]
                * matrix[(line_at + 2) % 3, (column + 2) % 3]
                - matrix[(line_at + 1) % 3, (column + 2) % 3]
                * matrix[(line_at + 2) % 3, (column + 1) % 3]
            )
        cofactors.append(jnp.stack(entries))
    return jnp.stack(cofactors)


def zone_force(
    displacement,
    velocity,
    energy,
    rho_weight,
    mass_share,
    energy_share,
    material_id,
    mix_mask,
    tables,
    table_z,
):
    value_table, slope_table, linear_table, weight_table = tables
    zone_x, zone_y = (energy.shape[1], energy.shape[2])
    disp_zone = zone_corners(displacement, zone_x, zone_y, table_z)
    vel_zone = zone_corners(velocity, zone_x, zone_y, table_z)
    identity = jnp.eye(3, dtype=jnp.float32)[:, :, None, None, None, None]
    jacobian = jnp.einsum("dqn,ncxyz->cdqxyz", slope_table, disp_zone, precision=highest) + identity
    velgrad = jnp.einsum("dqn,ncxyz->cdqxyz", slope_table, vel_zone, precision=highest)
    adjugate = adjugate_of(jacobian)
    determinant = jnp.sum(jacobian[0] * adjugate[:, 0], axis=0)
    density = rho_weight / determinant
    energy_points = jnp.einsum("qj,jxyz->qxyz", linear_table, energy, precision=highest)
    material = jnp.arange(MATS, dtype=jnp.int32)[:, None, None, None]
    present = jnp.where((mix_mask == 1) | (material_id[None] == material), 1.0, 0.0).astype(
        jnp.float32
    )
    weighted = present * mass_share
    mass_fraction = weighted / jnp.sum(weighted, 0, keepdims=True)
    gamma_less = jnp.asarray(gammas, jnp.float32)[:, None, None, None, None] - 1.0
    cold_part = jnp.asarray(cold_terms, jnp.float32)[:, None, None, None, None]
    pressure_load = (
        gamma_less * density[None] * (mass_fraction * energy_share)[:, None] * energy_points[None]
    )
    fraction = jnp.broadcast_to(
        (present / jnp.sum(present, 0, keepdims=True))[:, None], pressure_load.shape
    )
    for sweep_at in range(EQ_ITERS):
        grown_part = jnp.sqrt(fraction * (pressure_load + cold_part * fraction))
        fraction = grown_part / jnp.sum(grown_part, 0, keepdims=True)
    pressure = jnp.sum(pressure_load + cold_part * fraction, 0)
    stress = weight_table[:, None, None, None] * pressure
    force_zone = jnp.einsum(
        "dqn,dcqxyz->ncxyz", slope_table, adjugate * stress[None, None], precision=highest
    )
    divergence = jnp.sum(velgrad * jnp.swapaxes(adjugate, 0, 1), (0, 1))
    work_rate = jnp.einsum("qj,qxyz->jxyz", linear_table, stress * divergence, precision=highest)
    lumped = jnp.einsum(
        "qj,qxyz->jxyz",
        linear_table,
        weight_table[:, None, None, None] * rho_weight,
        precision=highest,
    )
    return (force_zone, -work_rate / lumped)


def mass_zone(node_field, mass_weight, tables, table_z):
    value_table = tables[0]
    corners = zone_corners(node_field, mass_weight.shape[1], mass_weight.shape[2], table_z)
    at_points = (
        jnp.einsum("qn,ncxyz->cqxyz", value_table, corners, precision=highest) * mass_weight[None]
    )
    return jnp.einsum("qn,cqxyz->ncxyz", value_table, at_points, precision=highest)


def assemble(local_sum):
    return join_axis(join_axis(local_sum, ("sub",), 2), DOM, 1)


CENTER = 0.196
HALF_WIDTH = 0.194
PAIRS = ((0, 0), (0, 1), (0, 2), (0, 3), (1, 1), (1, 2), (1, 3), (2, 2), (2, 3))


def dot_in(gram, left, right):
    value = 0.0
    for i in range(4):
        for j in range(4):
            if left[i] is None or right[j] is None or (i == 3 and j == 3):
                continue
            value = value + gram[(min(i, j), max(i, j))] * left[i] * right[j]
    return value


def axpy(scale, left, right):
    out = []
    for a, b in zip(left, right):
        if a is None:
            out.append(b)
        elif b is None:
            out.append(scale * a)
        else:
            out.append(scale * a + b)
    return out


def mapped_coefficients(p):
    p0, p1, p2 = (0.0 if v is None else v for v in p[:3])
    shifted = [0.5 * p1, p0 + 0.5 * p2, 0.5 * p1, 0.5 * p2]
    return [HALF_WIDTH * b + CENTER * a for a, b in zip((p0, p1, p2, 0.0), shifted)]


def cg_coefficients(gram):
    accel = [0.0, 0.0, 0.0, 0.0]
    residual = [1.0, 0.0, 0.0, 0.0]
    direction = residual
    norm_now = gram[(0, 0)]
    for sweep_at in range(CG_ITERS):
        mapped = mapped_coefficients(direction)
        step = norm_now / dot_in(gram, direction, mapped)
        accel = axpy(step, direction, accel)
        residual = axpy(-step, mapped, residual)
        if sweep_at + 1 < CG_ITERS:
            norm_next = dot_in(gram, residual, residual)
            direction = axpy(norm_next / norm_now, direction, residual)
            norm_now = norm_next
    return accel, residual


def per_device(
    velocity, displacement, energy, rho_weight, mass_share, energy_share, material_id, mix_mask
):
    tables = basis_tables()
    table_z = depth_table(energy.shape[3])
    force_zone, energy_rate = zone_force(
        displacement,
        velocity,
        energy,
        rho_weight,
        mass_share,
        energy_share,
        material_id,
        mix_mask,
        tables,
        table_z,
    )
    force_total = assemble(place_zones(force_zone, table_z))
    mass_weight = tables[3][:, None, None, None] * rho_weight

    def apply_mass(node_field):
        return assemble(place_zones(mass_zone(node_field, mass_weight, tables, table_z), table_z))

    def shifted(node_field):
        return (1.0 / HALF_WIDTH) * apply_mass(node_field) - (CENTER / HALF_WIDTH) * node_field

    basis = [force_total, shifted(force_total)]
    for _ in range(CG_ITERS - 1):
        basis.append(2.0 * shifted(basis[-1]) - basis[-2])
    owned = [field[:, :-1, :-1] for field in basis]
    products = jnp.stack([jnp.sum(owned[i] * owned[j]) for i, j in PAIRS])
    products = total(jnp.pad(products, (0, 16 - len(PAIRS))))
    gram = {pair: products[at] for at, pair in enumerate(PAIRS)}
    accel_of, residual_of = cg_coefficients(gram)
    accel = sum(accel_of[i] * basis[i] for i in range(3))
    residual = sum(residual_of[i] * basis[i] for i in range(4))
    return (accel, residual, energy_rate)


def solution(mesh):
    torus = Mesh(
        mesh.devices.reshape(mesh.shape["dom"] // 8, 4, 2, mesh.shape["sub"]), ("dom_0", "dom_1", "dom_2", "sub")
    )
    return jax.shard_map(
        per_device,
        mesh=torus,
        in_specs=(
            P(None, DOM, "sub", None),
            P(None, DOM, "sub", None),
            P(None, DOM, "sub", None),
            P(None, DOM, "sub", None),
            P(None, DOM, "sub", None),
            P(None, DOM, "sub", None),
            P(DOM, "sub", None),
            P(None, DOM, "sub", None),
        ),
        out_specs=(P(None, DOM, "sub", None), P(None, DOM, "sub", None), P(None, DOM, "sub", None)),
        check_vma=False,
    )
```

```python
import functools
import math

import jax
import jax.numpy as jnp
from jax import lax
from jax.experimental import pallas as pl
from jax.experimental.pallas import tpu as pltpu
from jax.sharding import Mesh
from jax.sharding import PartitionSpec as P

MATS = 4
EQ_ITERS = 4
CG_ITERS = 3
DOM_SUB = ("dom_0", "dom_1", "dom_2", "sub")
DOM = ("dom_0", "dom_1", "dom_2")


gammas = (1.4, 1.67, 2.0, 3.0)
cold_terms = (0.3, 1.2, 0.6, 2.4)
highest = lax.Precision.HIGHEST


def pair_groups(axes, offset):
    count = 1
    for axis in axes:
        count *= lax.axis_size(axis)
    return [[(i + offset) % count, (i + offset + 1) % count] for i in range(0, count, 2)]


def pair_sum(layer, axes, offset):
    gathered = lax.all_gather(layer, axes, axis_index_groups=pair_groups(axes, offset))
    return gathered[0] + gathered[1]


def join_axis(block, axes, dim):
    even = lax.axis_index(axes) % 2 == 0
    last = block.shape[dim] - 1
    low = lax.slice_in_dim(block, 0, 1, axis=dim)
    high = lax.slice_in_dim(block, last, last + 1, axis=dim)
    inner = pair_sum(jnp.where(even, high, low), axes, 0)
    outer = pair_sum(jnp.where(even, low, high), axes, 1)
    middle = lax.slice_in_dim(block, 1, last, axis=dim)
    return jnp.concatenate(
        [jnp.where(even, outer, inner), middle, jnp.where(even, inner, outer)], dim
    )


def total(values):
    for axes in (DOM, ("sub",)):
        count = 1
        for axis in axes:
            count *= lax.axis_size(axis)
        spread = jnp.broadcast_to(values[None], (count, values.shape[0]))
        gathered = lax.all_to_all(spread, axes, 0, 0, tiled=True)
        values = jnp.sum(gathered, 0)
    return gathered


ROOT = math.sqrt(0.15)
POINTS = (0.5 - ROOT, 0.5, 0.5 + ROOT)
QUAD = (5.0 / 18.0, 8.0 / 18.0, 5.0 / 18.0)
VALUE = tuple((2.0 * (t - 0.5) * (t - 1.0), -4.0 * t * (t - 1.0), 2.0 * t * (t - 0.5)) for t in POINTS)
SLOPE = tuple((4.0 * t - 3.0, 4.0 - 8.0 * t, 4.0 * t - 1.0) for t in POINTS)
LINEAR = tuple((1.0 - t, t) for t in POINTS)


def value_of(nodes):
    first, middle, last = nodes
    a, b, c = VALUE[0]
    scaled = b * middle
    return (a * first + scaled + c * last, middle, c * first + scaled + a * last)


def value_back(points):
    first, middle, last = points
    a, b, c = VALUE[0]
    return (a * first + c * last, b * (first + last) + middle, c * first + a * last)


def slope_of(nodes):
    first, middle, last = nodes
    a, b, c = SLOPE[0]
    scaled = b * middle
    return (a * first + scaled + c * last, last - first, -c * first - scaled - a * last)


def slope_back(points):
    first, middle, last = points
    a, b, c = SLOPE[0]
    return (a * first - middle - c * last, b * (first - last), c * first + middle - a * last)


def turn(array, shift):
    return pltpu.roll(array, shift % array.shape[-1], array.ndim - 1)


def even_lanes(rows):
    return lax.broadcasted_iota(jnp.int32, (rows, 128), 1) % 2 == 0


def depth_value(nodes, even, one, two):
    a, b, c = VALUE[0]
    scaled = b * one
    return jnp.where(even, a * nodes + scaled + c * two, nodes), c * nodes + scaled + a * two


def depth_value_back(near, far, even):
    a, b, c = VALUE[0]
    near_even = jnp.where(even, near, 0.0)
    ahead = turn(b * (near_even + far), 1) + turn(c * near_even + a * far, 2)
    return jnp.where(even, a * near + c * far, near) + ahead


def corners(ref, c, packs, rows):
    out = []
    for i in range(3):
        line = []
        for j in range(3):
            parts = [ref[c, 2 * zone + i, pl.ds(j, rows, stride=2), :] for zone in packs]
            line.append(parts[0] if len(parts) == 1 else jnp.concatenate(parts, 0))
        out.append(line)
    return out


def scatter(ref, c, packs, rows, nodes):
    for i in range(3):
        for j in range(3):
            for at, zone in enumerate(packs):
                part = nodes[i][j][at * rows : (at + 1) * rows]
                spot = (c, 2 * zone + i, pl.ds(j, rows, stride=2), slice(None))
                ref[spot] = ref[spot] + part


def mass_nodes(nodes, near_mass, far_mass, even):
    near = [[None] * 3 for _ in range(3)]
    far = [[None] * 3 for _ in range(3)]
    for i in range(3):
        for j in range(3):
            u = nodes[i][j]
            near[i][j], far[i][j] = depth_value(u, even, turn(u, -1), turn(u, -2))
    sides = []
    for field, mass in ((near, near_mass), (far, far_mass)):
        field = [value_of(line) for line in field]
        field = [value_of([field[i][j] for i in range(3)]) for j in range(3)]
        field = [[field[j][i] * mass[3 * i + j] for j in range(3)] for i in range(3)]
        field = [value_back(line) for line in field]
        field = [value_back([field[i][j] for i in range(3)]) for j in range(3)]
        sides.append(field)
    return [[depth_value_back(sides[0][j][i], sides[1][j][i], even) for j in range(3)] for i in range(3)]


def spread_tables():
    zone = lax.broadcasted_iota(jnp.int32, (64, 128), 0)
    lane = lax.broadcasted_iota(jnp.int32, (64, 128), 1)
    one, zero = jnp.float32(1.0), jnp.float32(0.0)
    even = jnp.where(lane == 2 * zone, one, zero)
    odd = jnp.where(lane == 2 * zone + 1, one, zero)
    return even, odd


def collect_tables(which):
    lane = lax.broadcasted_iota(jnp.int32, (128, 64), 0)
    zone = lax.broadcasted_iota(jnp.int32, (128, 64), 1)
    even, odd = lane == 2 * zone, lane == 2 * zone + 1
    near = jnp.where(even, LINEAR[0][which], jnp.where(odd, LINEAR[1][which], 0.0))
    far = jnp.where(even, LINEAR[2][which], 0.0)
    return near.astype(jnp.float32), far.astype(jnp.float32)


def dot32(left, right):
    return jnp.dot(left, right, precision=highest, preferred_element_type=jnp.float32)


def force_kernel(disp, vel, energy, rho, share, portion, ident, mix, force, rate, near_out, far_out, grad, work):
    packs, rows = (0, 1), energy.shape[2]
    count = 2 * rows
    even = even_lanes(count)

    def packed(ref, at):
        return jnp.concatenate([ref[at, 0], ref[at, 1]], 0)

    even_table, odd_table = spread_tables()
    both_table = even_table + odd_table
    material = jnp.concatenate([ident[0], ident[1]], 0)
    present = [
        jnp.where((packed(mix, m) == 1) | (material == m), 1.0, 0.0).astype(jnp.float32) for m in range(MATS)
    ]
    weighted = [present[m] * packed(share, m) for m in range(MATS)]
    weight_sum = weighted[0] + weighted[1] + weighted[2] + weighted[3]
    present_sum = present[0] + present[1] + present[2] + present[3]
    zone_rows = [
        (gammas[m] - 1.0) * (weighted[m] / weight_sum * packed(portion, m)) for m in range(MATS)
    ]
    zone_rows += [present[m] / present_sum for m in range(MATS)]
    zone_rows += [packed(energy, j) for j in range(8)]
    wide = dot32(jnp.concatenate(zone_rows, 0), both_table)
    wide = [wide[count * k : count * (k + 1)] for k in range(16)]
    loads, start, corner_energy = wide[:4], wide[4:8], wide[8:]
    rho_rows = [jnp.concatenate([packed(rho, 3 * p + k) for p in range(9)], 0) for k in range(3)]
    near_rho = dot32(rho_rows[0], even_table) + dot32(rho_rows[1], odd_table)
    far_rho = dot32(rho_rows[2], even_table)
    near_rho = [near_rho[count * p : count * (p + 1)] for p in range(9)]
    far_rho = [far_rho[count * p : count * (p + 1)] for p in range(9)]
    near_weight = jnp.where(even, QUAD[0], QUAD[1])
    far_weight = jnp.where(even, QUAD[2], 0.0)
    near_point = jnp.where(even, POINTS[0], POINTS[1])
    a, b, c = SLOPE[0]

    for field, ref in enumerate((disp, vel)):
        for comp in range(3):
            nodes = corners(ref, comp, packs, rows)
            values = [[None] * 3 for _ in range(3)], [[None] * 3 for _ in range(3)]
            slopes = [[None] * 3 for _ in range(3)], [[None] * 3 for _ in range(3)]
            for i in range(3):
                for j in range(3):
                    u = nodes[i][j]
                    one, two = turn(u, -1), turn(u, -2)
                    near, far = depth_value(u, even, one, two)
                    values[0][i][j], values[1][i][j] = near, jnp.where(even, far, 0.0)
                    scaled = b * one
                    slopes[0][i][j] = jnp.where(even, a * u + scaled + c * two, one - turn(u, 1))
                    slopes[1][i][j] = jnp.where(even, -c * u - scaled - a * two, 0.0)
            for side in range(2):
                plain = [value_of(line) for line in values[side]]
                sloped = [slope_of(line) for line in values[side]]
                deep = [value_of(line) for line in slopes[side]]
                for j in range(3):
                    along = (
                        slope_of([plain[i][j] for i in range(3)]),
                        value_of([sloped[i][j] for i in range(3)]),
                        value_of([deep[i][j] for i in range(3)]),
                    )
                    for d in range(3):
                        for i in range(3):
                            grad[field, side, 3 * i + j, 3 * comp + d] = along[d][i]

    for i in range(3):
        for j in range(3):
            spot = 3 * i + j
            plane = QUAD[i] * QUAD[j]
            mixed = []
            for k in range(2):
                low = LINEAR[j][0] * corner_energy[k] + LINEAR[j][1] * corner_energy[2 + k]
                high = LINEAR[j][0] * corner_energy[4 + k] + LINEAR[j][1] * corner_energy[6 + k]
                mixed.append(LINEAR[i][0] * low + LINEAR[i][1] * high)
            rise = mixed[1] - mixed[0]
            for side in range(2):
                weight = plane * (near_weight if side == 0 else far_weight)
                density_weight = near_rho[spot] if side == 0 else far_rho[spot]
                point = near_point if side == 0 else POINTS[2]
                jac = [[grad[0, side, spot, 3 * cc + d] + (1.0 if cc == d else 0.0) for d in range(3)] for cc in range(3)]
                adj = [
                    [
                        jac[(line + 1) % 3][(col + 1) % 3] * jac[(line + 2) % 3][(col + 2) % 3]
                        - jac[(line + 1) % 3][(col + 2) % 3] * jac[(line + 2) % 3][(col + 1) % 3]
                        for line in range(3)
                    ]
                    for col in range(3)
                ]
                determinant = jac[0][0] * adj[0][0] + jac[0][1] * adj[1][0] + jac[0][2] * adj[2][0]
                scale = density_weight / determinant * (mixed[0] + point * rise)
                load = [loads[m] * scale for m in range(MATS)]
                fraction = list(start)
                for _ in range(EQ_ITERS):
                    grown = [
                        jnp.sqrt(fraction[m] * (load[m] + cold_terms[m] * fraction[m])) for m in range(MATS)
                    ]
                    inverse = 1.0 / (grown[0] + grown[1] + grown[2] + grown[3])
                    fraction = [grown[m] * inverse for m in range(MATS)]
                terms = [load[m] + cold_terms[m] * fraction[m] for m in range(MATS)]
                stress = weight * (terms[0] + terms[1] + terms[2] + terms[3])
                divergence = 0.0
                for cc in range(3):
                    for d in range(3):
                        divergence = divergence + grad[1, side, spot, 3 * cc + d] * adj[d][cc]
                work[side, spot] = stress * divergence
                for cc in range(3):
                    for d in range(3):
                        grad[0, side, spot, 3 * cc + d] = stress * adj[d][cc]
                (near_out if side == 0 else far_out)[spot] = weight * density_weight

    force[...] = jnp.zeros_like(force)
    for comp in range(3):
        plain = [[None] * 3 for _ in range(3)], [[None] * 3 for _ in range(3)]
        deep = [[None] * 3 for _ in range(3)], [[None] * 3 for _ in range(3)]
        for side in range(2):
            lines = []
            for j in range(3):
                part = [[grad[0, side, 3 * i + j, 3 * comp + d] for i in range(3)] for d in range(3)]
                lines.append((slope_back(part[0]), value_back(part[1]), value_back(part[2])))
            for i in range(3):
                first = value_back([lines[j][0][i] for j in range(3)])
                second = slope_back([lines[j][1][i] for j in range(3)])
                third = value_back([lines[j][2][i] for j in range(3)])
                for j in range(3):
                    plain[side][i][j] = first[j] + second[j]
                    deep[side][i][j] = third[j]
        out = [[None] * 3 for _ in range(3)]
        va, vb, vc = VALUE[0]
        for i in range(3):
            for j in range(3):
                near, far = plain[0][i][j], plain[1][i][j]
                near_s, far_s = deep[0][i][j], deep[1][i][j]
                near_even = jnp.where(even, near, 0.0)
                near_s_even = jnp.where(even, near_s, 0.0)
                here = jnp.where(even, va * near + vc * far + a * near_s - c * far_s, near)
                next_one = jnp.where(even, vb * (near + far) + b * (near_s - far_s), near_s)
                next_two = vc * near_even + va * far + c * near_s_even - a * far_s
                behind = jnp.where(even, 0.0, near_s)
                out[i][j] = here + turn(next_one, 1) + turn(next_two, 2) - turn(behind, -1)
        scatter(force, comp, packs, rows, out)

    def collected(read):
        lines = [[], []]
        for side in range(2):
            for jx in range(2):
                for jy in range(2):
                    value = None
                    for i in range(3):
                        inner = None
                        for j in range(3):
                            term = LINEAR[j][jy] * read(side, 3 * i + j)
                            inner = term if inner is None else inner + term
                        inner = LINEAR[i][jx] * inner
                        value = inner if value is None else value + inner
                    lines[side].append(value)
        near, far = jnp.concatenate(lines[0], 0), jnp.concatenate(lines[1], 0)
        out = []
        for jz in range(2):
            near_table, far_table = collect_tables(jz)
            out.append(dot32(near, near_table) + dot32(far, far_table))
        return out

    done = collected(lambda side, spot: work[side, spot])
    lumped = collected(lambda side, spot: (near_out if side == 0 else far_out)[spot])
    for jz in range(2):
        ratio = -done[jz] / lumped[jz]
        for jxy in range(4):
            for zone in range(2):
                base = count * jxy + rows * zone
                rate[2 * jxy + jz, zone] = ratio[base : base + rows]


def mass_kernel(first, image, older, old, near_mass, far_mass, new, partial):
    packs, rows = (0, 1), near_mass.shape[1] // 2
    even = even_lanes(2 * rows)
    if first == 0:
        new[...] = image[...]
    elif first == 1:
        new[...] = (1.0 / HALF_WIDTH) * image[...] - (CENTER / HALF_WIDTH) * old[...]
    else:
        new[...] = (2.0 / HALF_WIDTH) * image[...] - (2.0 * CENTER / HALF_WIDTH) * old[...] - older[...]
    near = [near_mass[p] for p in range(9)]
    far = [far_mass[p] for p in range(9)]
    partial[...] = jnp.zeros_like(partial)
    for comp in range(3):
        nodes = corners(new, comp, packs, rows)
        scatter(partial, comp, packs, rows, mass_nodes(nodes, near, far, even))


def product_kernel(image, t0, t1, t2, t3, products):
    t3[...] = (2.0 / HALF_WIDTH) * image[...] - (2.0 * CENTER / HALF_WIDTH) * t2[...] - t1[...]
    refs = (t0, t1, t2, t3)
    wide, tall = image.shape[1], image.shape[2]
    lane = lax.broadcasted_iota(jnp.int32, (1, 128), 1)
    sums = [None] * len(PAIRS)
    for comp in range(3):
        for x in range(wide - 1):
            parts = [ref[comp, x, 0 : tall - 1, :] for ref in refs]
            for at, (i, j) in enumerate(PAIRS):
                term = parts[i] * parts[j]
                sums[at] = term if sums[at] is None else sums[at] + term
    row = jnp.zeros((1, 128), jnp.float32)
    for at in range(len(PAIRS)):
        value = jnp.sum(jnp.sum(sums[at], 0, keepdims=True), 1, keepdims=True)
        row = jnp.where(lane == at, value, row)
    products[...] = row


def finish_kernel(gathered, t0, t1, t2, t3, accel, residual):
    row = jnp.sum(gathered[...], 0, keepdims=True)
    gram = {pair: row[:, at : at + 1] for at, pair in enumerate(PAIRS)}
    accel_of, residual_of = cg_coefficients(gram)
    fields = (t0, t1, t2, t3)
    wide = t0.shape[1]
    for comp in range(3):
        for x in range(wide):
            parts = [field[comp, x] for field in fields]
            accel[comp, x] = accel_of[0] * parts[0] + accel_of[1] * parts[1] + accel_of[2] * parts[2]
            residual[comp, x] = (
                residual_of[0] * parts[0] + residual_of[1] * parts[1] + residual_of[2] * parts[2] + residual_of[3] * parts[3]
            )


def local_call(kernel, name, outs, scratch=()):
    return pl.pallas_call(
        kernel,
        out_shape=[jax.ShapeDtypeStruct(shape, jnp.float32) for shape in outs],
        scratch_shapes=[pltpu.VMEM(shape, jnp.float32) for shape in scratch],
        name=name,
    )


def assemble(local_sum):
    return join_axis(join_axis(local_sum, ("sub",), 2), DOM, 1)


CENTER = 0.196
HALF_WIDTH = 0.194
PAIRS = ((0, 0), (0, 1), (0, 2), (0, 3), (1, 1), (1, 2), (1, 3), (2, 2), (2, 3))


def dot_in(gram, left, right):
    value = 0.0
    for i in range(4):
        for j in range(4):
            if left[i] is None or right[j] is None or (i == 3 and j == 3):
                continue
            value = value + gram[(min(i, j), max(i, j))] * left[i] * right[j]
    return value


def axpy(scale, left, right):
    out = []
    for a, b in zip(left, right):
        if a is None:
            out.append(b)
        elif b is None:
            out.append(scale * a)
        else:
            out.append(scale * a + b)
    return out


def mapped_coefficients(p):
    p0, p1, p2 = (0.0 if v is None else v for v in p[:3])
    shifted = [0.5 * p1, p0 + 0.5 * p2, 0.5 * p1, 0.5 * p2]
    return [HALF_WIDTH * b + CENTER * a for a, b in zip((p0, p1, p2, 0.0), shifted)]


def cg_coefficients(gram):
    accel = [0.0, 0.0, 0.0, 0.0]
    residual = [1.0, 0.0, 0.0, 0.0]
    direction = residual
    norm_now = gram[(0, 0)]
    for sweep_at in range(CG_ITERS):
        mapped = mapped_coefficients(direction)
        step = norm_now / dot_in(gram, direction, mapped)
        accel = axpy(step, direction, accel)
        residual = axpy(-step, mapped, residual)
        if sweep_at + 1 < CG_ITERS:
            norm_next = dot_in(gram, residual, residual)
            direction = axpy(norm_next / norm_now, direction, residual)
            norm_now = norm_next
    return accel, residual


def per_device(
    velocity, displacement, energy, rho_weight, mass_share, energy_share, material_id, mix_mask
):
    field = velocity.shape
    count = energy.shape[1] * energy.shape[2]
    mass = (9, count, 128)
    partial, energy_rate, near_mass, far_mass = local_call(
        force_kernel, "force", (field, energy.shape, mass, mass), ((2, 2, 9, 9, count, 128), (2, 9, count, 128))
    )(displacement, velocity, energy, rho_weight, mass_share, energy_share, material_id, mix_mask)
    image = assemble(partial)
    basis = [image, image]
    for at in range(CG_ITERS):
        new, partial = local_call(functools.partial(mass_kernel, at), f"mass_{at}", (field, field))(
            image, basis[-2], basis[-1], near_mass, far_mass
        )
        basis.append(new)
        image = assemble(partial)
    t0, t1, t2 = basis[2:]
    t3, products = local_call(product_kernel, "product", (field, (1, 128)))(image, t0, t1, t2)
    gathered = total(products[0, :16])
    accel, residual = local_call(finish_kernel, "finish", (field, field))(gathered, t0, t1, t2, t3)
    return (accel, residual, energy_rate)


def solution(mesh):
    torus = Mesh(
        mesh.devices.reshape(mesh.shape["dom"] // 8, 4, 2, mesh.shape["sub"]), ("dom_0", "dom_1", "dom_2", "sub")
    )
    return jax.shard_map(
        per_device,
        mesh=torus,
        in_specs=(
            P(None, DOM, "sub", None),
            P(None, DOM, "sub", None),
            P(None, DOM, "sub", None),
            P(None, DOM, "sub", None),
            P(None, DOM, "sub", None),
            P(None, DOM, "sub", None),
            P(DOM, "sub", None),
            P(None, DOM, "sub", None),
        ),
        out_specs=(P(None, DOM, "sub", None), P(None, DOM, "sub", None), P(None, DOM, "sub", None)),
        check_vma=False,
    )
```

```python
import functools
import math

import jax
import jax.numpy as jnp
from jax import lax
from jax.experimental import pallas as pl
from jax.experimental.pallas import tpu as pltpu
from jax.sharding import Mesh
from jax.sharding import PartitionSpec as P

MATS = 4
EQ_ITERS = 4
CG_ITERS = 3
DOM_SUB = ("dom_0", "dom_1", "dom_2", "sub")
DOM = ("dom_0", "dom_1", "dom_2")


gammas = (1.4, 1.67, 2.0, 3.0)
cold_terms = (0.3, 1.2, 0.6, 2.4)
highest = lax.Precision.HIGHEST


def pair_groups(axes, offset):
    count = 1
    for axis in axes:
        count *= lax.axis_size(axis)
    return [[(i + offset) % count, (i + offset + 1) % count] for i in range(0, count, 2)]


def pair_sum(layer, axes, offset):
    gathered = lax.all_gather(layer, axes, axis_index_groups=pair_groups(axes, offset))
    return gathered[0] + gathered[1]


def join_axis(block, axes, dim):
    even = lax.axis_index(axes) % 2 == 0
    last = block.shape[dim] - 1
    low = lax.slice_in_dim(block, 0, 1, axis=dim)
    high = lax.slice_in_dim(block, last, last + 1, axis=dim)
    inner = pair_sum(jnp.where(even, high, low), axes, 0)
    outer = pair_sum(jnp.where(even, low, high), axes, 1)
    middle = lax.slice_in_dim(block, 1, last, axis=dim)
    return jnp.concatenate(
        [jnp.where(even, outer, inner), middle, jnp.where(even, inner, outer)], dim
    )


ROOT = math.sqrt(0.15)
POINTS = (0.5 - ROOT, 0.5, 0.5 + ROOT)
QUAD = (5.0 / 18.0, 8.0 / 18.0, 5.0 / 18.0)
VALUE = tuple((2.0 * (t - 0.5) * (t - 1.0), -4.0 * t * (t - 1.0), 2.0 * t * (t - 0.5)) for t in POINTS)
SLOPE = tuple((4.0 * t - 3.0, 4.0 - 8.0 * t, 4.0 * t - 1.0) for t in POINTS)
LINEAR = tuple((1.0 - t, t) for t in POINTS)


def value_of(nodes):
    first, middle, last = nodes
    a, b, c = VALUE[0]
    scaled = b * middle
    return (a * first + scaled + c * last, middle, c * first + scaled + a * last)


def value_back(points):
    first, middle, last = points
    a, b, c = VALUE[0]
    return (a * first + c * last, b * (first + last) + middle, c * first + a * last)


def slope_of(nodes):
    first, middle, last = nodes
    a, b, c = SLOPE[0]
    scaled = b * middle
    return (a * first + scaled + c * last, last - first, -c * first - scaled - a * last)


def slope_back(points):
    first, middle, last = points
    a, b, c = SLOPE[0]
    return (a * first - middle - c * last, b * (first - last), c * first + middle - a * last)


def turn(array, shift):
    return pltpu.roll(array, shift % array.shape[-1], array.ndim - 1)


def even_lanes(rows):
    return lax.broadcasted_iota(jnp.int32, (rows, 128), 1) % 2 == 0


def depth_value(nodes, even, one, two):
    a, b, c = VALUE[0]
    scaled = b * one
    return jnp.where(even, a * nodes + scaled + c * two, nodes), c * nodes + scaled + a * two


def depth_value_back(near, far, even):
    a, b, c = VALUE[0]
    near_even = jnp.where(even, near, 0.0)
    ahead = turn(b * (near_even + far), 1) + turn(c * near_even + a * far, 2)
    return jnp.where(even, a * near + c * far, near) + ahead


def corners(ref, c, packs, rows):
    out = []
    for i in range(3):
        line = []
        for j in range(3):
            parts = [ref[c, 2 * zone + i, pl.ds(j, rows, stride=2), :] for zone in packs]
            line.append(parts[0] if len(parts) == 1 else jnp.concatenate(parts, 0))
        out.append(line)
    return out


def scatter(ref, c, packs, rows, nodes):
    for i in range(3):
        for j in range(3):
            for at, zone in enumerate(packs):
                part = nodes[i][j][at * rows : (at + 1) * rows]
                spot = (c, 2 * zone + i, pl.ds(j, rows, stride=2), slice(None))
                ref[spot] = ref[spot] + part


def mass_nodes(nodes, near_mass, far_mass, even):
    near = [[None] * 3 for _ in range(3)]
    far = [[None] * 3 for _ in range(3)]
    for i in range(3):
        for j in range(3):
            u = nodes[i][j]
            near[i][j], far[i][j] = depth_value(u, even, turn(u, -1), turn(u, -2))
    sides = []
    for field, mass in ((near, near_mass), (far, far_mass)):
        field = [value_of(line) for line in field]
        field = [value_of([field[i][j] for i in range(3)]) for j in range(3)]
        field = [[field[j][i] * mass[3 * i + j] for j in range(3)] for i in range(3)]
        field = [value_back(line) for line in field]
        field = [value_back([field[i][j] for i in range(3)]) for j in range(3)]
        sides.append(field)
    return [[depth_value_back(sides[0][j][i], sides[1][j][i], even) for j in range(3)] for i in range(3)]


def spread_tables():
    zone = lax.broadcasted_iota(jnp.int32, (64, 128), 0)
    lane = lax.broadcasted_iota(jnp.int32, (64, 128), 1)
    one, zero = jnp.float32(1.0), jnp.float32(0.0)
    even = jnp.where(lane == 2 * zone, one, zero)
    odd = jnp.where(lane == 2 * zone + 1, one, zero)
    return even, odd


def collect_tables(which):
    lane = lax.broadcasted_iota(jnp.int32, (128, 64), 0)
    zone = lax.broadcasted_iota(jnp.int32, (128, 64), 1)
    even, odd = lane == 2 * zone, lane == 2 * zone + 1
    near = jnp.where(even, LINEAR[0][which], jnp.where(odd, LINEAR[1][which], 0.0))
    far = jnp.where(even, LINEAR[2][which], 0.0)
    return near.astype(jnp.float32), far.astype(jnp.float32)


def dot32(left, right):
    return jnp.dot(left, right, precision=highest, preferred_element_type=jnp.float32)


def force_kernel(place, disp, vel, energy, rho, share, portion, ident, mix, force, rate, near_out, far_out, inner, outer, grad, work):
    packs, rows = (0, 1), energy.shape[2]
    count = 2 * rows
    even = even_lanes(count)

    def packed(ref, at):
        return jnp.concatenate([ref[at, 0], ref[at, 1]], 0)

    even_table, odd_table = spread_tables()
    both_table = even_table + odd_table
    material = jnp.concatenate([ident[0], ident[1]], 0)
    present = [
        jnp.where((packed(mix, m) == 1) | (material == m), 1.0, 0.0).astype(jnp.float32) for m in range(MATS)
    ]
    weighted = [present[m] * packed(share, m) for m in range(MATS)]
    weight_sum = weighted[0] + weighted[1] + weighted[2] + weighted[3]
    present_sum = present[0] + present[1] + present[2] + present[3]
    zone_rows = [
        (gammas[m] - 1.0) * (weighted[m] / weight_sum * packed(portion, m)) for m in range(MATS)
    ]
    zone_rows += [present[m] / present_sum for m in range(MATS)]
    zone_rows += [packed(energy, j) for j in range(8)]
    wide = dot32(jnp.concatenate(zone_rows, 0), both_table)
    wide = [wide[count * k : count * (k + 1)] for k in range(16)]
    loads, start, corner_energy = wide[:4], wide[4:8], wide[8:]
    rho_rows = [jnp.concatenate([packed(rho, 3 * p + k) for p in range(9)], 0) for k in range(3)]
    near_rho = dot32(rho_rows[0], even_table) + dot32(rho_rows[1], odd_table)
    far_rho = dot32(rho_rows[2], even_table)
    near_rho = [near_rho[count * p : count * (p + 1)] for p in range(9)]
    far_rho = [far_rho[count * p : count * (p + 1)] for p in range(9)]
    near_weight = jnp.where(even, QUAD[0], QUAD[1])
    far_weight = jnp.where(even, QUAD[2], 0.0)
    near_point = jnp.where(even, POINTS[0], POINTS[1])
    a, b, c = SLOPE[0]

    for field, ref in enumerate((disp, vel)):
        for comp in range(3):
            nodes = corners(ref, comp, packs, rows)
            values = [[None] * 3 for _ in range(3)], [[None] * 3 for _ in range(3)]
            slopes = [[None] * 3 for _ in range(3)], [[None] * 3 for _ in range(3)]
            for i in range(3):
                for j in range(3):
                    u = nodes[i][j]
                    one, two = turn(u, -1), turn(u, -2)
                    near, far = depth_value(u, even, one, two)
                    values[0][i][j], values[1][i][j] = near, jnp.where(even, far, 0.0)
                    scaled = b * one
                    slopes[0][i][j] = jnp.where(even, a * u + scaled + c * two, one - turn(u, 1))
                    slopes[1][i][j] = jnp.where(even, -c * u - scaled - a * two, 0.0)
            for side in range(2):
                plain = [value_of(line) for line in values[side]]
                sloped = [slope_of(line) for line in values[side]]
                deep = [value_of(line) for line in slopes[side]]
                for j in range(3):
                    along = (
                        slope_of([plain[i][j] for i in range(3)]),
                        value_of([sloped[i][j] for i in range(3)]),
                        value_of([deep[i][j] for i in range(3)]),
                    )
                    for d in range(3):
                        for i in range(3):
                            grad[field, side, 3 * i + j, 3 * comp + d] = along[d][i]

    for i in range(3):
        for j in range(3):
            spot = 3 * i + j
            plane = QUAD[i] * QUAD[j]
            mixed = []
            for k in range(2):
                low = LINEAR[j][0] * corner_energy[k] + LINEAR[j][1] * corner_energy[2 + k]
                high = LINEAR[j][0] * corner_energy[4 + k] + LINEAR[j][1] * corner_energy[6 + k]
                mixed.append(LINEAR[i][0] * low + LINEAR[i][1] * high)
            rise = mixed[1] - mixed[0]
            for side in range(2):
                weight = plane * (near_weight if side == 0 else far_weight)
                density_weight = near_rho[spot] if side == 0 else far_rho[spot]
                point = near_point if side == 0 else POINTS[2]
                jac = [[grad[0, side, spot, 3 * cc + d] + (1.0 if cc == d else 0.0) for d in range(3)] for cc in range(3)]
                adj = [
                    [
                        jac[(line + 1) % 3][(col + 1) % 3] * jac[(line + 2) % 3][(col + 2) % 3]
                        - jac[(line + 1) % 3][(col + 2) % 3] * jac[(line + 2) % 3][(col + 1) % 3]
                        for line in range(3)
                    ]
                    for col in range(3)
                ]
                determinant = jac[0][0] * adj[0][0] + jac[0][1] * adj[1][0] + jac[0][2] * adj[2][0]
                scale = density_weight / determinant * (mixed[0] + point * rise)
                load = [loads[m] * scale for m in range(MATS)]
                fraction = list(start)
                for _ in range(EQ_ITERS):
                    grown = [
                        jnp.sqrt(fraction[m] * (load[m] + cold_terms[m] * fraction[m])) for m in range(MATS)
                    ]
                    inverse = 1.0 / (grown[0] + grown[1] + grown[2] + grown[3])
                    fraction = [grown[m] * inverse for m in range(MATS)]
                terms = [load[m] + cold_terms[m] * fraction[m] for m in range(MATS)]
                stress = weight * (terms[0] + terms[1] + terms[2] + terms[3])
                divergence = 0.0
                for cc in range(3):
                    for d in range(3):
                        divergence = divergence + grad[1, side, spot, 3 * cc + d] * adj[d][cc]
                work[side, spot] = stress * divergence
                for cc in range(3):
                    for d in range(3):
                        grad[0, side, spot, 3 * cc + d] = stress * adj[d][cc]
                (near_out if side == 0 else far_out)[spot] = weight * density_weight

    force[...] = jnp.zeros_like(force)
    for comp in range(3):
        plain = [[None] * 3 for _ in range(3)], [[None] * 3 for _ in range(3)]
        deep = [[None] * 3 for _ in range(3)], [[None] * 3 for _ in range(3)]
        for side in range(2):
            lines = []
            for j in range(3):
                part = [[grad[0, side, 3 * i + j, 3 * comp + d] for i in range(3)] for d in range(3)]
                lines.append((slope_back(part[0]), value_back(part[1]), value_back(part[2])))
            for i in range(3):
                first = value_back([lines[j][0][i] for j in range(3)])
                second = slope_back([lines[j][1][i] for j in range(3)])
                third = value_back([lines[j][2][i] for j in range(3)])
                for j in range(3):
                    plain[side][i][j] = first[j] + second[j]
                    deep[side][i][j] = third[j]
        out = [[None] * 3 for _ in range(3)]
        va, vb, vc = VALUE[0]
        for i in range(3):
            for j in range(3):
                near, far = plain[0][i][j], plain[1][i][j]
                near_s, far_s = deep[0][i][j], deep[1][i][j]
                near_even = jnp.where(even, near, 0.0)
                near_s_even = jnp.where(even, near_s, 0.0)
                here = jnp.where(even, va * near + vc * far + a * near_s - c * far_s, near)
                next_one = jnp.where(even, vb * (near + far) + b * (near_s - far_s), near_s)
                next_two = vc * near_even + va * far + c * near_s_even - a * far_s
                behind = jnp.where(even, 0.0, near_s)
                out[i][j] = here + turn(next_one, 1) + turn(next_two, 2) - turn(behind, -1)
        scatter(force, comp, packs, rows, out)

    def collected(read):
        lines = [[], []]
        for side in range(2):
            for jx in range(2):
                for jy in range(2):
                    value = None
                    for i in range(3):
                        inner = None
                        for j in range(3):
                            term = LINEAR[j][jy] * read(side, 3 * i + j)
                            inner = term if inner is None else inner + term
                        inner = LINEAR[i][jx] * inner
                        value = inner if value is None else value + inner
                    lines[side].append(value)
        near, far = jnp.concatenate(lines[0], 0), jnp.concatenate(lines[1], 0)
        out = []
        for jz in range(2):
            near_table, far_table = collect_tables(jz)
            out.append(dot32(near, near_table) + dot32(far, far_table))
        return out

    done = collected(lambda side, spot: work[side, spot])
    lumped = collected(lambda side, spot: (near_out if side == 0 else far_out)[spot])
    for jz in range(2):
        ratio = -done[jz] / lumped[jz]
        for jxy in range(4):
            for zone in range(2):
                base = count * jxy + rows * zone
                rate[2 * jxy + jz, zone] = ratio[base : base + rows]

    def pack(ref, high):
        nodes_at, zones_at = (4, 2) if high else (0, 0)
        ref[75:80] = jnp.zeros((5, 128), jnp.float32)
        for x in range(5):
            for comp in range(3):
                spot = 5 * (3 * x + comp)
                ref[spot : spot + 5] = force[comp, x, nodes_at : nodes_at + 5, :]
        for zone in range(2):
            for p in range(18):
                spot = 80 + 2 * (18 * zone + p)
                source = near_out if p < 9 else far_out
                base = rows * zone + zones_at
                ref[spot : spot + 2] = source[p % 9, base : base + 2, :]

    @pl.when(place[1] == 0)
    def _():
        pack(inner, True)
        pack(outer, False)

    @pl.when(place[1] == 1)
    def _():
        pack(inner, False)
        pack(outer, True)


LAYER = 56
MASS_AT = 5 * LAYER
BLOCK = MASS_AT + 8 * 36


def widen_kernel(place, inner, outer, force, near, far, wide):
    def fill(lower, upper):
        for x in range(5):
            for comp in range(3):
                base, spot = LAYER * x + 17 * comp, 5 * (3 * x + comp)
                wide[base : base + 4] = lower[spot : spot + 4]
                wide[base + 4 : base + 5] = lower[spot + 4 : spot + 5] + force[comp, x, 0:1, :]
                wide[base + 5 : base + 12] = force[comp, x, 1:8, :]
                wide[base + 12 : base + 13] = force[comp, x, 8:9, :] + upper[spot : spot + 1]
                wide[base + 13 : base + 17] = upper[spot + 1 : spot + 5]
            wide[LAYER * x + 51 : LAYER * (x + 1)] = jnp.zeros((5, 128), jnp.float32)
        for zone in range(2):
            for p in range(18):
                base, spot = MASS_AT + 8 * (18 * zone + p), 80 + 2 * (18 * zone + p)
                source = near if p < 9 else far
                wide[base : base + 2] = lower[spot : spot + 2]
                wide[base + 2 : base + 6] = source[p % 9, 4 * zone : 4 * zone + 4, :]
                wide[base + 6 : base + 8] = upper[spot : spot + 2]

    @pl.when(place[1] == 0)
    def _():
        fill(outer.at[0], inner.at[1])

    @pl.when(place[1] == 1)
    def _():
        fill(inner.at[0], outer.at[1])


def close_kernel(place, pair, wide, closed):
    shared = pair[0, 4 * LAYER : 5 * LAYER] + pair[1, 0:LAYER]
    closed[...] = wide[...]

    @pl.when(place[0] == 0)
    def _():
        closed[4 * LAYER : 5 * LAYER] = shared

    @pl.when(place[0] == 1)
    def _():
        closed[0:LAYER] = shared


def krylov_kernel(place, pair, cross, edges, t0, t1, t2, partial, products, node, image, second, mass):
    def fill(layers, blocks):
        for at, (ref, base) in enumerate(layers):
            for comp in range(3):
                spot = base + 17 * comp
                node[comp, at] = ref[spot : spot + 17]
        for at, ref in enumerate(blocks):
            for k in range(2):
                for p in range(18):
                    spot = MASS_AT + 8 * (18 * k + p)
                    mass[2 * at + k, p] = ref[spot : spot + 8]

    shared = pair[0, 4 * LAYER : 5 * LAYER] + pair[1, 0:LAYER]

    @pl.when(place[0] == 0)
    def _():
        left, mine, right = cross.at[0], pair.at[0], pair.at[1]
        layers = [(left, LAYER * x) for x in range(4)] + [(edges.at[0], 0)]
        layers += [(mine, LAYER * x) for x in (1, 2, 3, 4)] + [(right, LAYER * x) for x in (1, 2, 3)]
        fill(layers + [(edges.at[1], 0)], (left, mine, right))
        for comp in range(3):
            node[comp, 8] = shared[17 * comp : 17 * comp + 17]

    @pl.when(place[0] == 1)
    def _():
        left, mine, right = pair.at[0], pair.at[1], cross.at[1]
        layers = [(edges.at[0], 0)] + [(left, LAYER * x) for x in (1, 2, 3, 4)]
        layers += [(mine, LAYER * x) for x in (1, 2, 3)] + [(edges.at[1], 0)]
        fill(layers + [(right, LAYER * x) for x in (1, 2, 3, 4)], (left, mine, right))
        for comp in range(3):
            node[comp, 4] = shared[17 * comp : 17 * comp + 17]

    def apply(source, target, comp, zones, start, rows):
        even = even_lanes(rows)
        first = start // 2
        for zone in zones:
            near = [mass[zone, p, first : first + rows, :] for p in range(9)]
            far = [mass[zone, 9 + p, first : first + rows, :] for p in range(9)]
            spots = [
                [(comp, 2 * zone + i, pl.ds(start + j, rows, stride=2), slice(None)) for j in range(3)]
                for i in range(3)
            ]
            out = mass_nodes([[source[spots[i][j]] for j in range(3)] for i in range(3)], near, far, even)
            for i in range(3):
                for j in range(3):
                    target[spots[i][j]] = target[spots[i][j]] + out[i][j]

    partial[...] = jnp.zeros_like(partial)
    lane = lax.broadcasted_iota(jnp.int32, (1, 128), 1)
    sums = [None] * 9

    def add(at, left, right):
        term = left * right
        term = jnp.sum(term, 0, keepdims=True)
        sums[at] = term if sums[at] is None else sums[at] + term

    for comp in range(3):
        image[comp] = jnp.zeros(image.shape[1:], jnp.float32)
        apply(node, image, comp, range(6), 0, 8)
        for x in range(2, 11):
            second[comp, x] = (1.0 / HALF_WIDTH) * image[comp, x] - (CENTER / HALF_WIDTH) * node[comp, x]
        image[comp] = jnp.zeros(image.shape[1:], jnp.float32)
        apply(second, image, comp, range(1, 5), 2, 6)
        for x in range(4, 9):
            t0[comp, x - 4] = node[comp, x, 4:13, :]
            t1[comp, x - 4] = second[comp, x, 4:13, :]
            t2[comp, x - 4] = (
                (2.0 / HALF_WIDTH) * image[comp, x, 4:13, :]
                - (2.0 * CENTER / HALF_WIDTH) * second[comp, x, 4:13, :]
                - node[comp, x, 4:13, :]
            )
        near = [jnp.concatenate([mass[2, p, 2:6, :], mass[3, p, 2:6, :]], 0) for p in range(9)]
        far = [jnp.concatenate([mass[2, 9 + p, 2:6, :], mass[3, 9 + p, 2:6, :]], 0) for p in range(9)]
        nodes = corners(t2, comp, (0, 1), 4)
        scatter(partial, comp, (0, 1), 4, mass_nodes(nodes, near, far, even_lanes(8)))
        for x in range(5):
            fields = [ref[comp, x] for ref in (t0, t1, t2)]
            last = partial[comp, x]
            for i in range(3):
                add(6 + i, fields[i], last)
            if x < 4:
                owned = [v[0:8] for v in fields]
                for at, (i, j) in enumerate(((0, 0), (0, 1), (0, 2), (1, 1), (1, 2), (2, 2))):
                    add(at, owned[i], owned[j])
    value = [jnp.sum(v, 1, keepdims=True) for v in sums]
    gram = {(0, 0): value[0], (0, 1): value[1], (0, 2): value[2], (1, 1): value[3], (1, 2): value[4], (2, 2): value[5]}
    for i in range(3):
        gram[(i, 3)] = (
            (2.0 / HALF_WIDTH) * value[6 + i]
            - (2.0 * CENTER / HALF_WIDTH) * gram[(i, 2)]
            - gram[(min(i, 1), max(i, 1))]
        )
    row = jnp.zeros((1, 128), jnp.float32)
    for at, spot in enumerate(PAIRS):
        row = jnp.where(lane == at, gram[spot], row)
    products[...] = row


def finish_kernel(place, gathered, image, t0, t1, t2, accel, residual):
    row = gathered[0, 15:16, :]
    for peer in range(1, gathered.shape[0]):
        row = row + gathered[peer, 15:16, :]
    gram = {pair: row[:, at : at + 1] for at, pair in enumerate(PAIRS)}
    accel_of, residual_of = cg_coefficients(gram)
    low, high = gathered.at[place[2]], gathered.at[place[3]]
    for comp in range(3):
        for x in range(5):
            spot = 5 * comp + x
            last = image[comp, x]
            at = lax.broadcasted_iota(jnp.int32, last.shape, 0)
            last = last + jnp.where(at == 0, low[spot : spot + 1, :], 0.0)
            last = last + jnp.where(at == 8, high[spot : spot + 1, :], 0.0)
            parts = [t0[comp, x], t1[comp, x], t2[comp, x]]
            parts.append((2.0 / HALF_WIDTH) * last - (2.0 * CENTER / HALF_WIDTH) * parts[2] - parts[1])
            accel[comp, x] = accel_of[0] * parts[0] + accel_of[1] * parts[1] + accel_of[2] * parts[2]
            residual[comp, x] = (
                residual_of[0] * parts[0]
                + residual_of[1] * parts[1]
                + residual_of[2] * parts[2]
                + residual_of[3] * parts[3]
            )


CENTER = 0.196
HALF_WIDTH = 0.194
PAIRS = ((0, 0), (0, 1), (0, 2), (0, 3), (1, 1), (1, 2), (1, 3), (2, 2), (2, 3))


def dot_in(gram, left, right):
    value = 0.0
    for i in range(4):
        for j in range(4):
            if left[i] is None or right[j] is None or (i == 3 and j == 3):
                continue
            value = value + gram[(min(i, j), max(i, j))] * left[i] * right[j]
    return value


def axpy(scale, left, right):
    out = []
    for a, b in zip(left, right):
        if a is None:
            out.append(b)
        elif b is None:
            out.append(scale * a)
        else:
            out.append(scale * a + b)
    return out


def mapped_coefficients(p):
    p0, p1, p2 = (0.0 if v is None else v for v in p[:3])
    shifted = [0.5 * p1, p0 + 0.5 * p2, 0.5 * p1, 0.5 * p2]
    return [HALF_WIDTH * b + CENTER * a for a, b in zip((p0, p1, p2, 0.0), shifted)]


def cg_coefficients(gram):
    accel = [0.0, 0.0, 0.0, 0.0]
    residual = [1.0, 0.0, 0.0, 0.0]
    direction = residual
    norm_now = gram[(0, 0)]
    for sweep_at in range(CG_ITERS):
        mapped = mapped_coefficients(direction)
        step = norm_now / dot_in(gram, direction, mapped)
        accel = axpy(step, direction, accel)
        residual = axpy(-step, mapped, residual)
        if sweep_at + 1 < CG_ITERS:
            norm_next = dot_in(gram, residual, residual)
            direction = axpy(norm_next / norm_now, direction, residual)
            norm_now = norm_next
    return accel, residual


def local_call(kernel, name, outs, scratch, place, *operands):
    return pl.pallas_call(
        kernel,
        out_shape=[jax.ShapeDtypeStruct(shape, jnp.float32) for shape in outs],
        in_specs=[pl.BlockSpec(memory_space=pltpu.SMEM)]
        + [pl.BlockSpec(memory_space=pltpu.VMEM) for _ in operands],
        scratch_shapes=[pltpu.VMEM(shape, jnp.float32) for shape in scratch],
        name=name,
    )(place, *operands)


def pair_gather(block, axes, offset):
    return lax.all_gather(block, axes, axis_index_groups=pair_groups(axes, offset))


def per_device(
    velocity, displacement, energy, rho_weight, mass_share, energy_share, material_id, mix_mask
):
    field = velocity.shape
    subs = lax.axis_size("sub")
    at_sub = lax.axis_index("sub")
    below, above = (at_sub + subs - 1) % subs, (at_sub + 1) % subs
    place = jnp.stack([lax.axis_index(DOM) % 2, at_sub % 2, below, above]).astype(jnp.int32)
    mass = (9, 8, 128)
    halo = (152, 128)
    partial, energy_rate, near_mass, far_mass, inner, outer = local_call(
        force_kernel,
        "force",
        (field, energy.shape, mass, mass, halo, halo),
        ((2, 2, 9, 9, 8, 128), (2, 9, 8, 128)),
        place, displacement, velocity, energy, rho_weight, mass_share, energy_share, material_id, mix_mask,
    )
    inner = pair_gather(inner, ("sub",), 0)
    outer = pair_gather(outer, ("sub",), 1)
    (wide,) = local_call(
        widen_kernel, "widen", ((BLOCK, 128),), (), place, inner, outer, partial, near_mass, far_mass
    )
    pair = pair_gather(wide, DOM, 0)
    (closed,) = local_call(close_kernel, "close", ((BLOCK, 128),), (), place, pair, wide)
    cross = pair_gather(closed, DOM, 1)
    edges = pair_gather(cross[0, 4 * LAYER : 5 * LAYER] + cross[1, :LAYER], DOM, 0)
    extended = (3, 13, 17, 128)
    t0, t1, t2, partial, products = local_call(
        krylov_kernel,
        "krylov",
        (field, field, field, field, (1, 128)),
        (extended, extended, extended, (6, 18, 8, 128)),
        place, pair, cross, edges,
    )
    image = join_axis(partial, DOM, 1)
    count = lax.axis_size(DOM)
    spread = jnp.broadcast_to(products[:, :16], (count, 16))
    row = jnp.sum(lax.all_to_all(spread, DOM, 0, 0, tiled=True), 0)
    row = jnp.pad(row, (0, 112))[None]
    low = jnp.concatenate([image[:, :, 0].reshape(15, 128), row], 0)
    high = jnp.concatenate([image[:, :, 8].reshape(15, 128), row], 0)
    peer = jnp.arange(subs, dtype=jnp.int32)[:, None, None]
    gathered = lax.all_to_all(jnp.where(peer == above, high, low), "sub", 0, 0, tiled=True)
    accel, residual = local_call(
        finish_kernel, "finish", (field, field), (), place, gathered, image, t0, t1, t2
    )
    return (accel, residual, energy_rate)


def solution(mesh):
    torus = Mesh(
        mesh.devices.reshape((8, 4, 2, mesh.shape["sub"]) if mesh.shape["dom"] == 64 else (1, 1, 2, mesh.shape["sub"])), ("dom_0", "dom_1", "dom_2", "sub")
    )
    return jax.shard_map(
        per_device,
        mesh=torus,
        in_specs=(
            P(None, DOM, "sub", None),
            P(None, DOM, "sub", None),
            P(None, DOM, "sub", None),
            P(None, DOM, "sub", None),
            P(None, DOM, "sub", None),
            P(None, DOM, "sub", None),
            P(DOM, "sub", None),
            P(None, DOM, "sub", None),
        ),
        out_specs=(P(None, DOM, "sub", None), P(None, DOM, "sub", None), P(None, DOM, "sub", None)),
        check_vma=False,
    )
```

```python
import functools
import math

import jax
import jax.numpy as jnp
from jax import lax
from jax.experimental import pallas as pl
from jax.experimental.pallas import tpu as pltpu
from jax.sharding import Mesh
from jax.sharding import PartitionSpec as P

MATS = 4
EQ_ITERS = 4
CG_ITERS = 3
DOM_SUB = ("dom_0", "dom_1", "dom_2", "sub")
DOM = ("dom_0", "dom_1", "dom_2")


gammas = (1.4, 1.67, 2.0, 3.0)
cold_terms = (0.3, 1.2, 0.6, 2.4)
highest = lax.Precision.HIGHEST


def pair_groups(axes, offset):
    count = 1
    for axis in axes:
        count *= lax.axis_size(axis)
    return [[(i + offset) % count, (i + offset + 1) % count] for i in range(0, count, 2)]


ROOT = math.sqrt(0.15)
POINTS = (0.5 - ROOT, 0.5, 0.5 + ROOT)
QUAD = (5.0 / 18.0, 8.0 / 18.0, 5.0 / 18.0)
VALUE = tuple((2.0 * (t - 0.5) * (t - 1.0), -4.0 * t * (t - 1.0), 2.0 * t * (t - 0.5)) for t in POINTS)
SLOPE = tuple((4.0 * t - 3.0, 4.0 - 8.0 * t, 4.0 * t - 1.0) for t in POINTS)
LINEAR = tuple((1.0 - t, t) for t in POINTS)


def value_of(nodes):
    first, middle, last = nodes
    a, b, c = VALUE[0]
    scaled = b * middle
    return (a * first + scaled + c * last, middle, c * first + scaled + a * last)


def value_back(points):
    first, middle, last = points
    a, b, c = VALUE[0]
    return (a * first + c * last, b * (first + last) + middle, c * first + a * last)


def slope_of(nodes):
    first, middle, last = nodes
    a, b, c = SLOPE[0]
    scaled = b * middle
    return (a * first + scaled + c * last, last - first, -c * first - scaled - a * last)


def slope_back(points):
    first, middle, last = points
    a, b, c = SLOPE[0]
    return (a * first - middle - c * last, b * (first - last), c * first + middle - a * last)


def turn(array, shift):
    return pltpu.roll(array, shift % array.shape[-1], array.ndim - 1)


def even_lanes(rows):
    return lax.broadcasted_iota(jnp.int32, (rows, 128), 1) % 2 == 0


def depth_value(nodes, even, one, two):
    a, b, c = VALUE[0]
    scaled = b * one
    return jnp.where(even, a * nodes + scaled + c * two, nodes), c * nodes + scaled + a * two


def depth_value_back(near, far, even):
    a, b, c = VALUE[0]
    near_even = jnp.where(even, near, 0.0)
    ahead = turn(b * (near_even + far), 1) + turn(c * near_even + a * far, 2)
    return jnp.where(even, a * near + c * far, near) + ahead


def corners(ref, c, packs, rows):
    out = []
    for i in range(3):
        line = []
        for j in range(3):
            parts = [ref[c, 2 * zone + i, pl.ds(j, rows, stride=2), :] for zone in packs]
            line.append(parts[0] if len(parts) == 1 else jnp.concatenate(parts, 0))
        out.append(line)
    return out


def scatter(ref, c, packs, rows, nodes):
    for i in range(3):
        for j in range(3):
            for at, zone in enumerate(packs):
                part = nodes[i][j][at * rows : (at + 1) * rows]
                spot = (c, 2 * zone + i, pl.ds(j, rows, stride=2), slice(None))
                ref[spot] = ref[spot] + part


def mass_nodes(nodes, near_mass, far_mass, even):
    near = [[None] * 3 for _ in range(3)]
    far = [[None] * 3 for _ in range(3)]
    for i in range(3):
        for j in range(3):
            u = nodes[i][j]
            near[i][j], far[i][j] = depth_value(u, even, turn(u, -1), turn(u, -2))
    sides = []
    for field, mass in ((near, near_mass), (far, far_mass)):
        field = [value_of(line) for line in field]
        field = [value_of([field[i][j] for i in range(3)]) for j in range(3)]
        field = [[field[j][i] * mass[3 * i + j] for j in range(3)] for i in range(3)]
        field = [value_back(line) for line in field]
        field = [value_back([field[i][j] for i in range(3)]) for j in range(3)]
        sides.append(field)
    return [[depth_value_back(sides[0][j][i], sides[1][j][i], even) for j in range(3)] for i in range(3)]


def spread_tables():
    zone = lax.broadcasted_iota(jnp.int32, (64, 128), 0)
    lane = lax.broadcasted_iota(jnp.int32, (64, 128), 1)
    one, zero = jnp.float32(1.0), jnp.float32(0.0)
    even = jnp.where(lane == 2 * zone, one, zero)
    odd = jnp.where(lane == 2 * zone + 1, one, zero)
    return even, odd


def collect_tables(which):
    lane = lax.broadcasted_iota(jnp.int32, (128, 64), 0)
    zone = lax.broadcasted_iota(jnp.int32, (128, 64), 1)
    even, odd = lane == 2 * zone, lane == 2 * zone + 1
    near = jnp.where(even, LINEAR[0][which], jnp.where(odd, LINEAR[1][which], 0.0))
    far = jnp.where(even, LINEAR[2][which], 0.0)
    return near.astype(jnp.float32), far.astype(jnp.float32)


def dot32(left, right):
    return jnp.dot(left, right, precision=highest, preferred_element_type=jnp.float32)


def force_kernel(disp, vel, energy, rho, share, portion, ident, mix, force, rate, near_out, far_out, inner, outer, grad, work, node):
    packs, rows = (0, 1), energy.shape[2]
    for field, ref in enumerate((disp, vel)):
        for x in range(5):
            for y in range(9):
                for comp in range(3):
                    node[field, comp, x, y : y + 1, :] = ref[x, y, comp : comp + 1, :]
    count = 2 * rows
    even = even_lanes(count)

    def packed(ref, at):
        return jnp.concatenate([ref[at, 0], ref[at, 1]], 0)

    even_table, odd_table = spread_tables()
    both_table = even_table + odd_table
    material = jnp.concatenate([ident[0], ident[1]], 0)
    present = [
        jnp.where((packed(mix, m) == 1) | (material == m), 1.0, 0.0).astype(jnp.float32) for m in range(MATS)
    ]
    weighted = [present[m] * packed(share, m) for m in range(MATS)]
    weight_sum = weighted[0] + weighted[1] + weighted[2] + weighted[3]
    present_sum = present[0] + present[1] + present[2] + present[3]
    zone_rows = [
        (gammas[m] - 1.0) * (weighted[m] / weight_sum * packed(portion, m)) for m in range(MATS)
    ]
    zone_rows += [present[m] / present_sum for m in range(MATS)]
    zone_rows += [packed(energy, j) for j in range(8)]
    wide = dot32(jnp.concatenate(zone_rows, 0), both_table)
    wide = [wide[count * k : count * (k + 1)] for k in range(16)]
    loads, start, corner_energy = wide[:4], wide[4:8], wide[8:]
    rho_rows = [jnp.concatenate([packed(rho, 3 * p + k) for p in range(9)], 0) for k in range(3)]
    near_rho = dot32(rho_rows[0], even_table) + dot32(rho_rows[1], odd_table)
    far_rho = dot32(rho_rows[2], even_table)
    near_rho = [near_rho[count * p : count * (p + 1)] for p in range(9)]
    far_rho = [far_rho[count * p : count * (p + 1)] for p in range(9)]
    near_weight = jnp.where(even, QUAD[0], QUAD[1])
    far_weight = jnp.where(even, QUAD[2], 0.0)
    near_point = jnp.where(even, POINTS[0], POINTS[1])
    a, b, c = SLOPE[0]

    for field in range(2):
        for comp in range(3):
            nodes = corners(node.at[field], comp, packs, rows)
            values = [[None] * 3 for _ in range(3)], [[None] * 3 for _ in range(3)]
            slopes = [[None] * 3 for _ in range(3)], [[None] * 3 for _ in range(3)]
            for i in range(3):
                for j in range(3):
                    u = nodes[i][j]
                    one, two = turn(u, -1), turn(u, -2)
                    near, far = depth_value(u, even, one, two)
                    values[0][i][j], values[1][i][j] = near, jnp.where(even, far, 0.0)
                    scaled = b * one
                    slopes[0][i][j] = jnp.where(even, a * u + scaled + c * two, one - turn(u, 1))
                    slopes[1][i][j] = jnp.where(even, -c * u - scaled - a * two, 0.0)
            for side in range(2):
                plain = [value_of(line) for line in values[side]]
                sloped = [slope_of(line) for line in values[side]]
                deep = [value_of(line) for line in slopes[side]]
                for j in range(3):
                    along = (
                        slope_of([plain[i][j] for i in range(3)]),
                        value_of([sloped[i][j] for i in range(3)]),
                        value_of([deep[i][j] for i in range(3)]),
                    )
                    for d in range(3):
                        for i in range(3):
                            grad[field, side, 3 * i + j, 3 * comp + d] = along[d][i]

    for i in range(3):
        for j in range(3):
            spot = 3 * i + j
            plane = QUAD[i] * QUAD[j]
            mixed = []
            for k in range(2):
                low = LINEAR[j][0] * corner_energy[k] + LINEAR[j][1] * corner_energy[2 + k]
                high = LINEAR[j][0] * corner_energy[4 + k] + LINEAR[j][1] * corner_energy[6 + k]
                mixed.append(LINEAR[i][0] * low + LINEAR[i][1] * high)
            rise = mixed[1] - mixed[0]
            for side in range(2):
                weight = plane * (near_weight if side == 0 else far_weight)
                density_weight = near_rho[spot] if side == 0 else far_rho[spot]
                point = near_point if side == 0 else POINTS[2]
                jac = [[grad[0, side, spot, 3 * cc + d] + (1.0 if cc == d else 0.0) for d in range(3)] for cc in range(3)]
                adj = [
                    [
                        jac[(line + 1) % 3][(col + 1) % 3] * jac[(line + 2) % 3][(col + 2) % 3]
                        - jac[(line + 1) % 3][(col + 2) % 3] * jac[(line + 2) % 3][(col + 1) % 3]
                        for line in range(3)
                    ]
                    for col in range(3)
                ]
                determinant = jac[0][0] * adj[0][0] + jac[0][1] * adj[1][0] + jac[0][2] * adj[2][0]
                scale = density_weight / determinant * (mixed[0] + point * rise)
                load = [loads[m] * scale for m in range(MATS)]
                fraction = list(start)
                for _ in range(EQ_ITERS):
                    grown = [
                        jnp.sqrt(fraction[m] * (load[m] + cold_terms[m] * fraction[m])) for m in range(MATS)
                    ]
                    inverse = 1.0 / (grown[0] + grown[1] + grown[2] + grown[3])
                    fraction = [grown[m] * inverse for m in range(MATS)]
                terms = [load[m] + cold_terms[m] * fraction[m] for m in range(MATS)]
                stress = weight * (terms[0] + terms[1] + terms[2] + terms[3])
                divergence = 0.0
                for cc in range(3):
                    for d in range(3):
                        divergence = divergence + grad[1, side, spot, 3 * cc + d] * adj[d][cc]
                work[side, spot] = stress * divergence
                for cc in range(3):
                    for d in range(3):
                        grad[0, side, spot, 3 * cc + d] = stress * adj[d][cc]
                (near_out if side == 0 else far_out)[spot] = weight * density_weight

    force[...] = jnp.zeros_like(force)
    for comp in range(3):
        plain = [[None] * 3 for _ in range(3)], [[None] * 3 for _ in range(3)]
        deep = [[None] * 3 for _ in range(3)], [[None] * 3 for _ in range(3)]
        for side in range(2):
            lines = []
            for j in range(3):
                part = [[grad[0, side, 3 * i + j, 3 * comp + d] for i in range(3)] for d in range(3)]
                lines.append((slope_back(part[0]), value_back(part[1]), value_back(part[2])))
            for i in range(3):
                first = value_back([lines[j][0][i] for j in range(3)])
                second = slope_back([lines[j][1][i] for j in range(3)])
                third = value_back([lines[j][2][i] for j in range(3)])
                for j in range(3):
                    plain[side][i][j] = first[j] + second[j]
                    deep[side][i][j] = third[j]
        out = [[None] * 3 for _ in range(3)]
        va, vb, vc = VALUE[0]
        for i in range(3):
            for j in range(3):
                near, far = plain[0][i][j], plain[1][i][j]
                near_s, far_s = deep[0][i][j], deep[1][i][j]
                near_even = jnp.where(even, near, 0.0)
                near_s_even = jnp.where(even, near_s, 0.0)
                here = jnp.where(even, va * near + vc * far + a * near_s - c * far_s, near)
                next_one = jnp.where(even, vb * (near + far) + b * (near_s - far_s), near_s)
                next_two = vc * near_even + va * far + c * near_s_even - a * far_s
                behind = jnp.where(even, 0.0, near_s)
                out[i][j] = here + turn(next_one, 1) + turn(next_two, 2) - turn(behind, -1)
        scatter(force, comp, packs, rows, out)

    def collected(read):
        lines = [[], []]
        for side in range(2):
            for jx in range(2):
                for jy in range(2):
                    value = None
                    for i in range(3):
                        inner = None
                        for j in range(3):
                            term = LINEAR[j][jy] * read(side, 3 * i + j)
                            inner = term if inner is None else inner + term
                        inner = LINEAR[i][jx] * inner
                        value = inner if value is None else value + inner
                    lines[side].append(value)
        near, far = jnp.concatenate(lines[0], 0), jnp.concatenate(lines[1], 0)
        out = []
        for jz in range(2):
            near_table, far_table = collect_tables(jz)
            out.append(dot32(near, near_table) + dot32(far, far_table))
        return out

    done = collected(lambda side, spot: work[side, spot])
    lumped = collected(lambda side, spot: (near_out if side == 0 else far_out)[spot])
    for jz in range(2):
        ratio = -done[jz] / lumped[jz]
        for jxy in range(4):
            for zone in range(2):
                base = count * jxy + rows * zone
                rate[2 * jxy + jz, zone] = ratio[base : base + rows]

    def pack(ref, high):
        nodes_at, zones_at = (4, 2) if high else (0, 0)
        ref[75:80] = jnp.zeros((5, 128), jnp.float32)
        for x in range(5):
            for comp in range(3):
                spot = 5 * (3 * x + comp)
                ref[spot : spot + 5] = force[comp, x, nodes_at : nodes_at + 5, :]
        for zone in range(2):
            for p in range(18):
                spot = 80 + 2 * (18 * zone + p)
                source = near_out if p < 9 else far_out
                base = rows * zone + zones_at
                ref[spot : spot + 2] = source[p % 9, base : base + 2, :]

    odd_sub = lax.rem(lax.axis_index("sub"), 2)

    @pl.when(odd_sub == 0)
    def _():
        pack(inner, True)
        pack(outer, False)

    @pl.when(odd_sub == 1)
    def _():
        pack(inner, False)
        pack(outer, True)


LAYER = 56
MASS_AT = 5 * LAYER
BLOCK = MASS_AT + 8 * 36


def widen_kernel(inner, outer, force, near, far, wide):
    def fill(lower, upper):
        for x in range(5):
            for comp in range(3):
                base, spot = LAYER * x + 17 * comp, 5 * (3 * x + comp)
                wide[base : base + 4] = lower[spot : spot + 4]
                wide[base + 4 : base + 5] = lower[spot + 4 : spot + 5] + force[comp, x, 0:1, :]
                wide[base + 5 : base + 12] = force[comp, x, 1:8, :]
                wide[base + 12 : base + 13] = force[comp, x, 8:9, :] + upper[spot : spot + 1]
                wide[base + 13 : base + 17] = upper[spot + 1 : spot + 5]
            wide[LAYER * x + 51 : LAYER * (x + 1)] = jnp.zeros((5, 128), jnp.float32)
        for zone in range(2):
            for p in range(18):
                base, spot = MASS_AT + 8 * (18 * zone + p), 80 + 2 * (18 * zone + p)
                source = near if p < 9 else far
                wide[base : base + 2] = lower[spot : spot + 2]
                wide[base + 2 : base + 6] = source[p % 9, 4 * zone : 4 * zone + 4, :]
                wide[base + 6 : base + 8] = upper[spot : spot + 2]

    odd_sub = lax.rem(lax.axis_index("sub"), 2)

    @pl.when(odd_sub == 0)
    def _():
        fill(outer, inner)

    @pl.when(odd_sub == 1)
    def _():
        fill(inner, outer)


def krylov_kernel(pair, cross, edges, t0, t1, t2, partial, inner, outer, products, node, image, second, mass):
    core = lax.axis_index("dom_2")
    def fill(layers, blocks):
        for at, (ref, base) in enumerate(layers):
            for comp in range(3):
                spot = base + 17 * comp
                node[comp, at] = ref[spot : spot + 17]
        for at, ref in enumerate(blocks):
            for k in range(2):
                for p in range(18):
                    spot = MASS_AT + 8 * (18 * k + p)
                    mass[2 * at + k, p] = ref[spot : spot + 8]

    shared = pair[0, 4 * LAYER : 5 * LAYER] + pair[1, 0:LAYER]

    @pl.when(core == 0)
    def _():
        left, mine, right = cross.at[0], pair.at[0], pair.at[1]
        layers = [(left, LAYER * x) for x in range(4)] + [(edges.at[0], 0)]
        layers += [(mine, LAYER * x) for x in (1, 2, 3, 4)] + [(right, LAYER * x) for x in (1, 2, 3)]
        fill(layers + [(edges.at[1], 0)], (left, mine, right))
        for comp in range(3):
            node[comp, 8] = shared[17 * comp : 17 * comp + 17]

    @pl.when(core == 1)
    def _():
        left, mine, right = pair.at[0], pair.at[1], cross.at[1]
        layers = [(edges.at[0], 0)] + [(left, LAYER * x) for x in (1, 2, 3, 4)]
        layers += [(mine, LAYER * x) for x in (1, 2, 3)] + [(edges.at[1], 0)]
        fill(layers + [(right, LAYER * x) for x in (1, 2, 3, 4)], (left, mine, right))
        for comp in range(3):
            node[comp, 4] = shared[17 * comp : 17 * comp + 17]

    def apply(source, target, comp, zones, start, rows):
        even = even_lanes(rows)
        first = start // 2
        for zone in zones:
            near = [mass[zone, p, first : first + rows, :] for p in range(9)]
            far = [mass[zone, 9 + p, first : first + rows, :] for p in range(9)]
            spots = [
                [(comp, 2 * zone + i, pl.ds(start + j, rows, stride=2), slice(None)) for j in range(3)]
                for i in range(3)
            ]
            out = mass_nodes([[source[spots[i][j]] for j in range(3)] for i in range(3)], near, far, even)
            for i in range(3):
                for j in range(3):
                    target[spots[i][j]] = target[spots[i][j]] + out[i][j]

    partial[...] = jnp.zeros_like(partial)
    lane = lax.broadcasted_iota(jnp.int32, (1, 128), 1)
    sums = [None] * 9

    def add(at, left, right):
        term = left * right
        term = jnp.sum(term, 0, keepdims=True)
        sums[at] = term if sums[at] is None else sums[at] + term

    for comp in range(3):
        image[comp] = jnp.zeros(image.shape[1:], jnp.float32)
        apply(node, image, comp, range(6), 0, 8)
        for x in range(2, 11):
            second[comp, x] = (1.0 / HALF_WIDTH) * image[comp, x] - (CENTER / HALF_WIDTH) * node[comp, x]
        image[comp] = jnp.zeros(image.shape[1:], jnp.float32)
        apply(second, image, comp, range(1, 5), 2, 6)
        for x in range(4, 9):
            t0[comp, x - 4] = node[comp, x, 4:13, :]
            t1[comp, x - 4] = second[comp, x, 4:13, :]
            t2[comp, x - 4] = (
                (2.0 / HALF_WIDTH) * image[comp, x, 4:13, :]
                - (2.0 * CENTER / HALF_WIDTH) * second[comp, x, 4:13, :]
                - node[comp, x, 4:13, :]
            )
        near = [jnp.concatenate([mass[2, p, 2:6, :], mass[3, p, 2:6, :]], 0) for p in range(9)]
        far = [jnp.concatenate([mass[2, 9 + p, 2:6, :], mass[3, 9 + p, 2:6, :]], 0) for p in range(9)]
        nodes = corners(t2, comp, (0, 1), 4)
        scatter(partial, comp, (0, 1), 4, mass_nodes(nodes, near, far, even_lanes(8)))
        for x in range(5):
            fields = [ref[comp, x] for ref in (t0, t1, t2)]
            last = partial[comp, x]
            for i in range(3):
                add(6 + i, fields[i], last)
            if x < 4:
                owned = [v[0:8] for v in fields]
                for at, (i, j) in enumerate(((0, 0), (0, 1), (0, 2), (1, 1), (1, 2), (2, 2))):
                    add(at, owned[i], owned[j])
    value = [jnp.sum(v, 1, keepdims=True) for v in sums]
    gram = {(0, 0): value[0], (0, 1): value[1], (0, 2): value[2], (1, 1): value[3], (1, 2): value[4], (2, 2): value[5]}
    for i in range(3):
        gram[(i, 3)] = (
            (2.0 / HALF_WIDTH) * value[6 + i]
            - (2.0 * CENTER / HALF_WIDTH) * gram[(i, 2)]
            - gram[(min(i, 1), max(i, 1))]
        )
    row = jnp.zeros((1, 128), jnp.float32)
    for at, spot in enumerate(PAIRS):
        row = jnp.where(lane == at, gram[spot], row)
    products[...] = jnp.broadcast_to(row[None, :, :16], products.shape)

    def edge(ref, x):
        ref[27:32] = jnp.zeros((5, 128), jnp.float32)
        for comp in range(3):
            ref[9 * comp : 9 * comp + 9] = partial[comp, x]

    @pl.when(core == 0)
    def _():
        edge(inner, 4)
        edge(outer, 0)

    @pl.when(core == 1)
    def _():
        edge(inner, 0)
        edge(outer, 4)


def finish_kernel(gathered, image, t0, t1, t2, accel, residual):
    row = gathered[0, 15:16, :]
    for peer in range(1, gathered.shape[0]):
        row = row + gathered[peer, 15:16, :]
    gram = {pair: row[:, at : at + 1] for at, pair in enumerate(PAIRS)}
    accel_of, residual_of = cg_coefficients(gram)
    subs = gathered.shape[0]
    at_sub = lax.axis_index("sub")
    low, high = gathered.at[lax.rem(at_sub + subs - 1, subs)], gathered.at[lax.rem(at_sub + 1, subs)]
    for comp in range(3):
        for x in range(5):
            spot = 5 * comp + x
            last = image[comp, x]
            at = lax.broadcasted_iota(jnp.int32, last.shape, 0)
            last = last + jnp.where(at == 0, low[spot : spot + 1, :], 0.0)
            last = last + jnp.where(at == 8, high[spot : spot + 1, :], 0.0)
            parts = [t0[comp, x], t1[comp, x], t2[comp, x]]
            parts.append((2.0 / HALF_WIDTH) * last - (2.0 * CENTER / HALF_WIDTH) * parts[2] - parts[1])
            accel[x, :, comp, :] = accel_of[0] * parts[0] + accel_of[1] * parts[1] + accel_of[2] * parts[2]
            residual[x, :, comp, :] = (
                residual_of[0] * parts[0]
                + residual_of[1] * parts[1]
                + residual_of[2] * parts[2]
                + residual_of[3] * parts[3]
            )


CENTER = 0.196
HALF_WIDTH = 0.194
PAIRS = ((0, 0), (0, 1), (0, 2), (0, 3), (1, 1), (1, 2), (1, 3), (2, 2), (2, 3))


def dot_in(gram, left, right):
    value = 0.0
    for i in range(4):
        for j in range(4):
            if left[i] is None or right[j] is None or (i == 3 and j == 3):
                continue
            value = value + gram[(min(i, j), max(i, j))] * left[i] * right[j]
    return value


def axpy(scale, left, right):
    out = []
    for a, b in zip(left, right):
        if a is None:
            out.append(b)
        elif b is None:
            out.append(scale * a)
        else:
            out.append(scale * a + b)
    return out


def mapped_coefficients(p):
    p0, p1, p2 = (0.0 if v is None else v for v in p[:3])
    shifted = [0.5 * p1, p0 + 0.5 * p2, 0.5 * p1, 0.5 * p2]
    return [HALF_WIDTH * b + CENTER * a for a, b in zip((p0, p1, p2, 0.0), shifted)]


def cg_coefficients(gram):
    accel = [0.0, 0.0, 0.0, 0.0]
    residual = [1.0, 0.0, 0.0, 0.0]
    direction = residual
    norm_now = gram[(0, 0)]
    for sweep_at in range(CG_ITERS):
        mapped = mapped_coefficients(direction)
        step = norm_now / dot_in(gram, direction, mapped)
        accel = axpy(step, direction, accel)
        residual = axpy(-step, mapped, residual)
        if sweep_at + 1 < CG_ITERS:
            norm_next = dot_in(gram, residual, residual)
            direction = axpy(norm_next / norm_now, direction, residual)
            norm_now = norm_next
    return accel, residual


def local_call(kernel, name, outs, scratch, *operands):
    return pl.pallas_call(
        kernel,
        out_shape=[jax.ShapeDtypeStruct(shape, jnp.float32) for shape in outs],
        in_specs=[pl.BlockSpec(memory_space=pltpu.VMEM) for _ in operands],
        out_specs=[pl.BlockSpec(memory_space=pltpu.VMEM) for _ in outs],
        scratch_shapes=[pltpu.VMEM(shape, jnp.float32) for shape in scratch],
        name=name,
    )(*operands)


def pair_gather(block, axes, offset):
    return lax.all_gather(block, axes, axis_index_groups=pair_groups(axes, offset))


def pair_swap(block, axes, offset):
    groups = pair_groups(axes, offset)
    return lax.ppermute(block, axes, [edge for a, b in groups for edge in ((a, b), (b, a))])


def per_device(
    velocity, displacement, energy, rho_weight, mass_share, energy_share, material_id, mix_mask
):
    field = velocity.shape
    turned = (field[1], field[2], field[0], field[3])
    subs = lax.axis_size("sub")
    above = (lax.axis_index("sub") + 1) % subs
    core = lax.axis_index("dom_2")
    mass = (9, 8, 128)
    halo = (152, 128)
    partial, energy_rate, near_mass, far_mass, inner, outer = local_call(
        force_kernel,
        "force",
        (field, energy.shape, mass, mass, halo, halo),
        ((2, 2, 9, 9, 8, 128), (2, 9, 8, 128), (2,) + field),
        jnp.transpose(displacement, (1, 2, 0, 3)),
        jnp.transpose(velocity, (1, 2, 0, 3)),
        energy, rho_weight, mass_share, energy_share, material_id, mix_mask,
    )
    inner = pair_swap(inner, ("sub",), 0)
    outer = pair_swap(outer, ("sub",), 1)
    (wide,) = local_call(
        widen_kernel, "widen", ((BLOCK, 128),), (), inner, outer, partial, near_mass, far_mass
    )
    pair = pair_gather(wide, DOM, 0)
    shared = pair[0, 4 * LAYER : 5 * LAYER] + pair[1, 0:LAYER]
    closed = lax.dynamic_update_slice(wide, shared, (4 * LAYER * (1 - core), 0))
    cross = pair_gather(closed, DOM, 1)
    edges = pair_gather(cross[0, 4 * LAYER : 5 * LAYER] + cross[1, :LAYER], DOM, 0)
    extended = (3, 13, 17, 128)
    count = lax.axis_size(DOM)
    t0, t1, t2, partial, inner, outer, spread = local_call(
        krylov_kernel,
        "krylov",
        (field, field, field, field, (32, 128), (32, 128), (count, 1, 16)),
        (extended, extended, extended, (6, 18, 8, 128)),
        pair, cross, edges,
    )
    inner = pair_gather(inner, DOM, 0)
    outer = pair_gather(outer, DOM, 1)
    inner = (inner[0] + inner[1])[:27].reshape(3, 1, 9, 128)
    outer = (outer[0] + outer[1])[:27].reshape(3, 1, 9, 128)
    low_x, high_x = jnp.where(core == 0, outer, inner), jnp.where(core == 0, inner, outer)
    image = jnp.concatenate([low_x, partial[:, 1:4], high_x], 1)
    row = jnp.sum(lax.all_to_all(spread, DOM, 0, 0, tiled=True), 0)
    row = jnp.pad(row, ((0, 0), (0, 112)))
    low = jnp.concatenate([image[:, :, 0].reshape(15, 128), row], 0)
    high = jnp.concatenate([image[:, :, 8].reshape(15, 128), row], 0)
    peer = jnp.arange(subs, dtype=jnp.int32)[:, None, None]
    gathered = lax.all_to_all(jnp.where(peer == above, high, low), "sub", 0, 0, tiled=True)
    accel, residual = local_call(
        finish_kernel, "finish", (turned, turned), (), gathered, image, t0, t1, t2
    )
    return (jnp.transpose(accel, (2, 0, 1, 3)), jnp.transpose(residual, (2, 0, 1, 3)), energy_rate)


def solution(mesh):
    torus = Mesh(
        mesh.devices.reshape((8, 4, 2, mesh.shape["sub"]) if mesh.shape["dom"] == 64 else (1, 1, 2, mesh.shape["sub"])), ("dom_0", "dom_1", "dom_2", "sub")
    )
    return jax.shard_map(
        per_device,
        mesh=torus,
        in_specs=(
            P(None, DOM, "sub", None),
            P(None, DOM, "sub", None),
            P(None, DOM, "sub", None),
            P(None, DOM, "sub", None),
            P(None, DOM, "sub", None),
            P(None, DOM, "sub", None),
            P(DOM, "sub", None),
            P(None, DOM, "sub", None),
        ),
        out_specs=(P(None, DOM, "sub", None), P(None, DOM, "sub", None), P(None, DOM, "sub", None)),
        check_vma=False,
    )
```

```python
import functools
import math

import jax
import jax.numpy as jnp
from jax import lax
from jax.experimental import pallas as pl
from jax.experimental.pallas import tpu as pltpu
from jax.sharding import Mesh
from jax.sharding import PartitionSpec as P

MATS = 4
EQ_ITERS = 4
CG_ITERS = 3
DOM_SUB = ("dom_0", "dom_1", "dom_2", "sub")
DOM = ("dom_0", "dom_1", "dom_2")


gammas = (1.4, 1.67, 2.0, 3.0)
cold_terms = (0.3, 1.2, 0.6, 2.4)
highest = lax.Precision.HIGHEST


def pair_groups(axes, offset):
    count = 1
    for axis in axes:
        count *= lax.axis_size(axis)
    return [[(i + offset) % count, (i + offset + 1) % count] for i in range(0, count, 2)]


ROOT = math.sqrt(0.15)
POINTS = (0.5 - ROOT, 0.5, 0.5 + ROOT)
QUAD = (5.0 / 18.0, 8.0 / 18.0, 5.0 / 18.0)
VALUE = tuple((2.0 * (t - 0.5) * (t - 1.0), -4.0 * t * (t - 1.0), 2.0 * t * (t - 0.5)) for t in POINTS)
SLOPE = tuple((4.0 * t - 3.0, 4.0 - 8.0 * t, 4.0 * t - 1.0) for t in POINTS)
LINEAR = tuple((1.0 - t, t) for t in POINTS)


def value_of(nodes):
    first, middle, last = nodes
    a, b, c = VALUE[0]
    scaled = b * middle
    return (a * first + scaled + c * last, middle, c * first + scaled + a * last)


def value_back(points):
    first, middle, last = points
    a, b, c = VALUE[0]
    return (a * first + c * last, b * (first + last) + middle, c * first + a * last)


def slope_of(nodes):
    first, middle, last = nodes
    a, b, c = SLOPE[0]
    scaled = b * middle
    return (a * first + scaled + c * last, last - first, -c * first - scaled - a * last)


def slope_back(points):
    first, middle, last = points
    a, b, c = SLOPE[0]
    return (a * first - middle - c * last, b * (first - last), c * first + middle - a * last)


def turn(array, shift):
    return pltpu.roll(array, shift % array.shape[-1], array.ndim - 1)


def even_lanes(rows):
    return lax.broadcasted_iota(jnp.int32, (rows, 128), 1) % 2 == 0


def depth_value(nodes, even, one, two):
    a, b, c = VALUE[0]
    scaled = b * one
    return jnp.where(even, a * nodes + scaled + c * two, nodes), c * nodes + scaled + a * two


def depth_value_back(near, far, even):
    a, b, c = VALUE[0]
    near_even = jnp.where(even, near, 0.0)
    ahead = turn(b * (near_even + far), 1) + turn(c * near_even + a * far, 2)
    return jnp.where(even, a * near + c * far, near) + ahead


def corners(ref, c, packs, rows):
    out = []
    for i in range(3):
        line = []
        for j in range(3):
            parts = [ref[c, 2 * zone + i, pl.ds(j, rows, stride=2), :] for zone in packs]
            line.append(parts[0] if len(parts) == 1 else jnp.concatenate(parts, 0))
        out.append(line)
    return out


def scatter(ref, c, packs, rows, nodes):
    for i in range(3):
        for j in range(3):
            for at, zone in enumerate(packs):
                part = nodes[i][j][at * rows : (at + 1) * rows]
                spot = (c, 2 * zone + i, pl.ds(j, rows, stride=2), slice(None))
                ref[spot] = ref[spot] + part


def mass_nodes(nodes, near_mass, far_mass, even):
    near = [[None] * 3 for _ in range(3)]
    far = [[None] * 3 for _ in range(3)]
    for i in range(3):
        for j in range(3):
            u = nodes[i][j]
            near[i][j], far[i][j] = depth_value(u, even, turn(u, -1), turn(u, -2))
    sides = []
    for field, mass in ((near, near_mass), (far, far_mass)):
        field = [value_of(line) for line in field]
        field = [value_of([field[i][j] for i in range(3)]) for j in range(3)]
        field = [[field[j][i] * mass[3 * i + j] for j in range(3)] for i in range(3)]
        field = [value_back(line) for line in field]
        field = [value_back([field[i][j] for i in range(3)]) for j in range(3)]
        sides.append(field)
    return [[depth_value_back(sides[0][j][i], sides[1][j][i], even) for j in range(3)] for i in range(3)]


def spread_tables():
    zone = lax.broadcasted_iota(jnp.int32, (64, 128), 0)
    lane = lax.broadcasted_iota(jnp.int32, (64, 128), 1)
    one, zero = jnp.float32(1.0), jnp.float32(0.0)
    even = jnp.where(lane == 2 * zone, one, zero)
    odd = jnp.where(lane == 2 * zone + 1, one, zero)
    return even, odd


def collect_tables(which):
    lane = lax.broadcasted_iota(jnp.int32, (128, 64), 0)
    zone = lax.broadcasted_iota(jnp.int32, (128, 64), 1)
    even, odd = lane == 2 * zone, lane == 2 * zone + 1
    near = jnp.where(even, LINEAR[0][which], jnp.where(odd, LINEAR[1][which], 0.0))
    far = jnp.where(even, LINEAR[2][which], 0.0)
    return near.astype(jnp.float32), far.astype(jnp.float32)


def dot32(left, right):
    return jnp.dot(left, right, precision=highest, preferred_element_type=jnp.float32)


def force_kernel(disp, vel, energy, rho, share, portion, ident, mix, force, rate, near_out, far_out, inner, outer, grad, work, node):
    packs, rows = (0, 1), energy.shape[2]
    for field, ref in enumerate((disp, vel)):
        for x in range(5):
            for y in range(9):
                for comp in range(3):
                    node[field, comp, x, y : y + 1, :] = ref[x, y, comp : comp + 1, :]
    count = 2 * rows
    even = even_lanes(count)

    def packed(ref, at):
        return jnp.concatenate([ref[at, 0], ref[at, 1]], 0)

    even_table, odd_table = spread_tables()
    both_table = even_table + odd_table
    material = jnp.concatenate([ident[0], ident[1]], 0)
    present = [
        jnp.where((packed(mix, m) == 1) | (material == m), 1.0, 0.0).astype(jnp.float32) for m in range(MATS)
    ]
    weighted = [present[m] * packed(share, m) for m in range(MATS)]
    weight_sum = weighted[0] + weighted[1] + weighted[2] + weighted[3]
    present_sum = present[0] + present[1] + present[2] + present[3]
    zone_rows = [
        (gammas[m] - 1.0) * (weighted[m] / weight_sum * packed(portion, m)) for m in range(MATS)
    ]
    zone_rows += [present[m] / present_sum for m in range(MATS)]
    zone_rows += [packed(energy, j) for j in range(8)]
    wide = dot32(jnp.concatenate(zone_rows, 0), both_table)
    wide = [wide[count * k : count * (k + 1)] for k in range(16)]
    loads, start, corner_energy = wide[:4], wide[4:8], wide[8:]
    rho_rows = [jnp.concatenate([packed(rho, 3 * p + k) for p in range(9)], 0) for k in range(3)]
    near_rho = dot32(rho_rows[0], even_table) + dot32(rho_rows[1], odd_table)
    far_rho = dot32(rho_rows[2], even_table)
    near_rho = [near_rho[count * p : count * (p + 1)] for p in range(9)]
    far_rho = [far_rho[count * p : count * (p + 1)] for p in range(9)]
    near_weight = jnp.where(even, QUAD[0], QUAD[1])
    far_weight = jnp.where(even, QUAD[2], 0.0)
    near_point = jnp.where(even, POINTS[0], POINTS[1])
    a, b, c = SLOPE[0]

    for field in range(2):
        for comp in range(3):
            nodes = corners(node.at[field], comp, packs, rows)
            values = [[None] * 3 for _ in range(3)], [[None] * 3 for _ in range(3)]
            slopes = [[None] * 3 for _ in range(3)], [[None] * 3 for _ in range(3)]
            for i in range(3):
                for j in range(3):
                    u = nodes[i][j]
                    one, two = turn(u, -1), turn(u, -2)
                    near, far = depth_value(u, even, one, two)
                    values[0][i][j], values[1][i][j] = near, jnp.where(even, far, 0.0)
                    scaled = b * one
                    slopes[0][i][j] = jnp.where(even, a * u + scaled + c * two, one - turn(u, 1))
                    slopes[1][i][j] = jnp.where(even, -c * u - scaled - a * two, 0.0)
            for side in range(2):
                plain = [value_of(line) for line in values[side]]
                sloped = [slope_of(line) for line in values[side]]
                deep = [value_of(line) for line in slopes[side]]
                for j in range(3):
                    along = (
                        slope_of([plain[i][j] for i in range(3)]),
                        value_of([sloped[i][j] for i in range(3)]),
                        value_of([deep[i][j] for i in range(3)]),
                    )
                    for d in range(3):
                        for i in range(3):
                            grad[field, side, 3 * i + j, 3 * comp + d] = along[d][i]

    for i in range(3):
        for j in range(3):
            spot = 3 * i + j
            plane = QUAD[i] * QUAD[j]
            mixed = []
            for k in range(2):
                low = LINEAR[j][0] * corner_energy[k] + LINEAR[j][1] * corner_energy[2 + k]
                high = LINEAR[j][0] * corner_energy[4 + k] + LINEAR[j][1] * corner_energy[6 + k]
                mixed.append(LINEAR[i][0] * low + LINEAR[i][1] * high)
            rise = mixed[1] - mixed[0]
            for side in range(2):
                weight = plane * (near_weight if side == 0 else far_weight)
                density_weight = near_rho[spot] if side == 0 else far_rho[spot]
                point = near_point if side == 0 else POINTS[2]
                jac = [[grad[0, side, spot, 3 * cc + d] + (1.0 if cc == d else 0.0) for d in range(3)] for cc in range(3)]
                adj = [
                    [
                        jac[(line + 1) % 3][(col + 1) % 3] * jac[(line + 2) % 3][(col + 2) % 3]
                        - jac[(line + 1) % 3][(col + 2) % 3] * jac[(line + 2) % 3][(col + 1) % 3]
                        for line in range(3)
                    ]
                    for col in range(3)
                ]
                determinant = jac[0][0] * adj[0][0] + jac[0][1] * adj[1][0] + jac[0][2] * adj[2][0]
                scale = density_weight / determinant * (mixed[0] + point * rise)
                load = [loads[m] * scale for m in range(MATS)]
                fraction = list(start)
                for _ in range(EQ_ITERS):
                    grown = [
                        jnp.sqrt(fraction[m] * (load[m] + cold_terms[m] * fraction[m])) for m in range(MATS)
                    ]
                    inverse = 1.0 / (grown[0] + grown[1] + grown[2] + grown[3])
                    fraction = [grown[m] * inverse for m in range(MATS)]
                terms = [load[m] + cold_terms[m] * fraction[m] for m in range(MATS)]
                stress = weight * (terms[0] + terms[1] + terms[2] + terms[3])
                divergence = 0.0
                for cc in range(3):
                    for d in range(3):
                        divergence = divergence + grad[1, side, spot, 3 * cc + d] * adj[d][cc]
                work[side, spot] = stress * divergence
                for cc in range(3):
                    for d in range(3):
                        grad[0, side, spot, 3 * cc + d] = stress * adj[d][cc]
                (near_out if side == 0 else far_out)[spot] = weight * density_weight

    force[...] = jnp.zeros_like(force)
    for comp in range(3):
        plain = [[None] * 3 for _ in range(3)], [[None] * 3 for _ in range(3)]
        deep = [[None] * 3 for _ in range(3)], [[None] * 3 for _ in range(3)]
        for side in range(2):
            lines = []
            for j in range(3):
                part = [[grad[0, side, 3 * i + j, 3 * comp + d] for i in range(3)] for d in range(3)]
                lines.append((slope_back(part[0]), value_back(part[1]), value_back(part[2])))
            for i in range(3):
                first = value_back([lines[j][0][i] for j in range(3)])
                second = slope_back([lines[j][1][i] for j in range(3)])
                third = value_back([lines[j][2][i] for j in range(3)])
                for j in range(3):
                    plain[side][i][j] = first[j] + second[j]
                    deep[side][i][j] = third[j]
        out = [[None] * 3 for _ in range(3)]
        va, vb, vc = VALUE[0]
        for i in range(3):
            for j in range(3):
                near, far = plain[0][i][j], plain[1][i][j]
                near_s, far_s = deep[0][i][j], deep[1][i][j]
                near_even = jnp.where(even, near, 0.0)
                near_s_even = jnp.where(even, near_s, 0.0)
                here = jnp.where(even, va * near + vc * far + a * near_s - c * far_s, near)
                next_one = jnp.where(even, vb * (near + far) + b * (near_s - far_s), near_s)
                next_two = vc * near_even + va * far + c * near_s_even - a * far_s
                behind = jnp.where(even, 0.0, near_s)
                out[i][j] = here + turn(next_one, 1) + turn(next_two, 2) - turn(behind, -1)
        scatter(force, comp, packs, rows, out)

    def collected(read):
        lines = [[], []]
        for side in range(2):
            for jx in range(2):
                for jy in range(2):
                    value = None
                    for i in range(3):
                        inner = None
                        for j in range(3):
                            term = LINEAR[j][jy] * read(side, 3 * i + j)
                            inner = term if inner is None else inner + term
                        inner = LINEAR[i][jx] * inner
                        value = inner if value is None else value + inner
                    lines[side].append(value)
        near, far = jnp.concatenate(lines[0], 0), jnp.concatenate(lines[1], 0)
        out = []
        for jz in range(2):
            near_table, far_table = collect_tables(jz)
            out.append(dot32(near, near_table) + dot32(far, far_table))
        return out

    done = collected(lambda side, spot: work[side, spot])
    lumped = collected(lambda side, spot: (near_out if side == 0 else far_out)[spot])
    for jz in range(2):
        ratio = -done[jz] / lumped[jz]
        for jxy in range(4):
            for zone in range(2):
                base = count * jxy + rows * zone
                rate[2 * jxy + jz, zone] = ratio[base : base + rows]

    def pack(ref, high):
        nodes_at, zones_at = (4, 2) if high else (0, 0)
        ref[75:80] = jnp.zeros((5, 128), jnp.float32)
        for x in range(5):
            for comp in range(3):
                spot = 5 * (3 * x + comp)
                ref[spot : spot + 5] = force[comp, x, nodes_at : nodes_at + 5, :]
        for zone in range(2):
            for p in range(18):
                spot = 80 + 2 * (18 * zone + p)
                source = near_out if p < 9 else far_out
                base = rows * zone + zones_at
                ref[spot : spot + 2] = source[p % 9, base : base + 2, :]

    odd_sub = lax.rem(lax.axis_index("sub"), 2)

    @pl.when(odd_sub == 0)
    def _():
        pack(inner, True)
        pack(outer, False)

    @pl.when(odd_sub == 1)
    def _():
        pack(inner, False)
        pack(outer, True)


LAYER = 56
MASS_AT = 5 * LAYER
BLOCK = MASS_AT + 8 * 36


def widen_kernel(inner, outer, force, near, far, wide):
    def fill(lower, upper):
        for x in range(5):
            for comp in range(3):
                base, spot = LAYER * x + 17 * comp, 5 * (3 * x + comp)
                wide[base : base + 4] = lower[spot : spot + 4]
                wide[base + 4 : base + 5] = lower[spot + 4 : spot + 5] + force[comp, x, 0:1, :]
                wide[base + 5 : base + 12] = force[comp, x, 1:8, :]
                wide[base + 12 : base + 13] = force[comp, x, 8:9, :] + upper[spot : spot + 1]
                wide[base + 13 : base + 17] = upper[spot + 1 : spot + 5]
            wide[LAYER * x + 51 : LAYER * (x + 1)] = jnp.zeros((5, 128), jnp.float32)
        for zone in range(2):
            for p in range(18):
                base, spot = MASS_AT + 8 * (18 * zone + p), 80 + 2 * (18 * zone + p)
                source = near if p < 9 else far
                wide[base : base + 2] = lower[spot : spot + 2]
                wide[base + 2 : base + 6] = source[p % 9, 4 * zone : 4 * zone + 4, :]
                wide[base + 6 : base + 8] = upper[spot : spot + 2]

    odd_sub = lax.rem(lax.axis_index("sub"), 2)

    @pl.when(odd_sub == 0)
    def _():
        fill(outer, inner)

    @pl.when(odd_sub == 1)
    def _():
        fill(inner, outer)


def krylov_kernel(pair, cross, edges, t0, t1, t2, partial, inner, outer, products, node, image, second, mass):
    core = lax.axis_index("dom_2")
    def fill(layers, blocks):
        for at, (ref, base) in enumerate(layers):
            for comp in range(3):
                spot = base + 17 * comp
                node[comp, at] = ref[spot : spot + 17]
        for at, ref in enumerate(blocks):
            for k in range(2):
                for p in range(18):
                    spot = MASS_AT + 8 * (18 * k + p)
                    mass[2 * at + k, p] = ref[spot : spot + 8]

    shared = pair[0, 4 * LAYER : 5 * LAYER] + pair[1, 0:LAYER]

    @pl.when(core == 0)
    def _():
        left, mine, right = cross.at[0], pair.at[0], pair.at[1]
        layers = [(left, LAYER * x) for x in range(4)] + [(edges.at[0], 0)]
        layers += [(mine, LAYER * x) for x in (1, 2, 3, 4)] + [(right, LAYER * x) for x in (1, 2, 3)]
        fill(layers + [(edges.at[1], 0)], (left, mine, right))
        for comp in range(3):
            node[comp, 8] = shared[17 * comp : 17 * comp + 17]

    @pl.when(core == 1)
    def _():
        left, mine, right = pair.at[0], pair.at[1], cross.at[1]
        layers = [(edges.at[0], 0)] + [(left, LAYER * x) for x in (1, 2, 3, 4)]
        layers += [(mine, LAYER * x) for x in (1, 2, 3)] + [(edges.at[1], 0)]
        fill(layers + [(right, LAYER * x) for x in (1, 2, 3, 4)], (left, mine, right))
        for comp in range(3):
            node[comp, 4] = shared[17 * comp : 17 * comp + 17]

    def apply(source, target, comp, zones, start, rows):
        even = even_lanes(rows)
        first = start // 2
        for zone in zones:
            near = [mass[zone, p, first : first + rows, :] for p in range(9)]
            far = [mass[zone, 9 + p, first : first + rows, :] for p in range(9)]
            spots = [
                [(comp, 2 * zone + i, pl.ds(start + j, rows, stride=2), slice(None)) for j in range(3)]
                for i in range(3)
            ]
            out = mass_nodes([[source[spots[i][j]] for j in range(3)] for i in range(3)], near, far, even)
            for i in range(3):
                for j in range(3):
                    target[spots[i][j]] = target[spots[i][j]] + out[i][j]

    partial[...] = jnp.zeros_like(partial)
    lane = lax.broadcasted_iota(jnp.int32, (1, 128), 1)
    sums = [None] * 9

    def add(at, left, right):
        term = left * right
        term = jnp.sum(term, 0, keepdims=True)
        sums[at] = term if sums[at] is None else sums[at] + term

    for comp in range(3):
        image[comp] = jnp.zeros(image.shape[1:], jnp.float32)
        apply(node, image, comp, range(6), 0, 8)
        for x in range(2, 11):
            second[comp, x] = (1.0 / HALF_WIDTH) * image[comp, x] - (CENTER / HALF_WIDTH) * node[comp, x]
        image[comp] = jnp.zeros(image.shape[1:], jnp.float32)
        apply(second, image, comp, range(1, 5), 2, 6)
        for x in range(4, 9):
            t0[comp, x - 4] = node[comp, x, 4:13, :]
            t1[comp, x - 4] = second[comp, x, 4:13, :]
            t2[comp, x - 4] = (
                (2.0 / HALF_WIDTH) * image[comp, x, 4:13, :]
                - (2.0 * CENTER / HALF_WIDTH) * second[comp, x, 4:13, :]
                - node[comp, x, 4:13, :]
            )
        near = [jnp.concatenate([mass[2, p, 2:6, :], mass[3, p, 2:6, :]], 0) for p in range(9)]
        far = [jnp.concatenate([mass[2, 9 + p, 2:6, :], mass[3, 9 + p, 2:6, :]], 0) for p in range(9)]
        nodes = corners(t2, comp, (0, 1), 4)
        scatter(partial, comp, (0, 1), 4, mass_nodes(nodes, near, far, even_lanes(8)))
        for x in range(5):
            fields = [ref[comp, x] for ref in (t0, t1, t2)]
            last = partial[comp, x]
            for i in range(3):
                add(6 + i, fields[i], last)
            if x < 4:
                owned = [v[0:8] for v in fields]
                for at, (i, j) in enumerate(((0, 0), (0, 1), (0, 2), (1, 1), (1, 2), (2, 2))):
                    add(at, owned[i], owned[j])
    value = [jnp.sum(v, 1, keepdims=True) for v in sums]
    gram = {(0, 0): value[0], (0, 1): value[1], (0, 2): value[2], (1, 1): value[3], (1, 2): value[4], (2, 2): value[5]}
    for i in range(3):
        gram[(i, 3)] = (
            (2.0 / HALF_WIDTH) * value[6 + i]
            - (2.0 * CENTER / HALF_WIDTH) * gram[(i, 2)]
            - gram[(min(i, 1), max(i, 1))]
        )
    row = jnp.zeros((1, 128), jnp.float32)
    for at, spot in enumerate(PAIRS):
        row = jnp.where(lane == at, gram[spot], row)
    products[...] = jnp.broadcast_to(row[None, :, :16], products.shape)

    def edge(ref, x):
        ref[27:32] = jnp.zeros((5, 128), jnp.float32)
        for comp in range(3):
            ref[9 * comp : 9 * comp + 9] = partial[comp, x]

    @pl.when(core == 0)
    def _():
        edge(inner, 4)
        edge(outer, 0)

    @pl.when(core == 1)
    def _():
        edge(inner, 0)
        edge(outer, 4)


def finish_kernel(gathered, image, t0, t1, t2, accel, residual):
    row = gathered[0, 15:16, :]
    for peer in range(1, gathered.shape[0]):
        row = row + gathered[peer, 15:16, :]
    gram = {pair: row[:, at : at + 1] for at, pair in enumerate(PAIRS)}
    accel_of, residual_of = cg_coefficients(gram)
    subs = gathered.shape[0]
    at_sub = lax.axis_index("sub")
    low, high = gathered.at[lax.rem(at_sub + subs - 1, subs)], gathered.at[lax.rem(at_sub + 1, subs)]
    for comp in range(3):
        for x in range(5):
            spot = 5 * comp + x
            last = image[comp, x]
            at = lax.broadcasted_iota(jnp.int32, last.shape, 0)
            last = last + jnp.where(at == 0, low[spot : spot + 1, :], 0.0)
            last = last + jnp.where(at == 8, high[spot : spot + 1, :], 0.0)
            parts = [t0[comp, x], t1[comp, x], t2[comp, x]]
            parts.append((2.0 / HALF_WIDTH) * last - (2.0 * CENTER / HALF_WIDTH) * parts[2] - parts[1])
            accel[x, :, comp, :] = accel_of[0] * parts[0] + accel_of[1] * parts[1] + accel_of[2] * parts[2]
            residual[x, :, comp, :] = (
                residual_of[0] * parts[0]
                + residual_of[1] * parts[1]
                + residual_of[2] * parts[2]
                + residual_of[3] * parts[3]
            )


CENTER = 0.196
HALF_WIDTH = 0.194
PAIRS = ((0, 0), (0, 1), (0, 2), (0, 3), (1, 1), (1, 2), (1, 3), (2, 2), (2, 3))


def dot_in(gram, left, right):
    value = 0.0
    for i in range(4):
        for j in range(4):
            if left[i] is None or right[j] is None or (i == 3 and j == 3):
                continue
            value = value + gram[(min(i, j), max(i, j))] * left[i] * right[j]
    return value


def axpy(scale, left, right):
    out = []
    for a, b in zip(left, right):
        if a is None:
            out.append(b)
        elif b is None:
            out.append(scale * a)
        else:
            out.append(scale * a + b)
    return out


def mapped_coefficients(p):
    p0, p1, p2 = (0.0 if v is None else v for v in p[:3])
    shifted = [0.5 * p1, p0 + 0.5 * p2, 0.5 * p1, 0.5 * p2]
    return [HALF_WIDTH * b + CENTER * a for a, b in zip((p0, p1, p2, 0.0), shifted)]


def cg_coefficients(gram):
    accel = [0.0, 0.0, 0.0, 0.0]
    residual = [1.0, 0.0, 0.0, 0.0]
    direction = residual
    norm_now = gram[(0, 0)]
    for sweep_at in range(CG_ITERS):
        mapped = mapped_coefficients(direction)
        step = norm_now / dot_in(gram, direction, mapped)
        accel = axpy(step, direction, accel)
        residual = axpy(-step, mapped, residual)
        if sweep_at + 1 < CG_ITERS:
            norm_next = dot_in(gram, residual, residual)
            direction = axpy(norm_next / norm_now, direction, residual)
            norm_now = norm_next
    return accel, residual


def local_call(kernel, name, outs, scratch, *operands):
    return pl.pallas_call(
        kernel,
        out_shape=[jax.ShapeDtypeStruct(shape, jnp.float32) for shape in outs],
        in_specs=[pl.BlockSpec(memory_space=pltpu.VMEM) for _ in operands],
        out_specs=[pl.BlockSpec(memory_space=pltpu.VMEM) for _ in outs],
        scratch_shapes=[pltpu.VMEM(shape, jnp.float32) for shape in scratch],
        compiler_params=pltpu.CompilerParams(vmem_limit_bytes=12 * 1024 * 1024),
        name=name,
    )(*operands)


def pair_gather(block, axes, offset):
    return lax.all_gather(block, axes, axis_index_groups=pair_groups(axes, offset))


def pair_swap(block, axes, offset):
    groups = pair_groups(axes, offset)
    return lax.ppermute(block, axes, [edge for a, b in groups for edge in ((a, b), (b, a))])


def per_device(
    velocity, displacement, energy, rho_weight, mass_share, energy_share, material_id, mix_mask
):
    field = velocity.shape
    turned = (field[1], field[2], field[0], field[3])
    subs = lax.axis_size("sub")
    above = (lax.axis_index("sub") + 1) % subs
    core = lax.axis_index("dom_2")
    mass = (9, 8, 128)
    halo = (152, 128)
    partial, energy_rate, near_mass, far_mass, inner, outer = local_call(
        force_kernel,
        "force",
        (field, energy.shape, mass, mass, halo, halo),
        ((2, 2, 9, 9, 8, 128), (2, 9, 8, 128), (2,) + field),
        jnp.transpose(displacement, (1, 2, 0, 3)),
        jnp.transpose(velocity, (1, 2, 0, 3)),
        energy, rho_weight, mass_share, energy_share, material_id, mix_mask,
    )
    inner = pair_swap(inner, ("sub",), 0)
    outer = pair_swap(outer, ("sub",), 1)
    (wide,) = local_call(
        widen_kernel, "widen", ((BLOCK, 128),), (), inner, outer, partial, near_mass, far_mass
    )
    pair = pair_gather(wide, DOM, 0)
    shared = pair[0, 4 * LAYER : 5 * LAYER] + pair[1, 0:LAYER]
    closed = lax.dynamic_update_slice(wide, shared, (4 * LAYER * (1 - core), 0))
    cross = pair_gather(closed, DOM, 1)
    edges = pair_gather(cross[0, 4 * LAYER : 5 * LAYER] + cross[1, :LAYER], DOM, 0)
    extended = (3, 13, 17, 128)
    count = lax.axis_size(DOM)
    t0, t1, t2, partial, inner, outer, spread = local_call(
        krylov_kernel,
        "krylov",
        (field, field, field, field, (32, 128), (32, 128), (count, 1, 16)),
        (extended, extended, extended, (6, 18, 8, 128)),
        pair, cross, edges,
    )
    inner = pair_gather(inner, DOM, 0)
    outer = pair_gather(outer, DOM, 1)
    inner = (inner[0] + inner[1])[:27].reshape(3, 1, 9, 128)
    outer = (outer[0] + outer[1])[:27].reshape(3, 1, 9, 128)
    low_x, high_x = jnp.where(core == 0, outer, inner), jnp.where(core == 0, inner, outer)
    image = jnp.concatenate([low_x, partial[:, 1:4], high_x], 1)
    row = jnp.sum(lax.all_to_all(spread, DOM, 0, 0, tiled=True), 0)
    row = jnp.pad(row, ((0, 0), (0, 112)))
    low = jnp.concatenate([image[:, :, 0].reshape(15, 128), row], 0)
    high = jnp.concatenate([image[:, :, 8].reshape(15, 128), row], 0)
    peer = jnp.arange(subs, dtype=jnp.int32)[:, None, None]
    gathered = lax.all_to_all(jnp.where(peer == above, high, low), "sub", 0, 0, tiled=True)
    accel, residual = local_call(
        finish_kernel, "finish", (turned, turned), (), gathered, image, t0, t1, t2
    )
    return (jnp.transpose(accel, (2, 0, 1, 3)), jnp.transpose(residual, (2, 0, 1, 3)), energy_rate)


def solution(mesh):
    torus = Mesh(
        mesh.devices.reshape((8, 4, 2, mesh.shape["sub"]) if mesh.shape["dom"] == 64 else (1, 1, 2, mesh.shape["sub"])), ("dom_0", "dom_1", "dom_2", "sub")
    )
    return jax.shard_map(
        per_device,
        mesh=torus,
        in_specs=(
            P(None, DOM, "sub", None),
            P(None, DOM, "sub", None),
            P(None, DOM, "sub", None),
            P(None, DOM, "sub", None),
            P(None, DOM, "sub", None),
            P(None, DOM, "sub", None),
            P(DOM, "sub", None),
            P(None, DOM, "sub", None),
        ),
        out_specs=(P(None, DOM, "sub", None), P(None, DOM, "sub", None), P(None, DOM, "sub", None)),
        check_vma=False,
    )
```

```python
import functools
import math

import jax
import jax.numpy as jnp
from jax import lax
from jax.experimental import pallas as pl
from jax.experimental.pallas import tpu as pltpu
from jax.sharding import Mesh
from jax.sharding import PartitionSpec as P

MATS = 4
EQ_ITERS = 4
CG_ITERS = 3
DOM_SUB = ("dom_0", "dom_1", "dom_2", "sub")
DOM = ("dom_0", "dom_1", "dom_2")


gammas = (1.4, 1.67, 2.0, 3.0)
cold_terms = (0.3, 1.2, 0.6, 2.4)
highest = lax.Precision.HIGHEST


def pair_groups(axes, offset):
    count = 1
    for axis in axes:
        count *= lax.axis_size(axis)
    return [[(i + offset) % count, (i + offset + 1) % count] for i in range(0, count, 2)]


ROOT = math.sqrt(0.15)
POINTS = (0.5 - ROOT, 0.5, 0.5 + ROOT)
QUAD = (5.0 / 18.0, 8.0 / 18.0, 5.0 / 18.0)
VALUE = tuple((2.0 * (t - 0.5) * (t - 1.0), -4.0 * t * (t - 1.0), 2.0 * t * (t - 0.5)) for t in POINTS)
SLOPE = tuple((4.0 * t - 3.0, 4.0 - 8.0 * t, 4.0 * t - 1.0) for t in POINTS)
LINEAR = tuple((1.0 - t, t) for t in POINTS)


def value_of(nodes):
    first, middle, last = nodes
    a, b, c = VALUE[0]
    scaled = b * middle
    return (a * first + scaled + c * last, middle, c * first + scaled + a * last)


def value_back(points):
    first, middle, last = points
    a, b, c = VALUE[0]
    return (a * first + c * last, b * (first + last) + middle, c * first + a * last)


def slope_of(nodes):
    first, middle, last = nodes
    a, b, c = SLOPE[0]
    scaled = b * middle
    return (a * first + scaled + c * last, last - first, -c * first - scaled - a * last)


def slope_back(points):
    first, middle, last = points
    a, b, c = SLOPE[0]
    return (a * first - middle - c * last, b * (first - last), c * first + middle - a * last)


def turn(array, shift):
    return pltpu.roll(array, shift % array.shape[-1], array.ndim - 1)


def even_lanes(rows):
    return lax.broadcasted_iota(jnp.int32, (rows, 128), 1) % 2 == 0


def depth_value(nodes, even, one, two):
    a, b, c = VALUE[0]
    scaled = b * one
    return jnp.where(even, a * nodes + scaled + c * two, nodes), c * nodes + scaled + a * two


def depth_value_back(near, far, even):
    a, b, c = VALUE[0]
    near_even = jnp.where(even, near, 0.0)
    ahead = turn(b * (near_even + far), 1) + turn(c * near_even + a * far, 2)
    return jnp.where(even, a * near + c * far, near) + ahead


def corners(ref, c, packs, rows):
    out = []
    for i in range(3):
        line = []
        for j in range(3):
            parts = [ref[c, 2 * zone + i, pl.ds(j, rows, stride=2), :] for zone in packs]
            line.append(parts[0] if len(parts) == 1 else jnp.concatenate(parts, 0))
        out.append(line)
    return out


def scatter(ref, c, packs, rows, nodes):
    for i in range(3):
        for j in range(3):
            for at, zone in enumerate(packs):
                part = nodes[i][j][at * rows : (at + 1) * rows]
                spot = (c, 2 * zone + i, pl.ds(j, rows, stride=2), slice(None))
                ref[spot] = ref[spot] + part


def mass_nodes(nodes, near_mass, far_mass, even):
    near = [[None] * 3 for _ in range(3)]
    far = [[None] * 3 for _ in range(3)]
    for i in range(3):
        for j in range(3):
            u = nodes[i][j]
            near[i][j], far[i][j] = depth_value(u, even, turn(u, -1), turn(u, -2))
    sides = []
    for field, mass in ((near, near_mass), (far, far_mass)):
        field = [value_of(line) for line in field]
        field = [value_of([field[i][j] for i in range(3)]) for j in range(3)]
        field = [[field[j][i] * mass[3 * i + j] for j in range(3)] for i in range(3)]
        field = [value_back(line) for line in field]
        field = [value_back([field[i][j] for i in range(3)]) for j in range(3)]
        sides.append(field)
    return [[depth_value_back(sides[0][j][i], sides[1][j][i], even) for j in range(3)] for i in range(3)]


def spread_tables():
    zone = lax.broadcasted_iota(jnp.int32, (64, 128), 0)
    lane = lax.broadcasted_iota(jnp.int32, (64, 128), 1)
    one, zero = jnp.float32(1.0), jnp.float32(0.0)
    even = jnp.where(lane == 2 * zone, one, zero)
    odd = jnp.where(lane == 2 * zone + 1, one, zero)
    return even, odd


def collect_tables(which):
    lane = lax.broadcasted_iota(jnp.int32, (128, 64), 0)
    zone = lax.broadcasted_iota(jnp.int32, (128, 64), 1)
    even, odd = lane == 2 * zone, lane == 2 * zone + 1
    near = jnp.where(even, LINEAR[0][which], jnp.where(odd, LINEAR[1][which], 0.0))
    far = jnp.where(even, LINEAR[2][which], 0.0)
    return near.astype(jnp.float32), far.astype(jnp.float32)


def dot32(left, right):
    return jnp.dot(left, right, precision=highest, preferred_element_type=jnp.float32)


def force_kernel(*refs):
    sources, (force, rate, planes, inner, outer) = refs[:8], refs[8:13]
    grad, work, node, sems = refs[13:16] + refs[24:]
    near_out, far_out = planes.at[0:9], planes.at[9:18]
    disp, vel, energy, rho, share, portion, ident, mix = refs[16:24]
    copies = [pltpu.make_async_copy(a, b, sems.at[k]) for k, (a, b) in enumerate(zip(sources, refs[16:24]))]
    for copy in copies:
        copy.start()
    for copy in copies[2:]:
        copy.wait()
    packs, rows = (0, 1), energy.shape[2]
    count = 2 * rows
    even = even_lanes(count)

    def packed(ref, at):
        return jnp.concatenate([ref[at, 0], ref[at, 1]], 0)

    even_table, odd_table = spread_tables()
    both_table = even_table + odd_table
    material = jnp.concatenate([ident[0], ident[1]], 0)
    present = [
        jnp.where((packed(mix, m) == 1) | (material == m), 1.0, 0.0).astype(jnp.float32) for m in range(MATS)
    ]
    weighted = [present[m] * packed(share, m) for m in range(MATS)]
    weight_sum = weighted[0] + weighted[1] + weighted[2] + weighted[3]
    present_sum = present[0] + present[1] + present[2] + present[3]
    zone_rows = [
        (gammas[m] - 1.0) * (weighted[m] / weight_sum * packed(portion, m)) for m in range(MATS)
    ]
    zone_rows += [present[m] / present_sum for m in range(MATS)]
    zone_rows += [packed(energy, j) for j in range(8)]
    wide = dot32(jnp.concatenate(zone_rows, 0), both_table)
    wide = [wide[count * k : count * (k + 1)] for k in range(16)]
    loads, start, corner_energy = wide[:4], wide[4:8], wide[8:]
    rho_rows = [jnp.concatenate([packed(rho, 3 * p + k) for p in range(9)], 0) for k in range(3)]
    near_rho = dot32(rho_rows[0], even_table) + dot32(rho_rows[1], odd_table)
    far_rho = dot32(rho_rows[2], even_table)
    near_rho = [near_rho[count * p : count * (p + 1)] for p in range(9)]
    far_rho = [far_rho[count * p : count * (p + 1)] for p in range(9)]
    near_weight = jnp.where(even, QUAD[0], QUAD[1])
    far_weight = jnp.where(even, QUAD[2], 0.0)
    near_point = jnp.where(even, POINTS[0], POINTS[1])
    a, b, c = SLOPE[0]

    copies[0].wait()
    copies[1].wait()
    for field, ref in enumerate((disp, vel)):
        for x in range(5):
            for y in range(9):
                for comp in range(3):
                    node[field, comp, x, y : y + 1, :] = ref[x, y, comp : comp + 1, :]
    for field in range(2):
        for comp in range(3):
            nodes = corners(node.at[field], comp, packs, rows)
            values = [[None] * 3 for _ in range(3)], [[None] * 3 for _ in range(3)]
            slopes = [[None] * 3 for _ in range(3)], [[None] * 3 for _ in range(3)]
            for i in range(3):
                for j in range(3):
                    u = nodes[i][j]
                    one, two = turn(u, -1), turn(u, -2)
                    near, far = depth_value(u, even, one, two)
                    values[0][i][j], values[1][i][j] = near, jnp.where(even, far, 0.0)
                    scaled = b * one
                    slopes[0][i][j] = jnp.where(even, a * u + scaled + c * two, one - turn(u, 1))
                    slopes[1][i][j] = jnp.where(even, -c * u - scaled - a * two, 0.0)
            for side in range(2):
                plain = [value_of(line) for line in values[side]]
                sloped = [slope_of(line) for line in values[side]]
                deep = [value_of(line) for line in slopes[side]]
                for j in range(3):
                    along = (
                        slope_of([plain[i][j] for i in range(3)]),
                        value_of([sloped[i][j] for i in range(3)]),
                        value_of([deep[i][j] for i in range(3)]),
                    )
                    for d in range(3):
                        for i in range(3):
                            grad[field, side, 3 * i + j, 3 * comp + d] = along[d][i]

    for i in range(3):
        for j in range(3):
            spot = 3 * i + j
            plane = QUAD[i] * QUAD[j]
            mixed = []
            for k in range(2):
                low = LINEAR[j][0] * corner_energy[k] + LINEAR[j][1] * corner_energy[2 + k]
                high = LINEAR[j][0] * corner_energy[4 + k] + LINEAR[j][1] * corner_energy[6 + k]
                mixed.append(LINEAR[i][0] * low + LINEAR[i][1] * high)
            rise = mixed[1] - mixed[0]
            for side in range(2):
                weight = plane * (near_weight if side == 0 else far_weight)
                density_weight = near_rho[spot] if side == 0 else far_rho[spot]
                point = near_point if side == 0 else POINTS[2]
                jac = [[grad[0, side, spot, 3 * cc + d] + (1.0 if cc == d else 0.0) for d in range(3)] for cc in range(3)]
                adj = [
                    [
                        jac[(line + 1) % 3][(col + 1) % 3] * jac[(line + 2) % 3][(col + 2) % 3]
                        - jac[(line + 1) % 3][(col + 2) % 3] * jac[(line + 2) % 3][(col + 1) % 3]
                        for line in range(3)
                    ]
                    for col in range(3)
                ]
                determinant = jac[0][0] * adj[0][0] + jac[0][1] * adj[1][0] + jac[0][2] * adj[2][0]
                scale = density_weight / determinant * (mixed[0] + point * rise)
                load = [loads[m] * scale for m in range(MATS)]
                fraction = list(start)
                for _ in range(EQ_ITERS):
                    grown = [
                        jnp.sqrt(fraction[m] * (load[m] + cold_terms[m] * fraction[m])) for m in range(MATS)
                    ]
                    inverse = 1.0 / (grown[0] + grown[1] + grown[2] + grown[3])
                    fraction = [grown[m] * inverse for m in range(MATS)]
                terms = [load[m] + cold_terms[m] * fraction[m] for m in range(MATS)]
                stress = weight * (terms[0] + terms[1] + terms[2] + terms[3])
                divergence = 0.0
                for cc in range(3):
                    for d in range(3):
                        divergence = divergence + grad[1, side, spot, 3 * cc + d] * adj[d][cc]
                work[side, spot] = stress * divergence
                for cc in range(3):
                    for d in range(3):
                        grad[0, side, spot, 3 * cc + d] = stress * adj[d][cc]
                (near_out if side == 0 else far_out)[spot] = weight * density_weight

    force[...] = jnp.zeros_like(force)
    for comp in range(3):
        plain = [[None] * 3 for _ in range(3)], [[None] * 3 for _ in range(3)]
        deep = [[None] * 3 for _ in range(3)], [[None] * 3 for _ in range(3)]
        for side in range(2):
            lines = []
            for j in range(3):
                part = [[grad[0, side, 3 * i + j, 3 * comp + d] for i in range(3)] for d in range(3)]
                lines.append((slope_back(part[0]), value_back(part[1]), value_back(part[2])))
            for i in range(3):
                first = value_back([lines[j][0][i] for j in range(3)])
                second = slope_back([lines[j][1][i] for j in range(3)])
                third = value_back([lines[j][2][i] for j in range(3)])
                for j in range(3):
                    plain[side][i][j] = first[j] + second[j]
                    deep[side][i][j] = third[j]
        out = [[None] * 3 for _ in range(3)]
        va, vb, vc = VALUE[0]
        for i in range(3):
            for j in range(3):
                near, far = plain[0][i][j], plain[1][i][j]
                near_s, far_s = deep[0][i][j], deep[1][i][j]
                near_even = jnp.where(even, near, 0.0)
                near_s_even = jnp.where(even, near_s, 0.0)
                here = jnp.where(even, va * near + vc * far + a * near_s - c * far_s, near)
                next_one = jnp.where(even, vb * (near + far) + b * (near_s - far_s), near_s)
                next_two = vc * near_even + va * far + c * near_s_even - a * far_s
                behind = jnp.where(even, 0.0, near_s)
                out[i][j] = here + turn(next_one, 1) + turn(next_two, 2) - turn(behind, -1)
        scatter(force, comp, packs, rows, out)

    def collected(read):
        lines = [[], []]
        for side in range(2):
            for jx in range(2):
                for jy in range(2):
                    value = None
                    for i in range(3):
                        inner = None
                        for j in range(3):
                            term = LINEAR[j][jy] * read(side, 3 * i + j)
                            inner = term if inner is None else inner + term
                        inner = LINEAR[i][jx] * inner
                        value = inner if value is None else value + inner
                    lines[side].append(value)
        near, far = jnp.concatenate(lines[0], 0), jnp.concatenate(lines[1], 0)
        out = []
        for jz in range(2):
            near_table, far_table = collect_tables(jz)
            out.append(dot32(near, near_table) + dot32(far, far_table))
        return out

    done = collected(lambda side, spot: work[side, spot])
    lumped = collected(lambda side, spot: (near_out if side == 0 else far_out)[spot])
    for jz in range(2):
        ratio = -done[jz] / lumped[jz]
        for jxy in range(4):
            for zone in range(2):
                base = count * jxy + rows * zone
                rate[2 * jxy + jz, zone] = ratio[base : base + rows]

    def pack(ref, high):
        nodes_at, zones_at = (4, 2) if high else (0, 0)
        ref[75:80] = jnp.zeros((5, 128), jnp.float32)
        for x in range(5):
            for comp in range(3):
                spot = 5 * (3 * x + comp)
                ref[spot : spot + 5] = force[comp, x, nodes_at : nodes_at + 5, :]
        for zone in range(2):
            for p in range(18):
                spot = 80 + 2 * (18 * zone + p)
                source = near_out if p < 9 else far_out
                base = rows * zone + zones_at
                ref[spot : spot + 2] = source[p % 9, base : base + 2, :]

    odd_sub = lax.rem(lax.axis_index("sub"), 2)

    @pl.when(odd_sub == 0)
    def _():
        pack(inner, True)
        pack(outer, False)

    @pl.when(odd_sub == 1)
    def _():
        pack(inner, False)
        pack(outer, True)


LAYER = 56
MASS_AT = 5 * LAYER
BLOCK = MASS_AT + 8 * 36


def widen_kernel(inner, outer, force, planes, wide):
    def fill(lower, upper):
        for x in range(5):
            for comp in range(3):
                base, spot = LAYER * x + 17 * comp, 5 * (3 * x + comp)
                wide[base : base + 4] = lower[spot : spot + 4]
                wide[base + 4 : base + 5] = lower[spot + 4 : spot + 5] + force[comp, x, 0:1, :]
                wide[base + 5 : base + 12] = force[comp, x, 1:8, :]
                wide[base + 12 : base + 13] = force[comp, x, 8:9, :] + upper[spot : spot + 1]
                wide[base + 13 : base + 17] = upper[spot + 1 : spot + 5]
            wide[LAYER * x + 51 : LAYER * (x + 1)] = jnp.zeros((5, 128), jnp.float32)
        for zone in range(2):
            for p in range(18):
                base, spot = MASS_AT + 8 * (18 * zone + p), 80 + 2 * (18 * zone + p)
                wide[base : base + 2] = lower[spot : spot + 2]
                wide[base + 2 : base + 6] = planes[p, 4 * zone : 4 * zone + 4, :]
                wide[base + 6 : base + 8] = upper[spot : spot + 2]

    odd_sub = lax.rem(lax.axis_index("sub"), 2)

    @pl.when(odd_sub == 0)
    def _():
        fill(outer, inner)

    @pl.when(odd_sub == 1)
    def _():
        fill(inner, outer)


def krylov_kernel(pair, cross, edges, t0, t1, t2, partial, inner, outer, products, node, image, second, mass):
    core = lax.axis_index("dom_2")
    def fill(layers, blocks):
        for at, (ref, base) in enumerate(layers):
            for comp in range(3):
                spot = base + 17 * comp
                node[comp, at] = ref[spot : spot + 17]
        for at, ref in enumerate(blocks):
            for k in range(2):
                for p in range(18):
                    spot = MASS_AT + 8 * (18 * k + p)
                    mass[2 * at + k, p] = ref[spot : spot + 8]

    shared = pair[0, 4 * LAYER : 5 * LAYER] + pair[1, 0:LAYER]

    @pl.when(core == 0)
    def _():
        left, mine, right = cross.at[0], pair.at[0], pair.at[1]
        layers = [(left, LAYER * x) for x in range(4)] + [(edges.at[0], 0)]
        layers += [(mine, LAYER * x) for x in (1, 2, 3, 4)] + [(right, LAYER * x) for x in (1, 2, 3)]
        fill(layers + [(edges.at[1], 0)], (left, mine, right))
        for comp in range(3):
            node[comp, 8] = shared[17 * comp : 17 * comp + 17]

    @pl.when(core == 1)
    def _():
        left, mine, right = pair.at[0], pair.at[1], cross.at[1]
        layers = [(edges.at[0], 0)] + [(left, LAYER * x) for x in (1, 2, 3, 4)]
        layers += [(mine, LAYER * x) for x in (1, 2, 3)] + [(edges.at[1], 0)]
        fill(layers + [(right, LAYER * x) for x in (1, 2, 3, 4)], (left, mine, right))
        for comp in range(3):
            node[comp, 4] = shared[17 * comp : 17 * comp + 17]

    def apply(source, target, comp, zones, start, rows):
        even = even_lanes(rows)
        first = start // 2
        for zone in zones:
            near = [mass[zone, p, first : first + rows, :] for p in range(9)]
            far = [mass[zone, 9 + p, first : first + rows, :] for p in range(9)]
            spots = [
                [(comp, 2 * zone + i, pl.ds(start + j, rows, stride=2), slice(None)) for j in range(3)]
                for i in range(3)
            ]
            out = mass_nodes([[source[spots[i][j]] for j in range(3)] for i in range(3)], near, far, even)
            for i in range(3):
                for j in range(3):
                    target[spots[i][j]] = target[spots[i][j]] + out[i][j]

    partial[...] = jnp.zeros_like(partial)
    lane = lax.broadcasted_iota(jnp.int32, (1, 128), 1)
    sums = [None] * 9

    def add(at, left, right):
        term = left * right
        term = jnp.sum(term, 0, keepdims=True)
        sums[at] = term if sums[at] is None else sums[at] + term

    for comp in range(3):
        image[comp] = jnp.zeros(image.shape[1:], jnp.float32)
        apply(node, image, comp, range(6), 0, 8)
        for x in range(2, 11):
            second[comp, x] = (1.0 / HALF_WIDTH) * image[comp, x] - (CENTER / HALF_WIDTH) * node[comp, x]
        image[comp] = jnp.zeros(image.shape[1:], jnp.float32)
        apply(second, image, comp, range(1, 5), 2, 6)
        for x in range(4, 9):
            t0[comp, x - 4] = node[comp, x, 4:13, :]
            t1[comp, x - 4] = second[comp, x, 4:13, :]
            t2[comp, x - 4] = (
                (2.0 / HALF_WIDTH) * image[comp, x, 4:13, :]
                - (2.0 * CENTER / HALF_WIDTH) * second[comp, x, 4:13, :]
                - node[comp, x, 4:13, :]
            )
        near = [jnp.concatenate([mass[2, p, 2:6, :], mass[3, p, 2:6, :]], 0) for p in range(9)]
        far = [jnp.concatenate([mass[2, 9 + p, 2:6, :], mass[3, 9 + p, 2:6, :]], 0) for p in range(9)]
        nodes = corners(t2, comp, (0, 1), 4)
        scatter(partial, comp, (0, 1), 4, mass_nodes(nodes, near, far, even_lanes(8)))
        for x in range(5):
            fields = [ref[comp, x] for ref in (t0, t1, t2)]
            last = partial[comp, x]
            for i in range(3):
                add(6 + i, fields[i], last)
            if x < 4:
                owned = [v[0:8] for v in fields]
                for at, (i, j) in enumerate(((0, 0), (0, 1), (0, 2), (1, 1), (1, 2), (2, 2))):
                    add(at, owned[i], owned[j])
    value = [jnp.sum(v, 1, keepdims=True) for v in sums]
    gram = {(0, 0): value[0], (0, 1): value[1], (0, 2): value[2], (1, 1): value[3], (1, 2): value[4], (2, 2): value[5]}
    for i in range(3):
        gram[(i, 3)] = (
            (2.0 / HALF_WIDTH) * value[6 + i]
            - (2.0 * CENTER / HALF_WIDTH) * gram[(i, 2)]
            - gram[(min(i, 1), max(i, 1))]
        )
    row = jnp.zeros((1, 128), jnp.float32)
    for at, spot in enumerate(PAIRS):
        row = jnp.where(lane == at, gram[spot], row)
    products[...] = jnp.broadcast_to(row[None, :, :16], products.shape)

    def edge(ref, x):
        ref[27:32] = jnp.zeros((5, 128), jnp.float32)
        for comp in range(3):
            ref[9 * comp : 9 * comp + 9] = partial[comp, x]

    @pl.when(core == 0)
    def _():
        edge(inner, 4)
        edge(outer, 0)

    @pl.when(core == 1)
    def _():
        edge(inner, 0)
        edge(outer, 4)


def finish_kernel(gathered, image, t0, t1, t2, accel, residual):
    row = gathered[0, 15:16, :]
    for peer in range(1, gathered.shape[0]):
        row = row + gathered[peer, 15:16, :]
    gram = {pair: row[:, at : at + 1] for at, pair in enumerate(PAIRS)}
    accel_of, residual_of = cg_coefficients(gram)
    subs = gathered.shape[0]
    at_sub = lax.axis_index("sub")
    low, high = gathered.at[lax.rem(at_sub + subs - 1, subs)], gathered.at[lax.rem(at_sub + 1, subs)]
    for comp in range(3):
        for x in range(5):
            spot = 5 * comp + x
            last = image[comp, x]
            at = lax.broadcasted_iota(jnp.int32, last.shape, 0)
            last = last + jnp.where(at == 0, low[spot : spot + 1, :], 0.0)
            last = last + jnp.where(at == 8, high[spot : spot + 1, :], 0.0)
            parts = [t0[comp, x], t1[comp, x], t2[comp, x]]
            parts.append((2.0 / HALF_WIDTH) * last - (2.0 * CENTER / HALF_WIDTH) * parts[2] - parts[1])
            accel[x, :, comp, :] = accel_of[0] * parts[0] + accel_of[1] * parts[1] + accel_of[2] * parts[2]
            residual[x, :, comp, :] = (
                residual_of[0] * parts[0]
                + residual_of[1] * parts[1]
                + residual_of[2] * parts[2]
                + residual_of[3] * parts[3]
            )


CENTER = 0.196
HALF_WIDTH = 0.194
PAIRS = ((0, 0), (0, 1), (0, 2), (0, 3), (1, 1), (1, 2), (1, 3), (2, 2), (2, 3))


def dot_in(gram, left, right):
    value = 0.0
    for i in range(4):
        for j in range(4):
            if left[i] is None or right[j] is None or (i == 3 and j == 3):
                continue
            value = value + gram[(min(i, j), max(i, j))] * left[i] * right[j]
    return value


def axpy(scale, left, right):
    out = []
    for a, b in zip(left, right):
        if a is None:
            out.append(b)
        elif b is None:
            out.append(scale * a)
        else:
            out.append(scale * a + b)
    return out


def mapped_coefficients(p):
    p0, p1, p2 = (0.0 if v is None else v for v in p[:3])
    shifted = [0.5 * p1, p0 + 0.5 * p2, 0.5 * p1, 0.5 * p2]
    return [HALF_WIDTH * b + CENTER * a for a, b in zip((p0, p1, p2, 0.0), shifted)]


def cg_coefficients(gram):
    accel = [0.0, 0.0, 0.0, 0.0]
    residual = [1.0, 0.0, 0.0, 0.0]
    direction = residual
    norm_now = gram[(0, 0)]
    for sweep_at in range(CG_ITERS):
        mapped = mapped_coefficients(direction)
        step = norm_now / dot_in(gram, direction, mapped)
        accel = axpy(step, direction, accel)
        residual = axpy(-step, mapped, residual)
        if sweep_at + 1 < CG_ITERS:
            norm_next = dot_in(gram, residual, residual)
            direction = axpy(norm_next / norm_now, direction, residual)
            norm_now = norm_next
    return accel, residual


def local_call(kernel, name, outs, scratch, *operands, fetch=False):
    landing = [pltpu.VMEM(x.shape, x.dtype) for x in operands] + [pltpu.SemaphoreType.DMA((len(operands),))]
    return pl.pallas_call(
        kernel,
        out_shape=[jax.ShapeDtypeStruct(shape, jnp.float32) for shape in outs],
        in_specs=[pl.BlockSpec(memory_space=pltpu.HBM if fetch else pltpu.VMEM) for _ in operands],
        out_specs=[pl.BlockSpec(memory_space=pltpu.VMEM) for _ in outs],
        scratch_shapes=[pltpu.VMEM(shape, jnp.float32) for shape in scratch] + (landing if fetch else []),
        compiler_params=pltpu.CompilerParams(vmem_limit_bytes=(60 * 1024 if fetch else 12288) * 1024),
        name=name,
    )(*operands)


def pair_gather(block, axes, offset):
    return lax.all_gather(block, axes, axis_index_groups=pair_groups(axes, offset))


def pair_swap(block, axes, offset):
    groups = pair_groups(axes, offset)
    return lax.ppermute(block, axes, [edge for a, b in groups for edge in ((a, b), (b, a))])


def per_device(
    velocity, displacement, energy, rho_weight, mass_share, energy_share, material_id, mix_mask
):
    field = velocity.shape
    turned = (field[1], field[2], field[0], field[3])
    subs = lax.axis_size("sub")
    above = (lax.axis_index("sub") + 1) % subs
    core = lax.axis_index("dom_2")
    halo = (152, 128)
    partial, energy_rate, planes, inner, outer = local_call(
        force_kernel,
        "force",
        (field, energy.shape, (18, 8, 128), halo, halo),
        ((2, 2, 9, 9, 8, 128), (2, 9, 8, 128), (2,) + field),
        jnp.transpose(displacement, (1, 2, 0, 3)),
        jnp.transpose(velocity, (1, 2, 0, 3)),
        energy, rho_weight, mass_share, energy_share, material_id, mix_mask,
        fetch=True,
    )
    inner = pair_swap(inner, ("sub",), 0)
    outer = pair_swap(outer, ("sub",), 1)
    (wide,) = local_call(
        widen_kernel, "widen", ((BLOCK, 128),), (), inner, outer, partial, planes
    )
    pair = pair_gather(wide, DOM, 0)
    shared = pair[0, 4 * LAYER : 5 * LAYER] + pair[1, 0:LAYER]
    closed = lax.dynamic_update_slice(wide, shared, (4 * LAYER * (1 - core), 0))
    cross = pair_gather(closed, DOM, 1)
    edges = pair_gather(cross[0, 4 * LAYER : 5 * LAYER] + cross[1, :LAYER], DOM, 0)
    extended = (3, 13, 17, 128)
    count = lax.axis_size(DOM)
    t0, t1, t2, partial, inner, outer, spread = local_call(
        krylov_kernel,
        "krylov",
        (field, field, field, field, (32, 128), (32, 128), (count, 1, 16)),
        (extended, extended, extended, (6, 18, 8, 128)),
        pair, cross, edges,
    )
    inner = pair_gather(inner, DOM, 0)
    outer = pair_gather(outer, DOM, 1)
    inner = (inner[0] + inner[1])[:27].reshape(3, 1, 9, 128)
    outer = (outer[0] + outer[1])[:27].reshape(3, 1, 9, 128)
    low_x, high_x = jnp.where(core == 0, outer, inner), jnp.where(core == 0, inner, outer)
    image = jnp.concatenate([low_x, partial[:, 1:4], high_x], 1)
    row = jnp.sum(lax.all_to_all(spread, DOM, 0, 0, tiled=True), 0)
    row = jnp.pad(row, ((0, 0), (0, 112)))
    low = jnp.concatenate([image[:, :, 0].reshape(15, 128), row], 0)
    high = jnp.concatenate([image[:, :, 8].reshape(15, 128), row], 0)
    peer = jnp.arange(subs, dtype=jnp.int32)[:, None, None]
    gathered = lax.all_to_all(jnp.where(peer == above, high, low), "sub", 0, 0, tiled=True)
    accel, residual = local_call(
        finish_kernel, "finish", (turned, turned), (), gathered, image, t0, t1, t2
    )
    return (jnp.transpose(accel, (2, 0, 1, 3)), jnp.transpose(residual, (2, 0, 1, 3)), energy_rate)


def solution(mesh):
    torus = Mesh(
        mesh.devices.reshape((8, 4, 2, mesh.shape["sub"]) if mesh.shape["dom"] == 64 else (1, 1, 2, mesh.shape["sub"])), ("dom_0", "dom_1", "dom_2", "sub")
    )
    return jax.shard_map(
        per_device,
        mesh=torus,
        in_specs=(
            P(None, DOM, "sub", None),
            P(None, DOM, "sub", None),
            P(None, DOM, "sub", None),
            P(None, DOM, "sub", None),
            P(None, DOM, "sub", None),
            P(None, DOM, "sub", None),
            P(DOM, "sub", None),
            P(None, DOM, "sub", None),
        ),
        out_specs=(P(None, DOM, "sub", None), P(None, DOM, "sub", None), P(None, DOM, "sub", None)),
        check_vma=False,
    )
```

```python
import functools
import math

import jax
import jax.numpy as jnp
from jax import lax
from jax.experimental import pallas as pl
from jax.experimental.pallas import tpu as pltpu
from jax.sharding import Mesh
from jax.sharding import PartitionSpec as P

MATS = 4
EQ_ITERS = 4
CG_ITERS = 3
DOM_SUB = ("dom_0", "dom_1", "dom_2", "sub")
DOM = ("dom_0", "dom_1", "dom_2")


gammas = (1.4, 1.67, 2.0, 3.0)
cold_terms = (0.3, 1.2, 0.6, 2.4)
highest = lax.Precision.HIGHEST


def pair_groups(axes, offset):
    count = 1
    for axis in axes:
        count *= lax.axis_size(axis)
    return [[(i + offset) % count, (i + offset + 1) % count] for i in range(0, count, 2)]


ROOT = math.sqrt(0.15)
POINTS = (0.5 - ROOT, 0.5, 0.5 + ROOT)
QUAD = (5.0 / 18.0, 8.0 / 18.0, 5.0 / 18.0)
VALUE = tuple((2.0 * (t - 0.5) * (t - 1.0), -4.0 * t * (t - 1.0), 2.0 * t * (t - 0.5)) for t in POINTS)
SLOPE = tuple((4.0 * t - 3.0, 4.0 - 8.0 * t, 4.0 * t - 1.0) for t in POINTS)
LINEAR = tuple((1.0 - t, t) for t in POINTS)


def value_of(nodes):
    first, middle, last = nodes
    a, b, c = VALUE[0]
    scaled = b * middle
    return (a * first + scaled + c * last, middle, c * first + scaled + a * last)


def value_back(points):
    first, middle, last = points
    a, b, c = VALUE[0]
    return (a * first + c * last, b * (first + last) + middle, c * first + a * last)


def slope_of(nodes):
    first, middle, last = nodes
    a, b, c = SLOPE[0]
    scaled = b * middle
    return (a * first + scaled + c * last, last - first, -c * first - scaled - a * last)


def slope_back(points):
    first, middle, last = points
    a, b, c = SLOPE[0]
    return (a * first - middle - c * last, b * (first - last), c * first + middle - a * last)


def turn(array, shift):
    return pltpu.roll(array, shift % array.shape[-1], array.ndim - 1)


def even_lanes(rows):
    return lax.broadcasted_iota(jnp.int32, (rows, 128), 1) % 2 == 0


def depth_value(nodes, even, one, two):
    a, b, c = VALUE[0]
    scaled = b * one
    return jnp.where(even, a * nodes + scaled + c * two, nodes), c * nodes + scaled + a * two


def depth_value_back(near, far, even):
    a, b, c = VALUE[0]
    near_even = jnp.where(even, near, 0.0)
    ahead = turn(b * (near_even + far), 1) + turn(c * near_even + a * far, 2)
    return jnp.where(even, a * near + c * far, near) + ahead


def corners(ref, c, packs, rows):
    out = []
    for i in range(3):
        line = []
        for j in range(3):
            parts = [ref[c, 2 * zone + i, pl.ds(j, rows, stride=2), :] for zone in packs]
            line.append(parts[0] if len(parts) == 1 else jnp.concatenate(parts, 0))
        out.append(line)
    return out


def scatter(ref, c, packs, rows, nodes):
    for i in range(3):
        for j in range(3):
            for at, zone in enumerate(packs):
                part = nodes[i][j][at * rows : (at + 1) * rows]
                spot = (c, 2 * zone + i, pl.ds(j, rows, stride=2), slice(None))
                ref[spot] = ref[spot] + part


def mass_nodes(nodes, near_mass, far_mass, even):
    near = [[None] * 3 for _ in range(3)]
    far = [[None] * 3 for _ in range(3)]
    for i in range(3):
        for j in range(3):
            u = nodes[i][j]
            near[i][j], far[i][j] = depth_value(u, even, turn(u, -1), turn(u, -2))
    sides = []
    for field, mass in ((near, near_mass), (far, far_mass)):
        field = [value_of(line) for line in field]
        field = [value_of([field[i][j] for i in range(3)]) for j in range(3)]
        field = [[field[j][i] * mass[3 * i + j] for j in range(3)] for i in range(3)]
        field = [value_back(line) for line in field]
        field = [value_back([field[i][j] for i in range(3)]) for j in range(3)]
        sides.append(field)
    return [[depth_value_back(sides[0][j][i], sides[1][j][i], even) for j in range(3)] for i in range(3)]


def spread_tables():
    zone = lax.broadcasted_iota(jnp.int32, (64, 128), 0)
    lane = lax.broadcasted_iota(jnp.int32, (64, 128), 1)
    one, zero = jnp.float32(1.0), jnp.float32(0.0)
    even = jnp.where(lane == 2 * zone, one, zero)
    odd = jnp.where(lane == 2 * zone + 1, one, zero)
    return even, odd


def collect_tables(which):
    lane = lax.broadcasted_iota(jnp.int32, (128, 64), 0)
    zone = lax.broadcasted_iota(jnp.int32, (128, 64), 1)
    even, odd = lane == 2 * zone, lane == 2 * zone + 1
    near = jnp.where(even, LINEAR[0][which], jnp.where(odd, LINEAR[1][which], 0.0))
    far = jnp.where(even, LINEAR[2][which], 0.0)
    return near.astype(jnp.float32), far.astype(jnp.float32)


def dot32(left, right):
    return jnp.dot(left, right, precision=highest, preferred_element_type=jnp.float32)


def force_kernel(*refs):
    sources, (own, rate, inner, outer) = refs[:8], refs[8:12]
    grad, work, node, force, near_out, far_out, sems = refs[12:18] + refs[26:]
    disp, vel, energy, rho, share, portion, ident, mix = refs[18:26]
    copies = [pltpu.make_async_copy(a, b, sems.at[k]) for k, (a, b) in enumerate(zip(sources, refs[18:26]))]
    for copy in copies:
        copy.start()
    for copy in copies[2:]:
        copy.wait()
    packs, rows = (0, 1), energy.shape[2]
    count = 2 * rows
    even = even_lanes(count)

    def packed(ref, at):
        return jnp.concatenate([ref[at, 0], ref[at, 1]], 0)

    even_table, odd_table = spread_tables()
    both_table = even_table + odd_table
    material = jnp.concatenate([ident[0], ident[1]], 0)
    present = [
        jnp.where((packed(mix, m) == 1) | (material == m), 1.0, 0.0).astype(jnp.float32) for m in range(MATS)
    ]
    weighted = [present[m] * packed(share, m) for m in range(MATS)]
    weight_sum = weighted[0] + weighted[1] + weighted[2] + weighted[3]
    present_sum = present[0] + present[1] + present[2] + present[3]
    zone_rows = [
        (gammas[m] - 1.0) * (weighted[m] / weight_sum * packed(portion, m)) for m in range(MATS)
    ]
    zone_rows += [present[m] / present_sum for m in range(MATS)]
    zone_rows += [packed(energy, j) for j in range(8)]
    wide = dot32(jnp.concatenate(zone_rows, 0), both_table)
    wide = [wide[count * k : count * (k + 1)] for k in range(16)]
    loads, start, corner_energy = wide[:4], wide[4:8], wide[8:]
    rho_rows = [jnp.concatenate([packed(rho, 3 * p + k) for p in range(9)], 0) for k in range(3)]
    near_rho = dot32(rho_rows[0], even_table) + dot32(rho_rows[1], odd_table)
    far_rho = dot32(rho_rows[2], even_table)
    near_rho = [near_rho[count * p : count * (p + 1)] for p in range(9)]
    far_rho = [far_rho[count * p : count * (p + 1)] for p in range(9)]
    near_weight = jnp.where(even, QUAD[0], QUAD[1])
    far_weight = jnp.where(even, QUAD[2], 0.0)
    near_point = jnp.where(even, POINTS[0], POINTS[1])
    a, b, c = SLOPE[0]

    copies[0].wait()
    copies[1].wait()
    for field, ref in enumerate((disp, vel)):
        for x in range(5):
            for y in range(9):
                for comp in range(3):
                    node[field, comp, x, y : y + 1, :] = ref[x, y, comp : comp + 1, :]
    for field in range(2):
        for comp in range(3):
            nodes = corners(node.at[field], comp, packs, rows)
            values = [[None] * 3 for _ in range(3)], [[None] * 3 for _ in range(3)]
            slopes = [[None] * 3 for _ in range(3)], [[None] * 3 for _ in range(3)]
            for i in range(3):
                for j in range(3):
                    u = nodes[i][j]
                    one, two = turn(u, -1), turn(u, -2)
                    near, far = depth_value(u, even, one, two)
                    values[0][i][j], values[1][i][j] = near, jnp.where(even, far, 0.0)
                    scaled = b * one
                    slopes[0][i][j] = jnp.where(even, a * u + scaled + c * two, one - turn(u, 1))
                    slopes[1][i][j] = jnp.where(even, -c * u - scaled - a * two, 0.0)
            for side in range(2):
                plain = [value_of(line) for line in values[side]]
                sloped = [slope_of(line) for line in values[side]]
                deep = [value_of(line) for line in slopes[side]]
                for j in range(3):
                    along = (
                        slope_of([plain[i][j] for i in range(3)]),
                        value_of([sloped[i][j] for i in range(3)]),
                        value_of([deep[i][j] for i in range(3)]),
                    )
                    for d in range(3):
                        for i in range(3):
                            grad[field, side, 3 * i + j, 3 * comp + d] = along[d][i]

    for i in range(3):
        for j in range(3):
            spot = 3 * i + j
            plane = QUAD[i] * QUAD[j]
            mixed = []
            for k in range(2):
                low = LINEAR[j][0] * corner_energy[k] + LINEAR[j][1] * corner_energy[2 + k]
                high = LINEAR[j][0] * corner_energy[4 + k] + LINEAR[j][1] * corner_energy[6 + k]
                mixed.append(LINEAR[i][0] * low + LINEAR[i][1] * high)
            rise = mixed[1] - mixed[0]
            for side in range(2):
                weight = plane * (near_weight if side == 0 else far_weight)
                density_weight = near_rho[spot] if side == 0 else far_rho[spot]
                point = near_point if side == 0 else POINTS[2]
                jac = [[grad[0, side, spot, 3 * cc + d] + (1.0 if cc == d else 0.0) for d in range(3)] for cc in range(3)]
                adj = [
                    [
                        jac[(line + 1) % 3][(col + 1) % 3] * jac[(line + 2) % 3][(col + 2) % 3]
                        - jac[(line + 1) % 3][(col + 2) % 3] * jac[(line + 2) % 3][(col + 1) % 3]
                        for line in range(3)
                    ]
                    for col in range(3)
                ]
                determinant = jac[0][0] * adj[0][0] + jac[0][1] * adj[1][0] + jac[0][2] * adj[2][0]
                scale = density_weight / determinant * (mixed[0] + point * rise)
                load = [loads[m] * scale for m in range(MATS)]
                fraction = list(start)
                for _ in range(EQ_ITERS):
                    grown = [
                        jnp.sqrt(fraction[m] * (load[m] + cold_terms[m] * fraction[m])) for m in range(MATS)
                    ]
                    inverse = 1.0 / (grown[0] + grown[1] + grown[2] + grown[3])
                    fraction = [grown[m] * inverse for m in range(MATS)]
                terms = [load[m] + cold_terms[m] * fraction[m] for m in range(MATS)]
                stress = weight * (terms[0] + terms[1] + terms[2] + terms[3])
                divergence = 0.0
                for cc in range(3):
                    for d in range(3):
                        divergence = divergence + grad[1, side, spot, 3 * cc + d] * adj[d][cc]
                work[side, spot] = stress * divergence
                for cc in range(3):
                    for d in range(3):
                        grad[0, side, spot, 3 * cc + d] = stress * adj[d][cc]
                (near_out if side == 0 else far_out)[spot] = weight * density_weight

    force[...] = jnp.zeros_like(force)
    for comp in range(3):
        plain = [[None] * 3 for _ in range(3)], [[None] * 3 for _ in range(3)]
        deep = [[None] * 3 for _ in range(3)], [[None] * 3 for _ in range(3)]
        for side in range(2):
            lines = []
            for j in range(3):
                part = [[grad[0, side, 3 * i + j, 3 * comp + d] for i in range(3)] for d in range(3)]
                lines.append((slope_back(part[0]), value_back(part[1]), value_back(part[2])))
            for i in range(3):
                first = value_back([lines[j][0][i] for j in range(3)])
                second = slope_back([lines[j][1][i] for j in range(3)])
                third = value_back([lines[j][2][i] for j in range(3)])
                for j in range(3):
                    plain[side][i][j] = first[j] + second[j]
                    deep[side][i][j] = third[j]
        out = [[None] * 3 for _ in range(3)]
        va, vb, vc = VALUE[0]
        for i in range(3):
            for j in range(3):
                near, far = plain[0][i][j], plain[1][i][j]
                near_s, far_s = deep[0][i][j], deep[1][i][j]
                near_even = jnp.where(even, near, 0.0)
                near_s_even = jnp.where(even, near_s, 0.0)
                here = jnp.where(even, va * near + vc * far + a * near_s - c * far_s, near)
                next_one = jnp.where(even, vb * (near + far) + b * (near_s - far_s), near_s)
                next_two = vc * near_even + va * far + c * near_s_even - a * far_s
                behind = jnp.where(even, 0.0, near_s)
                out[i][j] = here + turn(next_one, 1) + turn(next_two, 2) - turn(behind, -1)
        scatter(force, comp, packs, rows, out)

    def collected(read):
        lines = [[], []]
        for side in range(2):
            for jx in range(2):
                for jy in range(2):
                    value = None
                    for i in range(3):
                        inner = None
                        for j in range(3):
                            term = LINEAR[j][jy] * read(side, 3 * i + j)
                            inner = term if inner is None else inner + term
                        inner = LINEAR[i][jx] * inner
                        value = inner if value is None else value + inner
                    lines[side].append(value)
        near, far = jnp.concatenate(lines[0], 0), jnp.concatenate(lines[1], 0)
        out = []
        for jz in range(2):
            near_table, far_table = collect_tables(jz)
            out.append(dot32(near, near_table) + dot32(far, far_table))
        return out

    done = collected(lambda side, spot: work[side, spot])
    lumped = collected(lambda side, spot: (near_out if side == 0 else far_out)[spot])
    for jz in range(2):
        ratio = -done[jz] / lumped[jz]
        for jxy in range(4):
            for zone in range(2):
                base = count * jxy + rows * zone
                rate[2 * jxy + jz, zone] = ratio[base : base + rows]

    for p in range(9):
        own[8 * p : 8 * p + 8] = near_out[p]
    for k in range(5):
        paired = far_out[2 * k] if k == 4 else far_out[2 * k] + turn(far_out[2 * k + 1], 1)
        own[8 * (9 + k) : 8 * (10 + k)] = paired
    own[247:248] = jnp.zeros((1, 128), jnp.float32)
    for comp in range(3):
        for x in range(5):
            own[112 + 9 * (5 * comp + x) : 121 + 9 * (5 * comp + x)] = force[comp, x]

    def pack(ref, high):
        nodes_at, zones_at = (4, 2) if high else (0, 0)
        ref[75:80] = jnp.zeros((5, 128), jnp.float32)
        for x in range(5):
            for comp in range(3):
                spot = 5 * (3 * x + comp)
                ref[spot : spot + 5] = force[comp, x, nodes_at : nodes_at + 5, :]
        for zone in range(2):
            for p in range(14):
                spot = 80 + 2 * (14 * zone + p)
                base = 8 * p + rows * zone + zones_at
                ref[spot : spot + 2] = own[base : base + 2]

    odd_sub = lax.rem(lax.axis_index("sub"), 2)

    @pl.when(odd_sub == 0)
    def _():
        pack(inner, True)
        pack(outer, False)

    @pl.when(odd_sub == 1)
    def _():
        pack(inner, False)
        pack(outer, True)


LAYER = 56
MASS_AT = 5 * LAYER
BLOCK = MASS_AT + 8 * 28


def widen_kernel(inner, outer, own, wide):
    def fill(lower, upper):
        for x in range(5):
            for comp in range(3):
                base, spot, at = LAYER * x + 17 * comp, 5 * (3 * x + comp), 112 + 9 * (5 * comp + x)
                wide[base : base + 4] = lower[spot : spot + 4]
                wide[base + 4 : base + 5] = lower[spot + 4 : spot + 5] + own[at : at + 1]
                wide[base + 5 : base + 12] = own[at + 1 : at + 8]
                wide[base + 12 : base + 13] = own[at + 8 : at + 9] + upper[spot : spot + 1]
                wide[base + 13 : base + 17] = upper[spot + 1 : spot + 5]
            wide[LAYER * x + 51 : LAYER * (x + 1)] = jnp.zeros((5, 128), jnp.float32)
        for zone in range(2):
            for p in range(14):
                base, spot = MASS_AT + 8 * (14 * zone + p), 80 + 2 * (14 * zone + p)
                wide[base : base + 2] = lower[spot : spot + 2]
                wide[base + 2 : base + 6] = own[8 * p + 4 * zone : 8 * p + 4 * zone + 4]
                wide[base + 6 : base + 8] = upper[spot : spot + 2]

    odd_sub = lax.rem(lax.axis_index("sub"), 2)

    @pl.when(odd_sub == 0)
    def _():
        fill(outer, inner)

    @pl.when(odd_sub == 1)
    def _():
        fill(inner, outer)


def krylov_kernel(pair, cross, edges, t0, t1, t2, partial, inner, outer, products, node, image, second, mass):
    core = lax.axis_index("dom_2")
    lanes = even_lanes(8)

    def fill(layers, blocks):
        for at, (ref, base) in enumerate(layers):
            for comp in range(3):
                spot = base + 17 * comp
                node[comp, at] = ref[spot : spot + 17]
        for at, ref in enumerate(blocks):
            for k in range(2):
                for p in range(14):
                    spot = MASS_AT + 8 * (14 * k + p)
                    plane = ref[spot : spot + 8]
                    if p < 9:
                        mass[2 * at + k, p] = plane
                    else:
                        mass[2 * at + k, 2 * p - 9] = jnp.where(lanes, plane, 0.0)
                        if p < 13:
                            mass[2 * at + k, 2 * p - 8] = jnp.where(lanes, turn(plane, -1), 0.0)

    shared = pair[0, 4 * LAYER : 5 * LAYER] + pair[1, 0:LAYER]

    @pl.when(core == 0)
    def _():
        left, mine, right = cross.at[0], pair.at[0], pair.at[1]
        layers = [(left, LAYER * x) for x in range(4)] + [(edges.at[0], 0)]
        layers += [(mine, LAYER * x) for x in (1, 2, 3, 4)] + [(right, LAYER * x) for x in (1, 2, 3)]
        fill(layers + [(edges.at[1], 0)], (left, mine, right))
        for comp in range(3):
            node[comp, 8] = shared[17 * comp : 17 * comp + 17]

    @pl.when(core == 1)
    def _():
        left, mine, right = pair.at[0], pair.at[1], cross.at[1]
        layers = [(edges.at[0], 0)] + [(left, LAYER * x) for x in (1, 2, 3, 4)]
        layers += [(mine, LAYER * x) for x in (1, 2, 3)] + [(edges.at[1], 0)]
        fill(layers + [(right, LAYER * x) for x in (1, 2, 3, 4)], (left, mine, right))
        for comp in range(3):
            node[comp, 4] = shared[17 * comp : 17 * comp + 17]

    def apply(source, target, comp, zones, start, rows):
        even = even_lanes(rows)
        first = start // 2
        for zone in zones:
            near = [mass[zone, p, first : first + rows, :] for p in range(9)]
            far = [mass[zone, 9 + p, first : first + rows, :] for p in range(9)]
            spots = [
                [(comp, 2 * zone + i, pl.ds(start + j, rows, stride=2), slice(None)) for j in range(3)]
                for i in range(3)
            ]
            out = mass_nodes([[source[spots[i][j]] for j in range(3)] for i in range(3)], near, far, even)
            for i in range(3):
                for j in range(3):
                    target[spots[i][j]] = target[spots[i][j]] + out[i][j]

    partial[...] = jnp.zeros_like(partial)
    lane = lax.broadcasted_iota(jnp.int32, (1, 128), 1)
    sums = [None] * 9

    def add(at, left, right):
        term = left * right
        term = jnp.sum(term, 0, keepdims=True)
        sums[at] = term if sums[at] is None else sums[at] + term

    for comp in range(3):
        image[comp] = jnp.zeros(image.shape[1:], jnp.float32)
        apply(node, image, comp, range(6), 0, 8)
        for x in range(2, 11):
            second[comp, x] = (1.0 / HALF_WIDTH) * image[comp, x] - (CENTER / HALF_WIDTH) * node[comp, x]
        image[comp] = jnp.zeros(image.shape[1:], jnp.float32)
        apply(second, image, comp, range(1, 5), 2, 6)
        for x in range(4, 9):
            t0[comp, x - 4] = node[comp, x, 4:13, :]
            t1[comp, x - 4] = second[comp, x, 4:13, :]
            t2[comp, x - 4] = (
                (2.0 / HALF_WIDTH) * image[comp, x, 4:13, :]
                - (2.0 * CENTER / HALF_WIDTH) * second[comp, x, 4:13, :]
                - node[comp, x, 4:13, :]
            )
        near = [jnp.concatenate([mass[2, p, 2:6, :], mass[3, p, 2:6, :]], 0) for p in range(9)]
        far = [jnp.concatenate([mass[2, 9 + p, 2:6, :], mass[3, 9 + p, 2:6, :]], 0) for p in range(9)]
        nodes = corners(t2, comp, (0, 1), 4)
        scatter(partial, comp, (0, 1), 4, mass_nodes(nodes, near, far, even_lanes(8)))
        for x in range(5):
            fields = [ref[comp, x] for ref in (t0, t1, t2)]
            last = partial[comp, x]
            for i in range(3):
                add(6 + i, fields[i], last)
            if x < 4:
                owned = [v[0:8] for v in fields]
                for at, (i, j) in enumerate(((0, 0), (0, 1), (0, 2), (1, 1), (1, 2), (2, 2))):
                    add(at, owned[i], owned[j])
    value = [jnp.sum(v, 1, keepdims=True) for v in sums]
    gram = {(0, 0): value[0], (0, 1): value[1], (0, 2): value[2], (1, 1): value[3], (1, 2): value[4], (2, 2): value[5]}
    for i in range(3):
        gram[(i, 3)] = (
            (2.0 / HALF_WIDTH) * value[6 + i]
            - (2.0 * CENTER / HALF_WIDTH) * gram[(i, 2)]
            - gram[(min(i, 1), max(i, 1))]
        )
    row = jnp.zeros((1, 128), jnp.float32)
    for at, spot in enumerate(PAIRS):
        row = jnp.where(lane == at, gram[spot], row)
    products[...] = jnp.broadcast_to(row[None, :, :16], products.shape)

    def edge(ref, x):
        ref[27:32] = jnp.zeros((5, 128), jnp.float32)
        for comp in range(3):
            ref[9 * comp : 9 * comp + 9] = partial[comp, x]

    @pl.when(core == 0)
    def _():
        edge(inner, 4)
        edge(outer, 0)

    @pl.when(core == 1)
    def _():
        edge(inner, 0)
        edge(outer, 4)


def finish_kernel(gathered, image, t0, t1, t2, accel, residual):
    row = gathered[0, 15:16, :]
    for peer in range(1, gathered.shape[0]):
        row = row + gathered[peer, 15:16, :]
    gram = {pair: row[:, at : at + 1] for at, pair in enumerate(PAIRS)}
    accel_of, residual_of = cg_coefficients(gram)
    subs = gathered.shape[0]
    at_sub = lax.axis_index("sub")
    low, high = gathered.at[lax.rem(at_sub + subs - 1, subs)], gathered.at[lax.rem(at_sub + 1, subs)]
    for comp in range(3):
        for x in range(5):
            spot = 5 * comp + x
            last = image[comp, x]
            at = lax.broadcasted_iota(jnp.int32, last.shape, 0)
            last = last + jnp.where(at == 0, low[spot : spot + 1, :], 0.0)
            last = last + jnp.where(at == 8, high[spot : spot + 1, :], 0.0)
            parts = [t0[comp, x], t1[comp, x], t2[comp, x]]
            parts.append((2.0 / HALF_WIDTH) * last - (2.0 * CENTER / HALF_WIDTH) * parts[2] - parts[1])
            accel[x, :, comp, :] = accel_of[0] * parts[0] + accel_of[1] * parts[1] + accel_of[2] * parts[2]
            residual[x, :, comp, :] = (
                residual_of[0] * parts[0]
                + residual_of[1] * parts[1]
                + residual_of[2] * parts[2]
                + residual_of[3] * parts[3]
            )


CENTER = 0.196
HALF_WIDTH = 0.194
PAIRS = ((0, 0), (0, 1), (0, 2), (0, 3), (1, 1), (1, 2), (1, 3), (2, 2), (2, 3))


def dot_in(gram, left, right):
    value = 0.0
    for i in range(4):
        for j in range(4):
            if left[i] is None or right[j] is None or (i == 3 and j == 3):
                continue
            value = value + gram[(min(i, j), max(i, j))] * left[i] * right[j]
    return value


def axpy(scale, left, right):
    out = []
    for a, b in zip(left, right):
        if a is None:
            out.append(b)
        elif b is None:
            out.append(scale * a)
        else:
            out.append(scale * a + b)
    return out


def mapped_coefficients(p):
    p0, p1, p2 = (0.0 if v is None else v for v in p[:3])
    shifted = [0.5 * p1, p0 + 0.5 * p2, 0.5 * p1, 0.5 * p2]
    return [HALF_WIDTH * b + CENTER * a for a, b in zip((p0, p1, p2, 0.0), shifted)]


def cg_coefficients(gram):
    accel = [0.0, 0.0, 0.0, 0.0]
    residual = [1.0, 0.0, 0.0, 0.0]
    direction = residual
    norm_now = gram[(0, 0)]
    for sweep_at in range(CG_ITERS):
        mapped = mapped_coefficients(direction)
        step = norm_now / dot_in(gram, direction, mapped)
        accel = axpy(step, direction, accel)
        residual = axpy(-step, mapped, residual)
        if sweep_at + 1 < CG_ITERS:
            norm_next = dot_in(gram, residual, residual)
            direction = axpy(norm_next / norm_now, direction, residual)
            norm_now = norm_next
    return accel, residual


def local_call(kernel, name, outs, scratch, *operands, fetch=False):
    landing = [pltpu.VMEM(x.shape, x.dtype) for x in operands] + [pltpu.SemaphoreType.DMA((len(operands),))]
    return pl.pallas_call(
        kernel,
        out_shape=[jax.ShapeDtypeStruct(shape, jnp.float32) for shape in outs],
        in_specs=[pl.BlockSpec(memory_space=pltpu.HBM if fetch else pltpu.VMEM) for _ in operands],
        out_specs=[pl.BlockSpec(memory_space=pltpu.VMEM) for _ in outs],
        scratch_shapes=[pltpu.VMEM(shape, jnp.float32) for shape in scratch] + (landing if fetch else []),
        compiler_params=pltpu.CompilerParams(vmem_limit_bytes=(60 * 1024 if fetch else 12288) * 1024),
        name=name,
    )(*operands)


def pair_gather(block, axes, offset):
    return lax.all_gather(block, axes, axis_index_groups=pair_groups(axes, offset))


def pair_swap(block, axes, offset):
    groups = pair_groups(axes, offset)
    return lax.ppermute(block, axes, [edge for a, b in groups for edge in ((a, b), (b, a))])


def per_device(
    velocity, displacement, energy, rho_weight, mass_share, energy_share, material_id, mix_mask
):
    field = velocity.shape
    turned = (field[1], field[2], field[0], field[3])
    subs = lax.axis_size("sub")
    above = (lax.axis_index("sub") + 1) % subs
    core = lax.axis_index("dom_2")
    halo = (136, 128)
    own, energy_rate, inner, outer = local_call(
        force_kernel,
        "force",
        ((248, 128), energy.shape, halo, halo),
        ((2, 2, 9, 9, 8, 128), (2, 9, 8, 128), (2,) + field, field, (9, 8, 128), (9, 8, 128)),
        jnp.transpose(displacement, (1, 2, 0, 3)),
        jnp.transpose(velocity, (1, 2, 0, 3)),
        energy, rho_weight, mass_share, energy_share, material_id, mix_mask,
        fetch=True,
    )
    inner = pair_swap(inner, ("sub",), 0)
    outer = pair_swap(outer, ("sub",), 1)
    (wide,) = local_call(
        widen_kernel, "widen", ((BLOCK, 128),), (), inner, outer, own
    )
    pair = pair_gather(wide, DOM, 0)
    shared = pair[0, 4 * LAYER : 5 * LAYER] + pair[1, 0:LAYER]
    closed = lax.dynamic_update_slice(wide, shared, (4 * LAYER * (1 - core), 0))
    cross = pair_gather(closed, DOM, 1)
    edges = pair_gather(cross[0, 4 * LAYER : 5 * LAYER] + cross[1, :LAYER], DOM, 0)
    extended = (3, 13, 17, 128)
    count = lax.axis_size(DOM)
    t0, t1, t2, partial, inner, outer, spread = local_call(
        krylov_kernel,
        "krylov",
        (field, field, field, field, (32, 128), (32, 128), (count, 1, 16)),
        (extended, extended, extended, (6, 18, 8, 128)),
        pair, cross, edges,
    )
    inner = pair_gather(inner, DOM, 0)
    outer = pair_gather(outer, DOM, 1)
    inner = (inner[0] + inner[1])[:27].reshape(3, 1, 9, 128)
    outer = (outer[0] + outer[1])[:27].reshape(3, 1, 9, 128)
    low_x, high_x = jnp.where(core == 0, outer, inner), jnp.where(core == 0, inner, outer)
    image = jnp.concatenate([low_x, partial[:, 1:4], high_x], 1)
    row = jnp.sum(lax.all_to_all(spread, DOM, 0, 0, tiled=True), 0)
    row = jnp.pad(row, ((0, 0), (0, 112)))
    low = jnp.concatenate([image[:, :, 0].reshape(15, 128), row], 0)
    high = jnp.concatenate([image[:, :, 8].reshape(15, 128), row], 0)
    peer = jnp.arange(subs, dtype=jnp.int32)[:, None, None]
    gathered = lax.all_to_all(jnp.where(peer == above, high, low), "sub", 0, 0, tiled=True)
    accel, residual = local_call(
        finish_kernel, "finish", (turned, turned), (), gathered, image, t0, t1, t2
    )
    return (jnp.transpose(accel, (2, 0, 1, 3)), jnp.transpose(residual, (2, 0, 1, 3)), energy_rate)


def solution(mesh):
    torus = Mesh(
        mesh.devices.reshape((8, 4, 2, mesh.shape["sub"]) if mesh.shape["dom"] == 64 else (1, 1, 2, mesh.shape["sub"])), ("dom_0", "dom_1", "dom_2", "sub")
    )
    return jax.shard_map(
        per_device,
        mesh=torus,
        in_specs=(
            P(None, DOM, "sub", None),
            P(None, DOM, "sub", None),
            P(None, DOM, "sub", None),
            P(None, DOM, "sub", None),
            P(None, DOM, "sub", None),
            P(None, DOM, "sub", None),
            P(DOM, "sub", None),
            P(None, DOM, "sub", None),
        ),
        out_specs=(P(None, DOM, "sub", None), P(None, DOM, "sub", None), P(None, DOM, "sub", None)),
        check_vma=False,
    )
```

```python
import functools
import math

import jax
import jax.numpy as jnp
from jax import lax
from jax.experimental import pallas as pl
from jax.experimental.pallas import tpu as pltpu
from jax.sharding import Mesh
from jax.sharding import PartitionSpec as P

MATS = 4
EQ_ITERS = 4
CG_ITERS = 3
DOM_SUB = ("dom_0", "dom_1", "dom_2", "sub")
DOM = ("dom_0", "dom_1", "dom_2")


gammas = (1.4, 1.67, 2.0, 3.0)
cold_terms = (0.3, 1.2, 0.6, 2.4)
highest = lax.Precision.HIGHEST


def pair_groups(axes, offset):
    count = 1
    for axis in axes:
        count *= lax.axis_size(axis)
    return [[(i + offset) % count, (i + offset + 1) % count] for i in range(0, count, 2)]


ROOT = math.sqrt(0.15)
POINTS = (0.5 - ROOT, 0.5, 0.5 + ROOT)
QUAD = (5.0 / 18.0, 8.0 / 18.0, 5.0 / 18.0)
VALUE = tuple((2.0 * (t - 0.5) * (t - 1.0), -4.0 * t * (t - 1.0), 2.0 * t * (t - 0.5)) for t in POINTS)
SLOPE = tuple((4.0 * t - 3.0, 4.0 - 8.0 * t, 4.0 * t - 1.0) for t in POINTS)
LINEAR = tuple((1.0 - t, t) for t in POINTS)


def value_of(nodes):
    first, middle, last = nodes
    a, b, c = VALUE[0]
    scaled = b * middle
    return (a * first + scaled + c * last, middle, c * first + scaled + a * last)


def value_back(points):
    first, middle, last = points
    a, b, c = VALUE[0]
    return (a * first + c * last, b * (first + last) + middle, c * first + a * last)


def slope_of(nodes):
    first, middle, last = nodes
    a, b, c = SLOPE[0]
    scaled = b * middle
    return (a * first + scaled + c * last, last - first, -c * first - scaled - a * last)


def slope_back(points):
    first, middle, last = points
    a, b, c = SLOPE[0]
    return (a * first - middle - c * last, b * (first - last), c * first + middle - a * last)


def turn(array, shift):
    return pltpu.roll(array, shift % array.shape[-1], array.ndim - 1)


def even_lanes(rows):
    return lax.broadcasted_iota(jnp.int32, (rows, 128), 1) % 2 == 0


def depth_value(nodes, even, one, two):
    a, b, c = VALUE[0]
    scaled = b * one
    return jnp.where(even, a * nodes + scaled + c * two, nodes), c * nodes + scaled + a * two


def depth_value_back(near, far, even):
    a, b, c = VALUE[0]
    near_even = jnp.where(even, near, 0.0)
    ahead = turn(b * (near_even + far), 1) + turn(c * near_even + a * far, 2)
    return jnp.where(even, a * near + c * far, near) + ahead


def corners(ref, c, packs, rows):
    out = []
    for i in range(3):
        line = []
        for j in range(3):
            parts = [ref[c, 2 * zone + i, pl.ds(j, rows, stride=2), :] for zone in packs]
            line.append(parts[0] if len(parts) == 1 else jnp.concatenate(parts, 0))
        out.append(line)
    return out


def scatter(ref, c, packs, rows, nodes):
    for i in range(3):
        for j in range(3):
            for at, zone in enumerate(packs):
                part = nodes[i][j][at * rows : (at + 1) * rows]
                spot = (c, 2 * zone + i, pl.ds(j, rows, stride=2), slice(None))
                ref[spot] = ref[spot] + part


def mass_nodes(nodes, near_mass, far_mass, even):
    near = [[None] * 3 for _ in range(3)]
    far = [[None] * 3 for _ in range(3)]
    for i in range(3):
        for j in range(3):
            u = nodes[i][j]
            near[i][j], far[i][j] = depth_value(u, even, turn(u, -1), turn(u, -2))
    sides = []
    for field, mass in ((near, near_mass), (far, far_mass)):
        field = [value_of(line) for line in field]
        field = [value_of([field[i][j] for i in range(3)]) for j in range(3)]
        field = [[field[j][i] * mass[3 * i + j] for j in range(3)] for i in range(3)]
        field = [value_back(line) for line in field]
        field = [value_back([field[i][j] for i in range(3)]) for j in range(3)]
        sides.append(field)
    return [[depth_value_back(sides[0][j][i], sides[1][j][i], even) for j in range(3)] for i in range(3)]


def spread_tables():
    zone = lax.broadcasted_iota(jnp.int32, (64, 128), 0)
    lane = lax.broadcasted_iota(jnp.int32, (64, 128), 1)
    one, zero = jnp.float32(1.0), jnp.float32(0.0)
    even = jnp.where(lane == 2 * zone, one, zero)
    odd = jnp.where(lane == 2 * zone + 1, one, zero)
    return even, odd


def collect_tables(which):
    lane = lax.broadcasted_iota(jnp.int32, (128, 64), 0)
    zone = lax.broadcasted_iota(jnp.int32, (128, 64), 1)
    even, odd = lane == 2 * zone, lane == 2 * zone + 1
    near = jnp.where(even, LINEAR[0][which], jnp.where(odd, LINEAR[1][which], 0.0))
    far = jnp.where(even, LINEAR[2][which], 0.0)
    return near.astype(jnp.float32), far.astype(jnp.float32)


def dot32(left, right):
    return jnp.dot(left, right, precision=highest, preferred_element_type=jnp.float32)


def force_kernel(*refs):
    sources, (own, rate, inner, outer) = refs[:8], refs[8:12]
    grad, work, node, force, near_out, far_out, sems = refs[12:18] + refs[26:]
    disp, vel, energy, rho, share, portion, ident, mix = refs[18:26]
    copies = [pltpu.make_async_copy(a, b, sems.at[k]) for k, (a, b) in enumerate(zip(sources, refs[18:26]))]
    for copy in copies:
        copy.start()
    for copy in copies[2:]:
        copy.wait()
    packs, rows = (0, 1), energy.shape[2]
    count = 2 * rows
    even = even_lanes(count)

    def packed(ref, at):
        return jnp.concatenate([ref[at, 0], ref[at, 1]], 0)

    even_table, odd_table = spread_tables()
    both_table = even_table + odd_table
    material = jnp.concatenate([ident[0], ident[1]], 0)
    present = [
        jnp.where((packed(mix, m) == 1) | (material == m), 1.0, 0.0).astype(jnp.float32) for m in range(MATS)
    ]
    weighted = [present[m] * packed(share, m) for m in range(MATS)]
    weight_sum = weighted[0] + weighted[1] + weighted[2] + weighted[3]
    present_sum = present[0] + present[1] + present[2] + present[3]
    zone_rows = [
        (gammas[m] - 1.0) * (weighted[m] / weight_sum * packed(portion, m)) for m in range(MATS)
    ]
    zone_rows += [present[m] / present_sum for m in range(MATS)]
    zone_rows += [packed(energy, j) for j in range(8)]
    wide = dot32(jnp.concatenate(zone_rows, 0), both_table)
    wide = [wide[count * k : count * (k + 1)] for k in range(16)]
    loads, start, corner_energy = wide[:4], wide[4:8], wide[8:]
    rho_rows = [jnp.concatenate([packed(rho, 3 * p + k) for p in range(9)], 0) for k in range(3)]
    near_rho = dot32(rho_rows[0], even_table) + dot32(rho_rows[1], odd_table)
    far_rho = dot32(rho_rows[2], even_table)
    near_rho = [near_rho[count * p : count * (p + 1)] for p in range(9)]
    far_rho = [far_rho[count * p : count * (p + 1)] for p in range(9)]
    near_weight = jnp.where(even, QUAD[0], QUAD[1])
    far_weight = jnp.where(even, QUAD[2], 0.0)
    near_point = jnp.where(even, POINTS[0], POINTS[1])
    a, b, c = SLOPE[0]

    copies[0].wait()
    copies[1].wait()
    for field, ref in enumerate((disp, vel)):
        for x in range(5):
            for y in range(9):
                for comp in range(3):
                    node[field, comp, x, y : y + 1, :] = ref[x, y, comp : comp + 1, :]
    for field in range(2):
        for comp in range(3):
            nodes = corners(node.at[field], comp, packs, rows)
            values = [[None] * 3 for _ in range(3)], [[None] * 3 for _ in range(3)]
            slopes = [[None] * 3 for _ in range(3)], [[None] * 3 for _ in range(3)]
            for i in range(3):
                for j in range(3):
                    u = nodes[i][j]
                    one, two = turn(u, -1), turn(u, -2)
                    near, far = depth_value(u, even, one, two)
                    values[0][i][j], values[1][i][j] = near, jnp.where(even, far, 0.0)
                    scaled = b * one
                    slopes[0][i][j] = jnp.where(even, a * u + scaled + c * two, one - turn(u, 1))
                    slopes[1][i][j] = jnp.where(even, -c * u - scaled - a * two, 0.0)
            for side in range(2):
                plain = [value_of(line) for line in values[side]]
                sloped = [slope_of(line) for line in values[side]]
                deep = [value_of(line) for line in slopes[side]]
                for j in range(3):
                    along = (
                        slope_of([plain[i][j] for i in range(3)]),
                        value_of([sloped[i][j] for i in range(3)]),
                        value_of([deep[i][j] for i in range(3)]),
                    )
                    for d in range(3):
                        for i in range(3):
                            grad[field, side, 3 * i + j, 3 * comp + d] = along[d][i]

    for i in range(3):
        for j in range(3):
            spot = 3 * i + j
            plane = QUAD[i] * QUAD[j]
            mixed = []
            for k in range(2):
                low = LINEAR[j][0] * corner_energy[k] + LINEAR[j][1] * corner_energy[2 + k]
                high = LINEAR[j][0] * corner_energy[4 + k] + LINEAR[j][1] * corner_energy[6 + k]
                mixed.append(LINEAR[i][0] * low + LINEAR[i][1] * high)
            rise = mixed[1] - mixed[0]
            for side in range(2):
                weight = plane * (near_weight if side == 0 else far_weight)
                density_weight = near_rho[spot] if side == 0 else far_rho[spot]
                point = near_point if side == 0 else POINTS[2]
                jac = [[grad[0, side, spot, 3 * cc + d] + (1.0 if cc == d else 0.0) for d in range(3)] for cc in range(3)]
                adj = [
                    [
                        jac[(line + 1) % 3][(col + 1) % 3] * jac[(line + 2) % 3][(col + 2) % 3]
                        - jac[(line + 1) % 3][(col + 2) % 3] * jac[(line + 2) % 3][(col + 1) % 3]
                        for line in range(3)
                    ]
                    for col in range(3)
                ]
                determinant = jac[0][0] * adj[0][0] + jac[0][1] * adj[1][0] + jac[0][2] * adj[2][0]
                scale = density_weight / determinant * (mixed[0] + point * rise)
                load = [loads[m] * scale for m in range(MATS)]
                fraction = list(start)
                for _ in range(EQ_ITERS):
                    grown = [
                        jnp.sqrt(fraction[m] * (load[m] + cold_terms[m] * fraction[m])) for m in range(MATS)
                    ]
                    inverse = 1.0 / (grown[0] + grown[1] + grown[2] + grown[3])
                    fraction = [grown[m] * inverse for m in range(MATS)]
                terms = [load[m] + cold_terms[m] * fraction[m] for m in range(MATS)]
                stress = weight * (terms[0] + terms[1] + terms[2] + terms[3])
                divergence = 0.0
                for cc in range(3):
                    for d in range(3):
                        divergence = divergence + grad[1, side, spot, 3 * cc + d] * adj[d][cc]
                work[side, spot] = stress * divergence
                for cc in range(3):
                    for d in range(3):
                        grad[0, side, spot, 3 * cc + d] = stress * adj[d][cc]
                (near_out if side == 0 else far_out)[spot] = weight * density_weight

    force[...] = jnp.zeros_like(force)
    for comp in range(3):
        plain = [[None] * 3 for _ in range(3)], [[None] * 3 for _ in range(3)]
        deep = [[None] * 3 for _ in range(3)], [[None] * 3 for _ in range(3)]
        for side in range(2):
            lines = []
            for j in range(3):
                part = [[grad[0, side, 3 * i + j, 3 * comp + d] for i in range(3)] for d in range(3)]
                lines.append((slope_back(part[0]), value_back(part[1]), value_back(part[2])))
            for i in range(3):
                first = value_back([lines[j][0][i] for j in range(3)])
                second = slope_back([lines[j][1][i] for j in range(3)])
                third = value_back([lines[j][2][i] for j in range(3)])
                for j in range(3):
                    plain[side][i][j] = first[j] + second[j]
                    deep[side][i][j] = third[j]
        out = [[None] * 3 for _ in range(3)]
        va, vb, vc = VALUE[0]
        for i in range(3):
            for j in range(3):
                near, far = plain[0][i][j], plain[1][i][j]
                near_s, far_s = deep[0][i][j], deep[1][i][j]
                near_even = jnp.where(even, near, 0.0)
                near_s_even = jnp.where(even, near_s, 0.0)
                here = jnp.where(even, va * near + vc * far + a * near_s - c * far_s, near)
                next_one = jnp.where(even, vb * (near + far) + b * (near_s - far_s), near_s)
                next_two = vc * near_even + va * far + c * near_s_even - a * far_s
                behind = jnp.where(even, 0.0, near_s)
                out[i][j] = here + turn(next_one, 1) + turn(next_two, 2) - turn(behind, -1)
        scatter(force, comp, packs, rows, out)

    def collected(read):
        lines = [[], []]
        for side in range(2):
            for jx in range(2):
                for jy in range(2):
                    value = None
                    for i in range(3):
                        inner = None
                        for j in range(3):
                            term = LINEAR[j][jy] * read(side, 3 * i + j)
                            inner = term if inner is None else inner + term
                        inner = LINEAR[i][jx] * inner
                        value = inner if value is None else value + inner
                    lines[side].append(value)
        near, far = jnp.concatenate(lines[0], 0), jnp.concatenate(lines[1], 0)
        out = []
        for jz in range(2):
            near_table, far_table = collect_tables(jz)
            out.append(dot32(near, near_table) + dot32(far, far_table))
        return out

    done = collected(lambda side, spot: work[side, spot])
    lumped = collected(lambda side, spot: (near_out if side == 0 else far_out)[spot])
    for jz in range(2):
        ratio = -done[jz] / lumped[jz]
        for jxy in range(4):
            for zone in range(2):
                base = count * jxy + rows * zone
                rate[2 * jxy + jz, zone] = ratio[base : base + rows]

    for p in range(9):
        own[8 * p : 8 * p + 8] = near_out[p]
    for k in range(5):
        paired = far_out[2 * k] if k == 4 else far_out[2 * k] + turn(far_out[2 * k + 1], 1)
        own[8 * (9 + k) : 8 * (10 + k)] = paired
    own[247:248] = jnp.zeros((1, 128), jnp.float32)
    for comp in range(3):
        for x in range(5):
            own[112 + 9 * (5 * comp + x) : 121 + 9 * (5 * comp + x)] = force[comp, x]

    def pack(ref, high):
        nodes_at, zones_at = (4, 2) if high else (0, 0)
        ref[75:80] = jnp.zeros((5, 128), jnp.float32)
        for x in range(5):
            for comp in range(3):
                spot = 5 * (3 * x + comp)
                ref[spot : spot + 5] = force[comp, x, nodes_at : nodes_at + 5, :]
        for zone in range(2):
            for p in range(14):
                spot = 80 + 2 * (14 * zone + p)
                base = 8 * p + rows * zone + zones_at
                ref[spot : spot + 2] = own[base : base + 2]

    odd_sub = lax.rem(lax.axis_index("sub"), 2)

    @pl.when(odd_sub == 0)
    def _():
        pack(inner, True)
        pack(outer, False)

    @pl.when(odd_sub == 1)
    def _():
        pack(inner, False)
        pack(outer, True)


LAYER = 56
MASS_AT = 5 * LAYER
BLOCK = MASS_AT + 8 * 28


def widen_kernel(inner, outer, own, wide):
    def fill(lower, upper):
        for x in range(5):
            for comp in range(3):
                base, spot, at = LAYER * x + 17 * comp, 5 * (3 * x + comp), 112 + 9 * (5 * comp + x)
                wide[base : base + 4] = lower[spot : spot + 4]
                wide[base + 4 : base + 5] = lower[spot + 4 : spot + 5] + own[at : at + 1]
                wide[base + 5 : base + 12] = own[at + 1 : at + 8]
                wide[base + 12 : base + 13] = own[at + 8 : at + 9] + upper[spot : spot + 1]
                wide[base + 13 : base + 17] = upper[spot + 1 : spot + 5]
            wide[LAYER * x + 51 : LAYER * (x + 1)] = jnp.zeros((5, 128), jnp.float32)
        for zone in range(2):
            for p in range(14):
                base, spot = MASS_AT + 8 * (14 * zone + p), 80 + 2 * (14 * zone + p)
                wide[base : base + 2] = lower[spot : spot + 2]
                wide[base + 2 : base + 6] = own[8 * p + 4 * zone : 8 * p + 4 * zone + 4]
                wide[base + 6 : base + 8] = upper[spot : spot + 2]

    odd_sub = lax.rem(lax.axis_index("sub"), 2)

    @pl.when(odd_sub == 0)
    def _():
        fill(outer, inner)

    @pl.when(odd_sub == 1)
    def _():
        fill(inner, outer)


def krylov_kernel(pair, cross, edges, t0, t1, t2, partial, inner, outer, products, node, image, second, mass):
    core = lax.axis_index("dom_2")
    lanes = even_lanes(8)

    def fill(layers, blocks):
        for at, (ref, base) in enumerate(layers):
            for comp in range(3):
                spot = base + 17 * comp
                node[comp, at] = ref[spot : spot + 17]
        for at, ref in enumerate(blocks):
            for k in range(2):
                for p in range(14):
                    spot = MASS_AT + 8 * (14 * k + p)
                    plane = ref[spot : spot + 8]
                    if p < 9:
                        mass[2 * at + k, p] = plane
                    else:
                        mass[2 * at + k, 2 * p - 9] = jnp.where(lanes, plane, 0.0)
                        if p < 13:
                            mass[2 * at + k, 2 * p - 8] = jnp.where(lanes, turn(plane, -1), 0.0)

    shared = pair[0, 4 * LAYER : 5 * LAYER] + pair[1, 0:LAYER]

    @pl.when(core == 0)
    def _():
        left, mine, right = cross.at[0], pair.at[0], pair.at[1]
        layers = [(left, LAYER * x) for x in range(4)] + [(edges.at[0], 0)]
        layers += [(mine, LAYER * x) for x in (1, 2, 3, 4)] + [(right, LAYER * x) for x in (1, 2, 3)]
        fill(layers + [(edges.at[1], 0)], (left, mine, right))
        for comp in range(3):
            node[comp, 8] = shared[17 * comp : 17 * comp + 17]

    @pl.when(core == 1)
    def _():
        left, mine, right = pair.at[0], pair.at[1], cross.at[1]
        layers = [(edges.at[0], 0)] + [(left, LAYER * x) for x in (1, 2, 3, 4)]
        layers += [(mine, LAYER * x) for x in (1, 2, 3)] + [(edges.at[1], 0)]
        fill(layers + [(right, LAYER * x) for x in (1, 2, 3, 4)], (left, mine, right))
        for comp in range(3):
            node[comp, 4] = shared[17 * comp : 17 * comp + 17]

    def apply(source, target, comp, zones, start, rows):
        even = even_lanes(rows)
        first = start // 2
        for zone in zones:
            near = [mass[zone, p, first : first + rows, :] for p in range(9)]
            far = [mass[zone, 9 + p, first : first + rows, :] for p in range(9)]
            spots = [
                [(comp, 2 * zone + i, pl.ds(start + j, rows, stride=2), slice(None)) for j in range(3)]
                for i in range(3)
            ]
            out = mass_nodes([[source[spots[i][j]] for j in range(3)] for i in range(3)], near, far, even)
            for i in range(3):
                for j in range(3):
                    target[spots[i][j]] = target[spots[i][j]] + out[i][j]

    partial[...] = jnp.zeros_like(partial)
    lane = lax.broadcasted_iota(jnp.int32, (1, 128), 1)
    sums = [None] * 9

    def add(at, left, right):
        term = left * right
        term = jnp.sum(term, 0, keepdims=True)
        sums[at] = term if sums[at] is None else sums[at] + term

    for comp in range(3):
        image[comp] = jnp.zeros(image.shape[1:], jnp.float32)
        apply(node, image, comp, range(6), 0, 8)
        for x in range(2, 11):
            second[comp, x] = (1.0 / HALF_WIDTH) * image[comp, x] - (CENTER / HALF_WIDTH) * node[comp, x]
        image[comp] = jnp.zeros(image.shape[1:], jnp.float32)
        apply(second, image, comp, range(1, 5), 2, 6)
        for x in range(4, 9):
            t0[comp, x - 4] = node[comp, x, 4:13, :]
            t1[comp, x - 4] = second[comp, x, 4:13, :]
            t2[comp, x - 4] = (
                (2.0 / HALF_WIDTH) * image[comp, x, 4:13, :]
                - (2.0 * CENTER / HALF_WIDTH) * second[comp, x, 4:13, :]
                - node[comp, x, 4:13, :]
            )
        near = [jnp.concatenate([mass[2, p, 2:6, :], mass[3, p, 2:6, :]], 0) for p in range(9)]
        far = [jnp.concatenate([mass[2, 9 + p, 2:6, :], mass[3, 9 + p, 2:6, :]], 0) for p in range(9)]
        nodes = corners(t2, comp, (0, 1), 4)
        scatter(partial, comp, (0, 1), 4, mass_nodes(nodes, near, far, even_lanes(8)))
        for x in range(5):
            fields = [ref[comp, x] for ref in (t0, t1, t2)]
            last = partial[comp, x]
            for i in range(3):
                add(6 + i, fields[i], last)
            if x < 4:
                owned = [v[0:8] for v in fields]
                for at, (i, j) in enumerate(((0, 0), (0, 1), (0, 2), (1, 1), (1, 2), (2, 2))):
                    add(at, owned[i], owned[j])
    value = [jnp.sum(v, 1, keepdims=True) for v in sums]
    gram = {(0, 0): value[0], (0, 1): value[1], (0, 2): value[2], (1, 1): value[3], (1, 2): value[4], (2, 2): value[5]}
    for i in range(3):
        gram[(i, 3)] = (
            (2.0 / HALF_WIDTH) * value[6 + i]
            - (2.0 * CENTER / HALF_WIDTH) * gram[(i, 2)]
            - gram[(min(i, 1), max(i, 1))]
        )
    row = jnp.zeros((1, 128), jnp.float32)
    for at, spot in enumerate(PAIRS):
        row = jnp.where(lane == at, gram[spot], row)
    products[...] = jnp.broadcast_to(row[None, :, :16], products.shape)

    def edge(ref, x):
        ref[27:32] = jnp.zeros((5, 128), jnp.float32)
        for comp in range(3):
            ref[9 * comp : 9 * comp + 9] = partial[comp, x]

    @pl.when(core == 0)
    def _():
        edge(inner, 4)
        edge(outer, 0)

    @pl.when(core == 1)
    def _():
        edge(inner, 0)
        edge(outer, 4)


def finish_kernel(gathered, image, t0, t1, t2, accel, residual):
    row = gathered[0, 15:16, :]
    for peer in range(1, gathered.shape[0]):
        row = row + gathered[peer, 15:16, :]
    gram = {pair: row[:, at : at + 1] for at, pair in enumerate(PAIRS)}
    accel_of, residual_of = cg_coefficients(gram)
    subs = gathered.shape[0]
    at_sub = lax.axis_index("sub")
    low, high = gathered.at[lax.rem(at_sub + subs - 1, subs)], gathered.at[lax.rem(at_sub + 1, subs)]
    for comp in range(3):
        for x in range(5):
            spot = 5 * comp + x
            last = image[comp, x]
            at = lax.broadcasted_iota(jnp.int32, last.shape, 0)
            last = last + jnp.where(at == 0, low[spot : spot + 1, :], 0.0)
            last = last + jnp.where(at == 8, high[spot : spot + 1, :], 0.0)
            parts = [t0[comp, x], t1[comp, x], t2[comp, x]]
            parts.append((2.0 / HALF_WIDTH) * last - (2.0 * CENTER / HALF_WIDTH) * parts[2] - parts[1])
            accel[x, :, comp, :] = accel_of[0] * parts[0] + accel_of[1] * parts[1] + accel_of[2] * parts[2]
            residual[x, :, comp, :] = (
                residual_of[0] * parts[0]
                + residual_of[1] * parts[1]
                + residual_of[2] * parts[2]
                + residual_of[3] * parts[3]
            )


CENTER = 0.196
HALF_WIDTH = 0.194
PAIRS = ((0, 0), (0, 1), (0, 2), (0, 3), (1, 1), (1, 2), (1, 3), (2, 2), (2, 3))


def dot_in(gram, left, right):
    value = 0.0
    for i in range(4):
        for j in range(4):
            if left[i] is None or right[j] is None or (i == 3 and j == 3):
                continue
            value = value + gram[(min(i, j), max(i, j))] * left[i] * right[j]
    return value


def axpy(scale, left, right):
    out = []
    for a, b in zip(left, right):
        if a is None:
            out.append(b)
        elif b is None:
            out.append(scale * a)
        else:
            out.append(scale * a + b)
    return out


def mapped_coefficients(p):
    p0, p1, p2 = (0.0 if v is None else v for v in p[:3])
    shifted = [0.5 * p1, p0 + 0.5 * p2, 0.5 * p1, 0.5 * p2]
    return [HALF_WIDTH * b + CENTER * a for a, b in zip((p0, p1, p2, 0.0), shifted)]


def cg_coefficients(gram):
    accel = [0.0, 0.0, 0.0, 0.0]
    residual = [1.0, 0.0, 0.0, 0.0]
    direction = residual
    norm_now = gram[(0, 0)]
    for sweep_at in range(CG_ITERS):
        mapped = mapped_coefficients(direction)
        step = norm_now / dot_in(gram, direction, mapped)
        accel = axpy(step, direction, accel)
        residual = axpy(-step, mapped, residual)
        if sweep_at + 1 < CG_ITERS:
            norm_next = dot_in(gram, residual, residual)
            direction = axpy(norm_next / norm_now, direction, residual)
            norm_now = norm_next
    return accel, residual


def local_call(kernel, name, outs, scratch, *operands, fetch=False):
    landing = [pltpu.VMEM(x.shape, x.dtype) for x in operands] + [pltpu.SemaphoreType.DMA((len(operands),))]
    return pl.pallas_call(
        kernel,
        out_shape=[jax.ShapeDtypeStruct(shape, jnp.float32) for shape in outs],
        in_specs=[pl.BlockSpec(memory_space=pltpu.HBM if fetch else pltpu.VMEM) for _ in operands],
        out_specs=[pl.BlockSpec(memory_space=pltpu.VMEM) for _ in outs],
        scratch_shapes=[pltpu.VMEM(shape, jnp.float32) for shape in scratch] + (landing if fetch else []),
        compiler_params=pltpu.CompilerParams(vmem_limit_bytes=(60 * 1024 if fetch else 12288) * 1024),
        name=name,
    )(*operands)


def pair_gather(block, axes, offset):
    return lax.all_gather(block, axes, axis_index_groups=pair_groups(axes, offset))


def pair_swap(block, axes, offset):
    groups = pair_groups(axes, offset)
    return lax.ppermute(block, axes, [edge for a, b in groups for edge in ((a, b), (b, a))])


def per_device(
    velocity, displacement, energy, rho_weight, mass_share, energy_share, material_id, mix_mask
):
    field = velocity.shape
    turned = (field[1], field[2], field[0], field[3])
    subs = lax.axis_size("sub")
    above = (lax.axis_index("sub") + 1) % subs
    core = lax.axis_index("dom_2")
    halo = (136, 128)
    own, energy_rate, inner, outer = local_call(
        force_kernel,
        "force",
        ((248, 128), energy.shape, halo, halo),
        ((2, 2, 9, 9, 8, 128), (2, 9, 8, 128), (2,) + field, field, (9, 8, 128), (9, 8, 128)),
        jnp.transpose(displacement, (1, 2, 0, 3)),
        jnp.transpose(velocity, (1, 2, 0, 3)),
        energy, rho_weight, mass_share, energy_share, material_id, mix_mask,
        fetch=True,
    )
    inner = pair_swap(inner, ("sub",), 0)
    outer = pair_swap(outer, ("sub",), 1)
    (wide,) = local_call(
        widen_kernel, "widen", ((BLOCK, 128),), (), inner, outer, own
    )
    pair = pair_gather(wide, DOM, 0)
    shared = pair[0, 4 * LAYER : 5 * LAYER] + pair[1, 0:LAYER]
    closed = lax.dynamic_update_slice(wide, shared, (4 * LAYER * (1 - core), 0))
    cross = pair_gather(closed, DOM, 1)
    edges = pair_gather(cross[0, 4 * LAYER : 5 * LAYER] + cross[1, :LAYER], DOM, 0)
    extended = (3, 13, 17, 128)
    count = lax.axis_size(DOM)
    t0, t1, t2, partial, inner, outer, spread = local_call(
        krylov_kernel,
        "krylov",
        (field, field, field, field, (32, 128), (32, 128), (count, 1, 16)),
        (extended, extended, extended, (6, 18, 8, 128)),
        pair, cross, edges,
    )
    inner = pair_gather(inner, DOM, 0)
    outer_far = pair_swap(outer, DOM, 1)
    inner = (inner[0] + inner[1])[:27].reshape(3, 1, 9, 128)
    outer = (outer + outer_far)[:27].reshape(3, 1, 9, 128)
    low_x, high_x = jnp.where(core == 0, outer, inner), jnp.where(core == 0, inner, outer)
    image = jnp.concatenate([low_x, partial[:, 1:4], high_x], 1)
    row = jnp.sum(lax.all_to_all(spread, DOM, 0, 0, tiled=True), 0)
    row = jnp.pad(row, ((0, 0), (0, 112)))
    low = jnp.concatenate([image[:, :, 0].reshape(15, 128), row], 0)
    high = jnp.concatenate([image[:, :, 8].reshape(15, 128), row], 0)
    peer = jnp.arange(subs, dtype=jnp.int32)[:, None, None]
    gathered = lax.all_to_all(jnp.where(peer == above, high, low), "sub", 0, 0, tiled=True)
    accel, residual = local_call(
        finish_kernel, "finish", (turned, turned), (), gathered, image, t0, t1, t2
    )
    return (jnp.transpose(accel, (2, 0, 1, 3)), jnp.transpose(residual, (2, 0, 1, 3)), energy_rate)


def solution(mesh):
    torus = Mesh(
        mesh.devices.reshape((8, 4, 2, mesh.shape["sub"]) if mesh.shape["dom"] == 64 else (1, 1, 2, mesh.shape["sub"])), ("dom_0", "dom_1", "dom_2", "sub")
    )
    return jax.shard_map(
        per_device,
        mesh=torus,
        in_specs=(
            P(None, DOM, "sub", None),
            P(None, DOM, "sub", None),
            P(None, DOM, "sub", None),
            P(None, DOM, "sub", None),
            P(None, DOM, "sub", None),
            P(None, DOM, "sub", None),
            P(DOM, "sub", None),
            P(None, DOM, "sub", None),
        ),
        out_specs=(P(None, DOM, "sub", None), P(None, DOM, "sub", None), P(None, DOM, "sub", None)),
        check_vma=False,
    )
```
